256 devices in a mesh: req: 2 (over core), row: 32 (over x, z), col: 4 (over y).
Axes of the slice: x: 4, y: 4, z: 8, core: 2. Of those that a mesh axis runs over, the one named last changes fastest.
Arguments:
- hidden: bfloat16 [2, 3072, 3072], P('req', 'row'), may hold values from -6 to 6
- text_hidden: bfloat16 [2, 128, 3072], P('req', 'row'), may hold values from -6 to 6
- text_len: int32 [2], replicated, may hold values from 32 to 128, as said below
- grid: int32 [2, 2], replicated, may hold values from 8 to 32, as said below
- timestep: int32 [2], replicated, may hold values from 250 to 999
- modulation: float32 [2, 8, 3072], P('req'), may hold values from -4 to 4
- q_gain: float32 [64], replicated, may hold values from 1 to 3
- k_gain: float32 [64], replicated, may hold values from 1 to 3
- w_qkv: bfloat16 [3, 3072, 3072], P(None, 'row', 'col'), may hold values from -0.109375 to 0.109375
- w_out: bfloat16 [3072, 3072], P('col'), may hold values from -0.109375 to 0.109375
- w_up: bfloat16 [3072, 12288], P(None, 'row'), may hold values from -0.109375 to 0.109375
- w_down: bfloat16 [12288, 3072], P('row'), may hold values from -0.0546875 to 0.0546875
- w_proj: bfloat16 [3072, 64], replicated, may hold values from -0.109375 to 0.109375
- latent: float32 [2, 3072, 64], P('req', ('row', 'col')), may hold values from -6 to 6
- conv_w: bfloat16 [3, 3, 16, 512], replicated, may hold values from -0.5 to 0.5
Outputs:
- hidden_out: bfloat16 [2, 3072, 3072], P('req', ('row', 'col'))
- new_latent: float32 [2, 3072, 64], P('req', ('row', 'col'))
- decoded: bfloat16 [2, 6, 64, 32, 512], P('req', None, 'row', 'col')
The draws below stay inside these ranges and needn't reach their ends.
Inputs may be any that keep to these rules, and one draw needn't show every extreme that they name: Each request's live token rows and columns; one of the two requests, drawn, fills its whole grid of 32 rows and 16 columns, the other keeps at least half of each. `text_len`: one of the two requests, drawn, has all 128 text tokens live. The previous timestep of the sampling step is timestep - 250.
All inputs are finite; a program needn't handle non-finite values.
Results may differ from the reference program's by a relative error of at most 0.014.
Values may be sent and summed in bfloat16 or wider, within the bound.
A program may use at most 128 MiB of HBM per device.

```python
import math
import jax
import jax.numpy as jnp
from jax import lax

REQS = 2
D = 3072
HEADS = 48
HEAD_DIM = 64
FF = 12288
CH = 16
DEC = 512
FR = 6
TR = 1
TC = 4
TEXT = 128
TRAIN_STEPS = 1000
STRIDE = 250
TD = 24
SEQ = 3072
TOK_ROWS = 32
TOK_COLS = 16
PIX_ROWS = 64
PIX_COLS = 32
PV = 64
N_ROW = 32
N_COL = 4


def draw_text_len(key, part):
    first_key, second_key = jax.random.split(jax.random.fold_in(key, 11))
    drawn = jax.random.randint(first_key, (REQS,), TEXT // 4, TEXT + 1)
    longest = jax.random.randint(second_key, (), 0, REQS)
    chosen = jnp.arange(REQS, dtype=jnp.int32) == longest
    return jnp.where(chosen, TEXT, drawn).astype(jnp.int32)


def draw_grid(key, part):
    first_key, second_key, third_key = jax.random.split(jax.random.fold_in(key, 23), 3)
    row_counts = jax.random.randint(first_key, (REQS,), TOK_ROWS // 2, TOK_ROWS + 1)
    col_counts = jax.random.randint(second_key, (REQS,), TOK_COLS // 2, TOK_COLS + 1)
    fullest = jax.random.randint(third_key, (), 0, REQS)
    chosen = jnp.arange(REQS, dtype=jnp.int32) == fullest
    row_counts = jnp.where(chosen, TOK_ROWS, row_counts)
    col_counts = jnp.where(chosen, TOK_COLS, col_counts)
    return jnp.stack([row_counts, col_counts], axis=1).astype(jnp.int32)


def block_scale(stream_key, extent, shards, smallest, high):
    def one(dim, blocks):
        heights = jax.random.uniform(jax.random.fold_in(jax.random.fold_in(stream_key, 6), dim), (blocks,), jnp.float32, smallest / len(shards), high / len(shards))
        return jnp.repeat(jnp.exp(heights), extent[dim] // blocks).reshape((-1,) + (1,) * (len(extent) - dim - 1))

    loudness = one(*shards[0])
    for cut in shards[1:]:
        loudness = loudness * one(*cut)
    return loudness


def bell_draw(stream_key, shape, scale, bound, pieces=(), held_as=jnp.bfloat16):
    level = block_scale(stream_key, shape, pieces, -0.22, 0.18) if pieces else 1.0
    result = jax.random.normal(stream_key, shape, jnp.float32) * scale * level
    return jnp.minimum(jnp.maximum(result, -bound), bound).astype(held_as)


def setup_inputs(seed: int = 0) -> dict:
    seeds = jax.random.split(jax.random.key(seed), 16)
    return {
        "hidden": bell_draw(seeds[0], (REQS, SEQ, D), 1.0, 6.0, ((0, 2), (1, 32))),
        "text_hidden": bell_draw(seeds[1], (REQS, TEXT, D), 1.0, 6.0, ((0, 2), (1, 32))),
        "text_len": draw_text_len(jax.random.fold_in(seeds[15], 71), 0),
        "grid": draw_grid(jax.random.fold_in(seeds[15], 71), 0),
        "timestep": jax.random.randint(seeds[4], (REQS,), STRIDE, TRAIN_STEPS).astype(jnp.int32),
        "modulation": bell_draw(seeds[5], (REQS, 8, D), 0.6, 4.0, ((0, 2),), jnp.float32),
        "q_gain": jnp.clip(jnp.exp(jax.random.uniform(seeds[6], (HEAD_DIM,), jnp.float32, math.log(1.0), math.log(3.0))), 1.0, 3.0),
        "k_gain": jnp.clip(jnp.exp(jax.random.uniform(seeds[7], (HEAD_DIM,), jnp.float32, math.log(1.0), math.log(3.0))), 1.0, 3.0),
        "w_qkv": bell_draw(seeds[8], (3, D, D), D ** -0.5, 0.109375, ((1, 32), (2, 4))),
        "w_out": bell_draw(seeds[9], (D, D), D ** -0.5, 0.109375, ((0, 4),)),
        "w_up": bell_draw(seeds[10], (D, FF), D ** -0.5, 0.109375, ((1, 32),)),
        "w_down": bell_draw(seeds[11], (FF, D), FF ** -0.5, 0.0546875, ((0, 32),)),
        "w_proj": bell_draw(seeds[12], (D, PV), D ** -0.5, 0.109375),
        "latent": bell_draw(seeds[13], (REQS, SEQ, PV), 1.0, 6.0, ((0, 2), (1, 128)), jnp.float32),
        "conv_w": bell_draw(seeds[14], (3, 3, CH, DEC), (9 * CH) ** -0.5, 0.5),
    }


latent_scale = 0.7

def layer_norm(tensor, epsilon):
    average = lax.optimization_barrier(jnp.mean(tensor, axis=-1, keepdims=True))
    centered = tensor - average
    spread = lax.optimization_barrier(jnp.mean(centered * centered, axis=-1, keepdims=True))
    return centered * lax.rsqrt(spread + epsilon)

def modulate(tensor, offset, factor):
    return (layer_norm(tensor, 1e-05) * (1.0 + factor) + offset).astype(jnp.bfloat16)

def head_norm(tensor, scaling):
    shaped = tensor.reshape(tensor.shape[0], HEADS, HEAD_DIM)
    return (layer_norm(shaped, 1e-06) * scaling).astype(jnp.bfloat16)

def pick_entry(entries, position):
    slot_ids = jnp.arange(entries.shape[0], dtype=jnp.int32)
    return jnp.sum(jnp.where(slot_ids == position, entries, jnp.zeros_like(entries)))

def solver_weights(step_index):
    plan = jnp.linspace(0.00085 ** 0.5, 0.012 ** 0.5, TRAIN_STEPS, dtype=jnp.float32) ** 2
    cumulative = jnp.cumprod(1.0 - plan)
    alpha_now = pick_entry(cumulative, step_index)
    alpha_prev = pick_entry(cumulative, step_index - STRIDE)
    root_now = jnp.sqrt(alpha_now)
    rest_now = jnp.sqrt(1.0 - alpha_now)
    root_prev = jnp.sqrt(alpha_prev)
    rest_prev = jnp.sqrt(1.0 - alpha_prev)
    return (root_prev * root_now + rest_prev * rest_now, rest_prev * root_now - root_prev * rest_now)

def video_live(rows_live, cols_live):
    positions = jnp.arange(SEQ, dtype=jnp.int32)
    owner_row = positions // (N_COL * TD)
    owner_col = positions // TD % N_COL
    local_ids = positions % TD
    token_row = owner_row * TR + local_ids // TC % TR
    token_col = owner_col * TC + local_ids % TC
    return ((token_row < rows_live) & (token_col < cols_live)).astype(jnp.float32)

def reference(hidden, text_hidden, text_len, grid, timestep, modulation, q_gain, k_gain, w_qkv, w_out, w_up, w_down, w_proj, latent, conv_w):
    score_scale = HEAD_DIM ** (-0.5)
    hidden_list = []
    latent_list = []
    decoded_list = []
    for request in range(REQS):
        adaptive = modulation[request]
        source = hidden[request].astype(jnp.float32)
        normed = modulate(source, adaptive[0], adaptive[1])
        text_normed = modulate(text_hidden[request].astype(jnp.float32), adaptive[0], adaptive[1])
        both_rows = jnp.concatenate([normed, text_normed], axis=0)
        queries = head_norm(jnp.dot(normed, w_qkv[0], preferred_element_type=jnp.float32), q_gain)
        key_block = head_norm(jnp.dot(both_rows, w_qkv[1], preferred_element_type=jnp.float32), k_gain)
        value_block = jnp.dot(both_rows, w_qkv[2], preferred_element_type=jnp.float32).astype(jnp.bfloat16)
        value_block = value_block.reshape(SEQ + TEXT, HEADS, HEAD_DIM)
        live_tokens = video_live(grid[request, 0], grid[request, 1])
        live_text = (jnp.arange(TEXT, dtype=jnp.int32) < text_len[request]).astype(jnp.float32)
        live_keys = jnp.concatenate([live_tokens, live_text], axis=0)

        def one_head(triple):
            head_query, head_key, head_value = triple
            scores = jnp.dot(head_query, head_key.T, preferred_element_type=jnp.float32) * score_scale
            raw_weights = jnp.exp(scores) * live_keys[None, :]
            totals = lax.optimization_barrier(jnp.sum(raw_weights, axis=1, keepdims=True))
            weighted = jnp.dot(raw_weights.astype(jnp.bfloat16), head_value, preferred_element_type=jnp.float32)
            return (weighted / totals).astype(jnp.bfloat16)
        head_outputs = lax.map(one_head, (queries.transpose(1, 0, 2), key_block.transpose(1, 0, 2), value_block.transpose(1, 0, 2)))
        attended = head_outputs.transpose(1, 0, 2).reshape(SEQ, D)
        projected = jnp.dot(attended, w_out, preferred_element_type=jnp.float32)
        mixed = lax.optimization_barrier((source + adaptive[2] * projected).astype(jnp.bfloat16)).astype(jnp.float32)
        second_norm = modulate(mixed, adaptive[3], adaptive[4])
        hidden_units = jax.nn.gelu(jnp.dot(second_norm, w_up, preferred_element_type=jnp.float32), approximate=True).astype(jnp.bfloat16)
        block_size = FF // N_ROW
        unit_blocks = hidden_units.reshape(SEQ, N_ROW, block_size).transpose(1, 0, 2)
        down_blocks = w_down.reshape(N_ROW, block_size, D)

        def add_block(running, blocks_pair):
            block_part = jnp.dot(blocks_pair[0], blocks_pair[1], preferred_element_type=jnp.float32).astype(jnp.bfloat16)
            return (running + lax.optimization_barrier(block_part).astype(jnp.float32), None)
        feed_out = lax.scan(add_block, jnp.zeros((SEQ, D), jnp.float32), (unit_blocks, down_blocks))[0]
        out_hidden = (mixed + adaptive[5] * feed_out).astype(jnp.bfloat16)
        final_norm = modulate(out_hidden.astype(jnp.float32), adaptive[6], adaptive[7])
        velocity = jnp.dot(final_norm, w_proj, preferred_element_type=jnp.float32)
        keep_part, velocity_part = solver_weights(timestep[request])
        updated = (keep_part * latent[request] + velocity_part * velocity) * live_tokens[:, None]
        pixels = updated.reshape(N_ROW, N_COL, FR, TR, TC, CH, 2, 2).transpose(2, 0, 3, 6, 1, 4, 7, 5)
        pixels = pixels.reshape(FR, PIX_ROWS, PIX_COLS, CH)
        scaled = (pixels / latent_scale).astype(jnp.bfloat16)
        padded = jnp.pad(scaled, ((0, 0), (1, 1), (1, 1), (0, 0)))
        running = jnp.zeros((FR, PIX_ROWS, PIX_COLS, DEC), jnp.float32)
        for row_tap in range(3):
            for col_tap in range(3):
                window = padded[:, row_tap:row_tap + PIX_ROWS, col_tap:col_tap + PIX_COLS, :].astype(jnp.float32)
                running = running + jnp.einsum('fyxc,cd->fyxd', window, conv_w[row_tap, col_tap].astype(jnp.float32))
        hidden_list.append(out_hidden)
        latent_list.append(updated)
        decoded_list.append(running.astype(jnp.bfloat16))
    return (jnp.stack(hidden_list, axis=0), jnp.stack(latent_list, axis=0), jnp.stack(decoded_list, axis=0))
```

```python
import jax
import jax.numpy as jnp
from jax import lax
from jax.sharding import PartitionSpec as P

CH = 16
FR = 6
TR = 1
TC = 4
TRAIN_STEPS = 1000
STRIDE = 250


latent_scale = 0.7


def extended(cells, sides, width):
    for axis, dim in sides:
        count = lax.axis_size(axis)
        ends = count - 1
        head = lax.slice_in_dim(cells, 0, width, axis=dim)
        tail = lax.slice_in_dim(cells, cells.shape[dim] - width, cells.shape[dim], axis=dim)
        cells = jnp.concatenate(
            [
                lax.ppermute(tail, axis, [(i, (i + 1) % count) for i in range(ends)]),
                cells,
                lax.ppermute(head, axis, [((i + 1) % count, i) for i in range(ends)]),
            ],
            axis=dim,
        )
    return cells


def layer_norm(tensor, epsilon):
    average = jnp.mean(tensor, axis=-1, keepdims=True)
    centered = tensor - average
    spread = jnp.mean(centered * centered, axis=-1, keepdims=True)
    return centered * lax.rsqrt(spread + epsilon)


def modulate(tensor, offset, factor):
    return (layer_norm(tensor, 1e-05) * (1.0 + factor) + offset).astype(jnp.bfloat16)


def head_norm(tensor, scaling):
    return (layer_norm(tensor, 1e-06) * scaling).astype(jnp.bfloat16)


def pick_entry(entries, position):
    slot_ids = jnp.arange(entries.shape[0], dtype=jnp.int32)
    return jnp.sum(jnp.where(slot_ids == position, entries, jnp.zeros_like(entries)))


def solver_weights(step_index):
    plan = jnp.linspace(0.00085**0.5, 0.012**0.5, TRAIN_STEPS, dtype=jnp.float32) ** 2
    cumulative = jnp.cumprod(1.0 - plan)
    alpha_now = pick_entry(cumulative, step_index)
    alpha_prev = pick_entry(cumulative, step_index - STRIDE)
    root_now = jnp.sqrt(alpha_now)
    rest_now = jnp.sqrt(1.0 - alpha_now)
    root_prev = jnp.sqrt(alpha_prev)
    rest_prev = jnp.sqrt(1.0 - alpha_prev)
    return (
        root_prev * root_now + rest_prev * rest_now,
        rest_prev * root_now - root_prev * rest_now,
    )


def key_mask(count, owners, grid, text_len, span, block_tokens, tile, text_rows):
    positions = jnp.arange(count, dtype=jnp.int32)
    owner_row = positions // span
    within = positions % span
    is_video = within < block_tokens
    owner_col = within // tile
    local_ids = within % tile
    token_row = owner_row * TR + local_ids // TC % TR
    token_col = owner_col * TC + local_ids % TC
    text_index = owner_row * text_rows + within - block_tokens
    matches = jnp.arange(grid.shape[0], dtype=jnp.int32)[None, :] == owners[:, None]
    rows_live = jnp.sum(jnp.where(matches, grid[None, :, 0], 0), axis=1)
    cols_live = jnp.sum(jnp.where(matches, grid[None, :, 1], 0), axis=1)
    text_lens = jnp.sum(jnp.where(matches, text_len[None, :], 0), axis=1)
    video_live = (token_row[None, :] < rows_live[:, None]) & (
        token_col[None, :] < cols_live[:, None]
    )
    text_live = text_index[None, :] < text_lens[:, None]
    return jnp.where(is_video[None, :], video_live, text_live).astype(jnp.float32)


def projector(stacked, piece):
    return jnp.einsum("gld,cde->cgle", stacked, piece, preferred_element_type=jnp.float32)


def attention_step(queries, owners, grid, text_len, span, block_tokens, tile, text_rows):
    score_scale = queries.shape[3] ** (-0.5)

    def attend(carry, pieces, start):
        key_piece, value_piece = pieces
        live_keys = key_mask(
            key_piece.shape[1], owners, grid, text_len, span, block_tokens, tile, text_rows
        )
        scores = (
            jnp.einsum("gqhd,gkhd->gqhk", queries, key_piece, preferred_element_type=jnp.float32)
            * score_scale
        )
        raw_weights = jnp.exp(scores) * live_keys[:, None, None, :]
        weighted = jnp.einsum(
            "gqhk,gkhd->gqhd",
            raw_weights.astype(jnp.bfloat16),
            value_piece,
            preferred_element_type=jnp.float32,
        )
        return (weighted, jnp.sum(raw_weights, axis=3))

    return attend


def shards(
    hidden,
    text_hidden,
    text_len,
    grid,
    timestep,
    modulation,
    q_gain,
    k_gain,
    w_qkv,
    w_out,
    w_up,
    w_down,
    w_proj,
    latent,
    conv_w,
):
    col_count = lax.axis_size("col")
    request_id = lax.axis_index("req")
    row_id = lax.axis_index("row")
    col_id = lax.axis_index("col")
    block_tokens = hidden.shape[1]
    tile = block_tokens // col_count
    text_rows = text_hidden.shape[1]
    head_dim = q_gain.shape[0]
    adaptive = modulation[0]
    source = hidden[0].astype(jnp.float32)
    joined = jnp.concatenate(
        [
            modulate(source, adaptive[0], adaptive[1]),
            modulate(text_hidden[0].astype(jnp.float32), adaptive[0], adaptive[1]),
        ],
        axis=0,
    )
    span = joined.shape[0]
    stacked = joined[None]
    owners = jnp.reshape(request_id, (1,))
    half_cols = w_qkv.shape[2] // 2
    own_half = lax.dynamic_slice_in_dim(w_qkv, request_id * half_cols, half_cols, 2)
    gathered_half = lax.all_gather(own_half, "row", axis=1, tiled=True)
    qkv = projector(stacked, lax.all_gather(gathered_half, "req", axis=2, tiled=True))
    groups = stacked.shape[0]
    heads_here = qkv.shape[3] // head_dim
    shaped = qkv.reshape(3, groups, span, heads_here, head_dim)
    queries = head_norm(shaped[0, :, :block_tokens], q_gain)
    key_block = head_norm(shaped[1], k_gain)
    value_block = shaped[2].astype(jnp.bfloat16)
    attend = attention_step(queries, owners, grid, text_len, span, block_tokens, tile, text_rows)
    empty_state = (jnp.zeros(queries.shape, jnp.float32), jnp.zeros(queries.shape[:3], jnp.float32))
    both = jnp.stack([key_block[0], value_block[0]], axis=0)[None]
    both = lax.all_gather(both, "row", axis=0, tiled=True)
    both = jnp.swapaxes(both, 0, 1).reshape(2, 1, -1, heads_here, head_dim)
    weighted, totals = attend(
        empty_state,
        (both[0], both[1]),
        jnp.int32(0),
    )
    attended = (
        (weighted / totals[..., None])
        .astype(jnp.bfloat16)
        .reshape(groups * block_tokens, heads_here * head_dim)
    )
    partial_out = jnp.dot(attended, w_out, preferred_element_type=jnp.float32)
    projected = lax.psum_scatter(partial_out, "col", scatter_dimension=0, tiled=True)
    own_rows = lax.dynamic_slice_in_dim(source, col_id * tile, tile, 0)
    mixed = lax.optimization_barrier(
        (own_rows + adaptive[2] * projected).astype(jnp.bfloat16)
    ).astype(jnp.float32)
    second_norm = modulate(mixed, adaptive[3], adaptive[4])
    hidden_units = jax.nn.gelu(
        jnp.dot(
            lax.all_gather(second_norm, "row", axis=0, tiled=True),
            w_up,
            preferred_element_type=jnp.float32,
        ),
        approximate=True,
    ).astype(jnp.bfloat16)
    feed_terms = jnp.dot(hidden_units, w_down, preferred_element_type=jnp.float32)
    feed_out = lax.psum_scatter(
        feed_terms.astype(jnp.bfloat16), "row", scatter_dimension=0, tiled=True
    ).astype(jnp.float32)
    out_hidden = (mixed + adaptive[5] * feed_out).astype(jnp.bfloat16)
    final_norm = modulate(out_hidden.astype(jnp.float32), adaptive[6], adaptive[7])
    velocity = jnp.dot(final_norm, w_proj, preferred_element_type=jnp.float32)
    local_ids = jnp.arange(tile, dtype=jnp.int32)
    token_row = row_id * TR + local_ids // TC % TR
    token_col = col_id * TC + local_ids % TC
    rows_live = pick_entry(grid[:, 0], request_id)
    cols_live = pick_entry(grid[:, 1], request_id)
    live_tokens = ((token_row < rows_live) & (token_col < cols_live)).astype(jnp.float32)
    keep_part, velocity_part = solver_weights(pick_entry(timestep, request_id))
    updated = (keep_part * latent[0] + velocity_part * velocity) * live_tokens[:, None]
    pixels = (
        updated.reshape(FR, TR, TC, CH, 2, 2)
        .transpose(0, 1, 4, 2, 5, 3)
        .reshape(FR, 2 * TR, 2 * TC, CH)
    )
    scaled = (pixels / latent_scale).astype(jnp.bfloat16)
    padded = extended(scaled, (("row", 1), ("col", 2)), 1)
    running = jnp.zeros((FR, 2 * TR, 2 * TC, conv_w.shape[3]), jnp.float32)
    for row_tap in range(3):
        for col_tap in range(3):
            window = padded[:, row_tap : row_tap + 2 * TR, col_tap : col_tap + 2 * TC, :]
            running = running + jnp.einsum(
                "fyxc,cd->fyxd",
                window,
                conv_w[row_tap, col_tap],
                preferred_element_type=jnp.float32,
            )
    return (out_hidden[None], updated[None], running.astype(jnp.bfloat16)[None])


def solution(mesh):
    placed = (
        P("req", "row", None),
        P("req", "row", None),
        P(),
        P(),
        P(),
        P("req", None, None),
        P(),
        P(),
        P(None, "row", "col"),
        P("col", None),
        P(None, "row"),
        P("row", None),
        P(),
        P("req", ("row", "col"), None),
        P(),
    )
    return jax.shard_map(
        shards,
        mesh=mesh,
        in_specs=placed,
        out_specs=(
            P("req", ("row", "col"), None),
            P("req", ("row", "col"), None),
            P("req", None, "row", "col", None),
        ),
        check_vma=False,
    )
```

```python
import functools

import jax
import jax.numpy as jnp
from jax import lax
from jax.sharding import PartitionSpec as P
from jax.experimental import pallas as pl
from jax.experimental.pallas import tpu as pltpu

MESH_IDS = pl.DeviceIdType.MESH

CH = 16
FR = 6
TR = 1
TC = 4
TRAIN_STEPS = 1000
STRIDE = 250


latent_scale = 0.7


def extended(cells, sides, width):
    for axis, dim in sides:
        count = lax.axis_size(axis)
        ends = count - 1
        head = lax.slice_in_dim(cells, 0, width, axis=dim)
        tail = lax.slice_in_dim(cells, cells.shape[dim] - width, cells.shape[dim], axis=dim)
        cells = jnp.concatenate(
            [
                lax.ppermute(tail, axis, [(i, (i + 1) % count) for i in range(ends)]),
                cells,
                lax.ppermute(head, axis, [((i + 1) % count, i) for i in range(ends)]),
            ],
            axis=dim,
        )
    return cells


def scatter_sum_kernel(count, rows, part_ref, out_ref, landed, send_sems, recv_sems, own_sem):
    me = lax.axis_index("row")
    req = lax.axis_index("req")
    col = lax.axis_index("col")
    barrier = pltpu.get_barrier_semaphore()
    for step in range(1, count):
        peer = lax.rem(me + step, count)
        pl.semaphore_signal(barrier, inc=1, device_id=(req, peer, col), device_id_type=MESH_IDS)
    pl.semaphore_wait(barrier, count - 1)
    own = pltpu.make_async_copy(part_ref.at[pl.ds(me * rows, rows)], landed.at[me], own_sem)
    own.start()
    sends = []
    for step in range(1, count):
        peer = lax.rem(me + step, count)
        copy = pltpu.make_async_remote_copy(
            src_ref=part_ref.at[pl.ds(peer * rows, rows)],
            dst_ref=landed.at[me],
            send_sem=send_sems.at[step],
            recv_sem=recv_sems.at[step],
            device_id=(req, peer, col),
            device_id_type=MESH_IDS,
        )
        copy.start()
        sends.append(copy)
    own.wait()
    for step in range(1, count):
        source = lax.rem(me + count - step, count)
        pltpu.make_async_remote_copy(
            src_ref=part_ref.at[pl.ds(me * rows, rows)],
            dst_ref=landed.at[source],
            send_sem=send_sems.at[step],
            recv_sem=recv_sems.at[step],
            device_id=(req, source, col),
            device_id_type=MESH_IDS,
        ).wait_recv()
    for copy in sends:
        copy.wait_send()
    total = landed[0].astype(jnp.float32)
    for slot in range(1, count):
        total = total + landed[slot].astype(jnp.float32)
    out_ref[...] = total


def row_scatter_sum(part):
    count = lax.axis_size("row")
    rows = part.shape[0] // count
    width = part.shape[1]
    return pl.pallas_call(
        functools.partial(scatter_sum_kernel, count, rows),
        out_shape=jax.ShapeDtypeStruct((rows, width), jnp.float32),
        in_specs=[pl.BlockSpec(memory_space=pl.ANY)],
        out_specs=pl.BlockSpec(memory_space=pltpu.VMEM),
        scratch_shapes=[
            pltpu.VMEM((count, rows, width), part.dtype),
            pltpu.SemaphoreType.DMA((count,)),
            pltpu.SemaphoreType.DMA((count,)),
            pltpu.SemaphoreType.DMA(()),
        ],
        compiler_params=pltpu.CompilerParams(
            collective_id=0, has_side_effects=True, vmem_limit_bytes=48 * 1024 * 1024
        ),
    )(part)


def layer_norm(tensor, epsilon):
    average = jnp.mean(tensor, axis=-1, keepdims=True)
    centered = tensor - average
    spread = jnp.mean(centered * centered, axis=-1, keepdims=True)
    return centered * lax.rsqrt(spread + epsilon)


def modulate(tensor, offset, factor):
    return (layer_norm(tensor, 1e-05) * (1.0 + factor) + offset).astype(jnp.bfloat16)


def head_norm(tensor, scaling):
    return (layer_norm(tensor, 1e-06) * scaling).astype(jnp.bfloat16)


def pick_entry(entries, position):
    slot_ids = jnp.arange(entries.shape[0], dtype=jnp.int32)
    return jnp.sum(jnp.where(slot_ids == position, entries, jnp.zeros_like(entries)))


def solver_weights(step_index):
    plan = jnp.linspace(0.00085**0.5, 0.012**0.5, TRAIN_STEPS, dtype=jnp.float32) ** 2
    cumulative = jnp.cumprod(1.0 - plan)
    alpha_now = pick_entry(cumulative, step_index)
    alpha_prev = pick_entry(cumulative, step_index - STRIDE)
    root_now = jnp.sqrt(alpha_now)
    rest_now = jnp.sqrt(1.0 - alpha_now)
    root_prev = jnp.sqrt(alpha_prev)
    rest_prev = jnp.sqrt(1.0 - alpha_prev)
    return (
        root_prev * root_now + rest_prev * rest_now,
        rest_prev * root_now - root_prev * rest_now,
    )


def key_mask(count, owners, grid, text_len, span, block_tokens, tile, text_rows):
    positions = jnp.arange(count, dtype=jnp.int32)
    owner_row = positions // span
    within = positions % span
    is_video = within < block_tokens
    owner_col = within // tile
    local_ids = within % tile
    token_row = owner_row * TR + local_ids // TC % TR
    token_col = owner_col * TC + local_ids % TC
    text_index = owner_row * text_rows + within - block_tokens
    matches = jnp.arange(grid.shape[0], dtype=jnp.int32)[None, :] == owners[:, None]
    rows_live = jnp.sum(jnp.where(matches, grid[None, :, 0], 0), axis=1)
    cols_live = jnp.sum(jnp.where(matches, grid[None, :, 1], 0), axis=1)
    text_lens = jnp.sum(jnp.where(matches, text_len[None, :], 0), axis=1)
    video_live = (token_row[None, :] < rows_live[:, None]) & (
        token_col[None, :] < cols_live[:, None]
    )
    text_live = text_index[None, :] < text_lens[:, None]
    return jnp.where(is_video[None, :], video_live, text_live).astype(jnp.float32)


def projector(stacked, piece):
    return jnp.einsum("gld,cde->cgle", stacked, piece, preferred_element_type=jnp.float32)


def attention_step(queries, owners, grid, text_len, span, block_tokens, tile, text_rows):
    score_scale = queries.shape[3] ** (-0.5)

    def attend(carry, pieces, start):
        key_piece, value_piece = pieces
        live_keys = key_mask(
            key_piece.shape[1], owners, grid, text_len, span, block_tokens, tile, text_rows
        )
        scores = (
            jnp.einsum("gqhd,gkhd->gqhk", queries, key_piece, preferred_element_type=jnp.float32)
            * score_scale
        )
        raw_weights = jnp.exp(scores) * live_keys[:, None, None, :]
        weighted = jnp.einsum(
            "gqhk,gkhd->gqhd",
            raw_weights.astype(jnp.bfloat16),
            value_piece,
            preferred_element_type=jnp.float32,
        )
        return (weighted, jnp.sum(raw_weights, axis=3))

    return attend


def shards(
    hidden,
    text_hidden,
    text_len,
    grid,
    timestep,
    modulation,
    q_gain,
    k_gain,
    w_qkv,
    w_out,
    w_up,
    w_down,
    w_proj,
    latent,
    conv_w,
):
    col_count = lax.axis_size("col")
    request_id = lax.axis_index("req")
    row_id = lax.axis_index("row")
    col_id = lax.axis_index("col")
    block_tokens = hidden.shape[1]
    tile = block_tokens // col_count
    text_rows = text_hidden.shape[1]
    head_dim = q_gain.shape[0]
    adaptive = modulation[0]
    source = hidden[0].astype(jnp.float32)
    joined = jnp.concatenate(
        [
            modulate(source, adaptive[0], adaptive[1]),
            modulate(text_hidden[0].astype(jnp.float32), adaptive[0], adaptive[1]),
        ],
        axis=0,
    )
    span = joined.shape[0]
    stacked = joined[None]
    owners = jnp.reshape(request_id, (1,))
    half_cols = w_qkv.shape[2] // 2
    own_half = lax.dynamic_slice_in_dim(w_qkv, request_id * half_cols, half_cols, 2)
    gathered_half = lax.all_gather(own_half, "row", axis=1, tiled=True)
    qkv = projector(stacked, lax.all_gather(gathered_half, "req", axis=2, tiled=True))
    groups = stacked.shape[0]
    heads_here = qkv.shape[3] // head_dim
    shaped = qkv.reshape(3, groups, span, heads_here, head_dim)
    queries = head_norm(shaped[0, :, :block_tokens], q_gain)
    key_block = head_norm(shaped[1], k_gain)
    value_block = shaped[2].astype(jnp.bfloat16)
    attend = attention_step(queries, owners, grid, text_len, span, block_tokens, tile, text_rows)
    empty_state = (jnp.zeros(queries.shape, jnp.float32), jnp.zeros(queries.shape[:3], jnp.float32))
    both = jnp.stack([key_block[0], value_block[0]], axis=0)[None]
    both = lax.all_gather(both, "row", axis=0, tiled=True)
    both = jnp.swapaxes(both, 0, 1).reshape(2, 1, -1, heads_here, head_dim)
    weighted, totals = attend(
        empty_state,
        (both[0], both[1]),
        jnp.int32(0),
    )
    attended = (
        (weighted / totals[..., None])
        .astype(jnp.bfloat16)
        .reshape(groups * block_tokens, heads_here * head_dim)
    )
    partial_out = jnp.dot(attended, w_out, preferred_element_type=jnp.float32)
    projected = lax.psum_scatter(partial_out, "col", scatter_dimension=0, tiled=True)
    own_rows = lax.dynamic_slice_in_dim(source, col_id * tile, tile, 0)
    mixed = lax.optimization_barrier(
        (own_rows + adaptive[2] * projected).astype(jnp.bfloat16)
    ).astype(jnp.float32)
    second_norm = modulate(mixed, adaptive[3], adaptive[4])
    hidden_units = jax.nn.gelu(
        jnp.dot(
            lax.all_gather(second_norm, "row", axis=0, tiled=True),
            w_up,
            preferred_element_type=jnp.float32,
        ),
        approximate=True,
    ).astype(jnp.bfloat16)
    feed_terms = jnp.dot(hidden_units, w_down, preferred_element_type=jnp.float32)
    feed_out = row_scatter_sum(feed_terms.astype(jnp.bfloat16))
    out_hidden = (mixed + adaptive[5] * feed_out).astype(jnp.bfloat16)
    final_norm = modulate(out_hidden.astype(jnp.float32), adaptive[6], adaptive[7])
    velocity = jnp.dot(final_norm, w_proj, preferred_element_type=jnp.float32)
    local_ids = jnp.arange(tile, dtype=jnp.int32)
    token_row = row_id * TR + local_ids // TC % TR
    token_col = col_id * TC + local_ids % TC
    rows_live = pick_entry(grid[:, 0], request_id)
    cols_live = pick_entry(grid[:, 1], request_id)
    live_tokens = ((token_row < rows_live) & (token_col < cols_live)).astype(jnp.float32)
    keep_part, velocity_part = solver_weights(pick_entry(timestep, request_id))
    updated = (keep_part * latent[0] + velocity_part * velocity) * live_tokens[:, None]
    pixels = (
        updated.reshape(FR, TR, TC, CH, 2, 2)
        .transpose(0, 1, 4, 2, 5, 3)
        .reshape(FR, 2 * TR, 2 * TC, CH)
    )
    scaled = (pixels / latent_scale).astype(jnp.bfloat16)
    padded = extended(scaled, (("row", 1), ("col", 2)), 1)
    running = jnp.zeros((FR, 2 * TR, 2 * TC, conv_w.shape[3]), jnp.float32)
    for row_tap in range(3):
        for col_tap in range(3):
            window = padded[:, row_tap : row_tap + 2 * TR, col_tap : col_tap + 2 * TC, :]
            running = running + jnp.einsum(
                "fyxc,cd->fyxd",
                window,
                conv_w[row_tap, col_tap],
                preferred_element_type=jnp.float32,
            )
    return (out_hidden[None], updated[None], running.astype(jnp.bfloat16)[None])


def solution(mesh):
    placed = (
        P("req", "row", None),
        P("req", "row", None),
        P(),
        P(),
        P(),
        P("req", None, None),
        P(),
        P(),
        P(None, "row", "col"),
        P("col", None),
        P(None, "row"),
        P("row", None),
        P(),
        P("req", ("row", "col"), None),
        P(),
    )
    return jax.shard_map(
        shards,
        mesh=mesh,
        in_specs=placed,
        out_specs=(
            P("req", ("row", "col"), None),
            P("req", ("row", "col"), None),
            P("req", None, "row", "col", None),
        ),
        check_vma=False,
    )
```

```python
import functools

import jax
import jax.numpy as jnp
from jax import lax
from jax.sharding import PartitionSpec as P
from jax.experimental import pallas as pl
from jax.experimental.pallas import tpu as pltpu

MESH_IDS = pl.DeviceIdType.MESH

CH = 16
FR = 6
TR = 1
TC = 4
TRAIN_STEPS = 1000
STRIDE = 250


latent_scale = 0.7


def extended(cells, sides, width):
    for axis, dim in sides:
        count = lax.axis_size(axis)
        ends = count - 1
        head = lax.slice_in_dim(cells, 0, width, axis=dim)
        tail = lax.slice_in_dim(cells, cells.shape[dim] - width, cells.shape[dim], axis=dim)
        cells = jnp.concatenate(
            [
                lax.ppermute(tail, axis, [(i, (i + 1) % count) for i in range(ends)]),
                cells,
                lax.ppermute(head, axis, [((i + 1) % count, i) for i in range(ends)]),
            ],
            axis=dim,
        )
    return cells


def peer_on(axis, peer):
    return tuple(peer if name == axis else lax.axis_index(name) for name in ("req", "row", "col"))


def scatter_sum_kernel(axis, count, rows, part_ref, out_ref, landed, send_sems, recv_sems, own_sem):
    me = lax.axis_index(axis)
    barrier = pltpu.get_barrier_semaphore()
    for step in range(1, count):
        peer = lax.rem(me + step, count)
        pl.semaphore_signal(barrier, inc=1, device_id=peer_on(axis, peer), device_id_type=MESH_IDS)
    pl.semaphore_wait(barrier, count - 1)
    own = pltpu.make_async_copy(part_ref.at[pl.ds(me * rows, rows)], landed.at[me], own_sem)
    own.start()
    sends = []
    for step in range(1, count):
        peer = lax.rem(me + step, count)
        copy = pltpu.make_async_remote_copy(
            src_ref=part_ref.at[pl.ds(peer * rows, rows)],
            dst_ref=landed.at[me],
            send_sem=send_sems.at[step],
            recv_sem=recv_sems.at[step],
            device_id=peer_on(axis, peer),
            device_id_type=MESH_IDS,
        )
        copy.start()
        sends.append(copy)
    own.wait()
    for step in range(1, count):
        source = lax.rem(me + count - step, count)
        pltpu.make_async_remote_copy(
            src_ref=part_ref.at[pl.ds(me * rows, rows)],
            dst_ref=landed.at[source],
            send_sem=send_sems.at[step],
            recv_sem=recv_sems.at[step],
            device_id=peer_on(axis, source),
            device_id_type=MESH_IDS,
        ).wait_recv()
    for copy in sends:
        copy.wait_send()
    total = landed[0].astype(jnp.float32)
    for slot in range(1, count):
        total = total + landed[slot].astype(jnp.float32)
    out_ref[...] = total


def scatter_sum(part, axis, kernel_id):
    count = lax.axis_size(axis)
    rows = part.shape[0] // count
    width = part.shape[1]
    return pl.pallas_call(
        functools.partial(scatter_sum_kernel, axis, count, rows),
        out_shape=jax.ShapeDtypeStruct((rows, width), jnp.float32),
        in_specs=[pl.BlockSpec(memory_space=pl.ANY)],
        out_specs=pl.BlockSpec(memory_space=pltpu.VMEM),
        scratch_shapes=[
            pltpu.VMEM((count, rows, width), part.dtype),
            pltpu.SemaphoreType.DMA((count,)),
            pltpu.SemaphoreType.DMA((count,)),
            pltpu.SemaphoreType.DMA(()),
        ],
        compiler_params=pltpu.CompilerParams(
            collective_id=kernel_id, has_side_effects=True, vmem_limit_bytes=48 * 1024 * 1024
        ),
    )(part)


def attention_kernel(scale, q_ref, kv_ref, live_ref, out_ref):
    sources, _, block, width = kv_ref.shape
    lane = lax.broadcasted_iota(jnp.int32, (1, 128), 1)
    first = lane < 64
    live = live_ref[...]
    for pair in range(width // 128):
        cols = slice(pair * 128, (pair + 1) * 128)
        query = q_ref[:, cols]
        keys = kv_ref[:, 0, :, cols].reshape(sources * block, 128)
        values = kv_ref[:, 1, :, cols].reshape(sources * block, 128)
        results = []
        for half in (first, jnp.logical_not(first)):
            picked = jnp.where(half, query, jnp.zeros_like(query))
            scores = lax.dot_general(
                picked, keys, (((1,), (1,)), ((), ())), preferred_element_type=jnp.float32
            ) * scale
            weights = jnp.exp(scores) * live
            totals = jnp.sum(weights, axis=1, keepdims=True)
            summed = jnp.dot(weights.astype(jnp.bfloat16), values, preferred_element_type=jnp.float32)
            results.append(summed / totals)
        out_ref[:, cols] = jnp.where(first, results[0], results[1]).astype(out_ref.dtype)


def attention(queries, gathered, live, scale):
    return pl.pallas_call(
        functools.partial(attention_kernel, scale),
        out_shape=jax.ShapeDtypeStruct(queries.shape, jnp.bfloat16),
        in_specs=[pl.BlockSpec(memory_space=pltpu.VMEM)] * 3,
        out_specs=pl.BlockSpec(memory_space=pltpu.VMEM),
        compiler_params=pltpu.CompilerParams(vmem_limit_bytes=56 * 1024 * 1024),
    )(queries, gathered, live)


def layer_norm(tensor, epsilon):
    average = jnp.mean(tensor, axis=-1, keepdims=True)
    centered = tensor - average
    spread = jnp.mean(centered * centered, axis=-1, keepdims=True)
    return centered * lax.rsqrt(spread + epsilon)


def modulate(tensor, offset, factor):
    return (layer_norm(tensor, 1e-05) * (1.0 + factor) + offset).astype(jnp.bfloat16)


def head_norm(tensor, scaling):
    return (layer_norm(tensor, 1e-06) * scaling).astype(jnp.bfloat16)


def pick_entry(entries, position):
    slot_ids = jnp.arange(entries.shape[0], dtype=jnp.int32)
    return jnp.sum(jnp.where(slot_ids == position, entries, jnp.zeros_like(entries)))


def solver_weights(step_index):
    plan = jnp.linspace(0.00085**0.5, 0.012**0.5, TRAIN_STEPS, dtype=jnp.float32) ** 2
    cumulative = jnp.cumprod(1.0 - plan)
    alpha_now = pick_entry(cumulative, step_index)
    alpha_prev = pick_entry(cumulative, step_index - STRIDE)
    root_now = jnp.sqrt(alpha_now)
    rest_now = jnp.sqrt(1.0 - alpha_now)
    root_prev = jnp.sqrt(alpha_prev)
    rest_prev = jnp.sqrt(1.0 - alpha_prev)
    return (
        root_prev * root_now + rest_prev * rest_now,
        rest_prev * root_now - root_prev * rest_now,
    )


def key_mask(count, owners, grid, text_len, span, block_tokens, tile, text_rows):
    positions = jnp.arange(count, dtype=jnp.int32)
    owner_row = positions // span
    within = positions % span
    is_video = within < block_tokens
    owner_col = within // tile
    local_ids = within % tile
    token_row = owner_row * TR + local_ids // TC % TR
    token_col = owner_col * TC + local_ids % TC
    text_index = owner_row * text_rows + within - block_tokens
    matches = jnp.arange(grid.shape[0], dtype=jnp.int32)[None, :] == owners[:, None]
    rows_live = jnp.sum(jnp.where(matches, grid[None, :, 0], 0), axis=1)
    cols_live = jnp.sum(jnp.where(matches, grid[None, :, 1], 0), axis=1)
    text_lens = jnp.sum(jnp.where(matches, text_len[None, :], 0), axis=1)
    video_live = (token_row[None, :] < rows_live[:, None]) & (
        token_col[None, :] < cols_live[:, None]
    )
    text_live = (text_index[None, :] < text_lens[:, None]) & (within < block_tokens + text_rows)[None, :]
    return jnp.where(is_video[None, :], video_live, text_live).astype(jnp.float32)


def projector(stacked, piece):
    return jnp.einsum("gld,cde->cgle", stacked, piece, preferred_element_type=jnp.float32)


def attention_step(queries, owners, grid, text_len, span, block_tokens, tile, text_rows):
    score_scale = queries.shape[3] ** (-0.5)

    def attend(carry, pieces, start):
        key_piece, value_piece = pieces
        live_keys = key_mask(
            key_piece.shape[1], owners, grid, text_len, span, block_tokens, tile, text_rows
        )
        scores = (
            jnp.einsum("gqhd,gkhd->gqhk", queries, key_piece, preferred_element_type=jnp.float32)
            * score_scale
        )
        raw_weights = jnp.exp(scores) * live_keys[:, None, None, :]
        weighted = jnp.einsum(
            "gqhk,gkhd->gqhd",
            raw_weights.astype(jnp.bfloat16),
            value_piece,
            preferred_element_type=jnp.float32,
        )
        return (weighted, jnp.sum(raw_weights, axis=3))

    return attend


def shards(
    hidden,
    text_hidden,
    text_len,
    grid,
    timestep,
    modulation,
    q_gain,
    k_gain,
    w_qkv,
    w_out,
    w_up,
    w_down,
    w_proj,
    latent,
    conv_w,
):
    col_count = lax.axis_size("col")
    request_id = lax.axis_index("req")
    row_id = lax.axis_index("row")
    col_id = lax.axis_index("col")
    block_tokens = hidden.shape[1]
    tile = block_tokens // col_count
    text_rows = text_hidden.shape[1]
    head_dim = q_gain.shape[0]
    adaptive = modulation[0]
    source = hidden[0].astype(jnp.float32)
    joined = jnp.concatenate(
        [
            modulate(source, adaptive[0], adaptive[1]),
            modulate(text_hidden[0].astype(jnp.float32), adaptive[0], adaptive[1]),
        ],
        axis=0,
    )
    span = joined.shape[0]
    stacked = joined[None]
    owners = jnp.reshape(request_id, (1,))
    half_cols = w_qkv.shape[2] // 2
    own_half = lax.dynamic_slice_in_dim(w_qkv, request_id * half_cols, half_cols, 2)
    gathered_half = lax.all_gather(own_half, "row", axis=1, tiled=True)
    qkv = projector(stacked, lax.all_gather(gathered_half, "req", axis=2, tiled=True))
    groups = stacked.shape[0]
    heads_here = qkv.shape[3] // head_dim
    shaped = qkv.reshape(3, groups, span, heads_here, head_dim)
    queries = head_norm(shaped[0, :, :block_tokens], q_gain)
    key_block = head_norm(shaped[1], k_gain)
    value_block = shaped[2].astype(jnp.bfloat16)
    attend = attention_step(queries, owners, grid, text_len, span, block_tokens, tile, text_rows)
    empty_state = (jnp.zeros(queries.shape, jnp.float32), jnp.zeros(queries.shape[:3], jnp.float32))
    padded_span = 128 * pl.cdiv(span, 128)
    both = jnp.stack([key_block[0], value_block[0]], axis=0).reshape(2, span, heads_here * head_dim)
    both = jnp.pad(both, ((0, 0), (0, padded_span - span), (0, 0)))[None]
    gathered = lax.all_gather(both, "row", axis=0, tiled=True)
    live = key_mask(
        gathered.shape[0] * padded_span, owners, grid, text_len, padded_span, block_tokens, tile, text_rows
    )
    attended = attention(
        queries[0].reshape(block_tokens, heads_here * head_dim),
        gathered,
        live,
        head_dim ** (-0.5),
    )
    partial_out = jnp.dot(attended, w_out, preferred_element_type=jnp.float32)
    projected = scatter_sum(partial_out, "col", 1)
    own_rows = lax.dynamic_slice_in_dim(source, col_id * tile, tile, 0)
    mixed = lax.optimization_barrier(
        (own_rows + adaptive[2] * projected).astype(jnp.bfloat16)
    ).astype(jnp.float32)
    second_norm = modulate(mixed, adaptive[3], adaptive[4])
    hidden_units = jax.nn.gelu(
        jnp.dot(
            lax.all_gather(second_norm, "row", axis=0, tiled=True),
            w_up,
            preferred_element_type=jnp.float32,
        ),
        approximate=True,
    ).astype(jnp.bfloat16)
    feed_terms = jnp.dot(hidden_units, w_down, preferred_element_type=jnp.float32)
    feed_out = scatter_sum(feed_terms.astype(jnp.bfloat16), "row", 0)
    out_hidden = (mixed + adaptive[5] * feed_out).astype(jnp.bfloat16)
    final_norm = modulate(out_hidden.astype(jnp.float32), adaptive[6], adaptive[7])
    velocity = jnp.dot(final_norm, w_proj, preferred_element_type=jnp.float32)
    local_ids = jnp.arange(tile, dtype=jnp.int32)
    token_row = row_id * TR + local_ids // TC % TR
    token_col = col_id * TC + local_ids % TC
    rows_live = pick_entry(grid[:, 0], request_id)
    cols_live = pick_entry(grid[:, 1], request_id)
    live_tokens = ((token_row < rows_live) & (token_col < cols_live)).astype(jnp.float32)
    keep_part, velocity_part = solver_weights(pick_entry(timestep, request_id))
    updated = (keep_part * latent[0] + velocity_part * velocity) * live_tokens[:, None]
    pixels = (
        updated.reshape(FR, TR, TC, CH, 2, 2)
        .transpose(0, 1, 4, 2, 5, 3)
        .reshape(FR, 2 * TR, 2 * TC, CH)
    )
    scaled = (pixels / latent_scale).astype(jnp.bfloat16)
    padded = extended(scaled, (("row", 1), ("col", 2)), 1)
    running = jnp.zeros((FR, 2 * TR, 2 * TC, conv_w.shape[3]), jnp.float32)
    for row_tap in range(3):
        for col_tap in range(3):
            window = padded[:, row_tap : row_tap + 2 * TR, col_tap : col_tap + 2 * TC, :]
            running = running + jnp.einsum(
                "fyxc,cd->fyxd",
                window,
                conv_w[row_tap, col_tap],
                preferred_element_type=jnp.float32,
            )
    return (out_hidden[None], updated[None], running.astype(jnp.bfloat16)[None])


def solution(mesh):
    placed = (
        P("req", "row", None),
        P("req", "row", None),
        P(),
        P(),
        P(),
        P("req", None, None),
        P(),
        P(),
        P(None, "row", "col"),
        P("col", None),
        P(None, "row"),
        P("row", None),
        P(),
        P("req", ("row", "col"), None),
        P(),
    )
    return jax.shard_map(
        shards,
        mesh=mesh,
        in_specs=placed,
        out_specs=(
            P("req", ("row", "col"), None),
            P("req", ("row", "col"), None),
            P("req", None, "row", "col", None),
        ),
        check_vma=False,
    )
```

```python
import functools

import jax
import jax.numpy as jnp
from jax import lax
from jax.sharding import PartitionSpec as P
from jax.experimental import pallas as pl
from jax.experimental.pallas import tpu as pltpu

MESH_IDS = pl.DeviceIdType.MESH

CH = 16
FR = 6
TR = 1
TC = 4
TRAIN_STEPS = 1000
STRIDE = 250


latent_scale = 0.7


def extended(cells, sides, width):
    for axis, dim in sides:
        count = lax.axis_size(axis)
        ends = count - 1
        head = lax.slice_in_dim(cells, 0, width, axis=dim)
        tail = lax.slice_in_dim(cells, cells.shape[dim] - width, cells.shape[dim], axis=dim)
        cells = jnp.concatenate(
            [
                lax.ppermute(tail, axis, [(i, (i + 1) % count) for i in range(ends)]),
                cells,
                lax.ppermute(head, axis, [((i + 1) % count, i) for i in range(ends)]),
            ],
            axis=dim,
        )
    return cells


def peer_on(axis, peer):
    return tuple(peer if name == axis else lax.axis_index(name) for name in ("req", "row", "col"))


def scatter_sum_kernel(axis, count, rows, part_ref, out_ref, landed, send_sems, recv_sems, own_sem):
    me = lax.axis_index(axis)
    barrier = pltpu.get_barrier_semaphore()
    for step in range(1, count):
        peer = lax.rem(me + step, count)
        pl.semaphore_signal(barrier, inc=1, device_id=peer_on(axis, peer), device_id_type=MESH_IDS)
    pl.semaphore_wait(barrier, count - 1)
    own = pltpu.make_async_copy(part_ref.at[pl.ds(me * rows, rows)], landed.at[me], own_sem)
    own.start()
    sends = []
    for step in range(1, count):
        peer = lax.rem(me + step, count)
        copy = pltpu.make_async_remote_copy(
            src_ref=part_ref.at[pl.ds(peer * rows, rows)],
            dst_ref=landed.at[me],
            send_sem=send_sems.at[step],
            recv_sem=recv_sems.at[step],
            device_id=peer_on(axis, peer),
            device_id_type=MESH_IDS,
        )
        copy.start()
        sends.append(copy)
    own.wait()
    for step in range(1, count):
        source = lax.rem(me + count - step, count)
        pltpu.make_async_remote_copy(
            src_ref=part_ref.at[pl.ds(me * rows, rows)],
            dst_ref=landed.at[source],
            send_sem=send_sems.at[step],
            recv_sem=recv_sems.at[step],
            device_id=peer_on(axis, source),
            device_id_type=MESH_IDS,
        ).wait_recv()
    for copy in sends:
        copy.wait_send()
    total = landed[0].astype(jnp.float32)
    for slot in range(1, count):
        total = total + landed[slot].astype(jnp.float32)
    out_ref[...] = total


def scatter_sum(part, axis, kernel_id):
    count = lax.axis_size(axis)
    rows = part.shape[0] // count
    width = part.shape[1]
    return pl.pallas_call(
        functools.partial(scatter_sum_kernel, axis, count, rows),
        out_shape=jax.ShapeDtypeStruct((rows, width), jnp.float32),
        in_specs=[pl.BlockSpec(memory_space=pl.ANY)],
        out_specs=pl.BlockSpec(memory_space=pltpu.VMEM),
        scratch_shapes=[
            pltpu.VMEM((count, rows, width), part.dtype),
            pltpu.SemaphoreType.DMA((count,)),
            pltpu.SemaphoreType.DMA((count,)),
            pltpu.SemaphoreType.DMA(()),
        ],
        compiler_params=pltpu.CompilerParams(
            collective_id=kernel_id, has_side_effects=True, vmem_limit_bytes=48 * 1024 * 1024
        ),
    )(part)


def attention_kernel(scale, q_ref, kv_ref, live_ref, out_ref):
    sources, _, block, width = kv_ref.shape
    lane = lax.broadcasted_iota(jnp.int32, (1, 128), 1)
    first = lane < 64
    live = live_ref[...]
    for pair in range(width // 128):
        cols = slice(pair * 128, (pair + 1) * 128)
        query = q_ref[:, cols]
        keys = kv_ref[:, 0, :, cols].reshape(sources * block, 128)
        values = kv_ref[:, 1, :, cols].reshape(sources * block, 128)
        results = []
        for half in (first, jnp.logical_not(first)):
            picked = jnp.where(half, query, jnp.zeros_like(query))
            scores = lax.dot_general(
                picked, keys, (((1,), (1,)), ((), ())), preferred_element_type=jnp.float32
            ) * scale
            weights = jnp.exp(scores) * live
            totals = jnp.sum(weights, axis=1, keepdims=True)
            summed = jnp.dot(weights.astype(jnp.bfloat16), values, preferred_element_type=jnp.float32)
            results.append(summed / totals)
        out_ref[:, cols] = jnp.where(first, results[0], results[1]).astype(out_ref.dtype)


def attention(queries, gathered, live, scale):
    return pl.pallas_call(
        functools.partial(attention_kernel, scale),
        out_shape=jax.ShapeDtypeStruct(queries.shape, jnp.bfloat16),
        in_specs=[pl.BlockSpec(memory_space=pltpu.VMEM)] * 3,
        out_specs=pl.BlockSpec(memory_space=pltpu.VMEM),
        compiler_params=pltpu.CompilerParams(vmem_limit_bytes=56 * 1024 * 1024),
    )(queries, gathered, live)


def ring_scatter_kernel(zs, xs, part_ref, out_ref, landed, outgoing, own_sum, crossed, ring_send, ring_recv, cross_send, cross_recv):
    me = lax.axis_index("row")
    xm = me // zs
    zm = me % zs
    ahead = xm * zs + lax.rem(zm + 1, zs)
    behind = xm * zs + lax.rem(zm + zs - 1, zs)
    half = part_ref.shape[3] // 2
    barrier = pltpu.get_barrier_semaphore()
    targets = [ahead, behind] + [lax.rem(xm + k, xs) * zs + zm for k in range(1, xs)]
    for peer in targets:
        pl.semaphore_signal(barrier, inc=1, device_id=peer_on("row", peer), device_id_type=MESH_IDS)
    pl.semaphore_wait(barrier, len(targets))
    ways = ((0, ahead, behind, -1), (1, behind, ahead, 1))
    pending = []
    for step in range(zs - 1):
        for way, dest, origin, sign in ways:
            cols = pl.ds(way * half, half)
            chunk = lax.rem(zm + sign * (1 + step) + 2 * zs, zs)
            if step == 0:
                source = part_ref.at[chunk, :, :, cols]
            else:
                arrived = pltpu.make_async_remote_copy(
                    src_ref=outgoing.at[way, step - 1],
                    dst_ref=landed.at[way, step - 1],
                    send_sem=ring_send.at[way, step - 1],
                    recv_sem=ring_recv.at[way, step - 1],
                    device_id=peer_on("row", origin),
                    device_id_type=MESH_IDS,
                )
                arrived.wait_recv()
                outgoing[way, step] = (
                    landed[way, step - 1].astype(jnp.float32)
                    + part_ref[chunk, :, :, cols].astype(jnp.float32)
                ).astype(outgoing.dtype)
                source = outgoing.at[way, step]
            copy = pltpu.make_async_remote_copy(
                src_ref=source,
                dst_ref=landed.at[way, step],
                send_sem=ring_send.at[way, step],
                recv_sem=ring_recv.at[way, step],
                device_id=peer_on("row", dest),
                device_id_type=MESH_IDS,
            )
            copy.start()
            pending.append(copy)
    last = zs - 2
    for way, dest, origin, sign in ways:
        cols = pl.ds(way * half, half)
        pltpu.make_async_remote_copy(
            src_ref=outgoing.at[way, last],
            dst_ref=landed.at[way, last],
            send_sem=ring_send.at[way, last],
            recv_sem=ring_recv.at[way, last],
            device_id=peer_on("row", origin),
            device_id_type=MESH_IDS,
        ).wait_recv()
        own_sum[:, :, cols] = landed[way, last].astype(jnp.float32) + part_ref[zm, :, :, cols].astype(jnp.float32)
    crossed[0] = own_sum[...].astype(crossed.dtype)
    sends = []
    for k in range(1, xs):
        peer_x = lax.rem(xm + k, xs)
        copy = pltpu.make_async_remote_copy(
            src_ref=crossed.at[0, peer_x],
            dst_ref=crossed.at[k, 0],
            send_sem=cross_send.at[k],
            recv_sem=cross_recv.at[k],
            device_id=peer_on("row", peer_x * zs + zm),
            device_id_type=MESH_IDS,
        )
        copy.start()
        sends.append(copy)
    total = own_sum[xm]
    for k in range(1, xs):
        origin_x = lax.rem(xm + xs - k, xs)
        pltpu.make_async_remote_copy(
            src_ref=crossed.at[0, 0],
            dst_ref=crossed.at[k, 0],
            send_sem=cross_send.at[k],
            recv_sem=cross_recv.at[k],
            device_id=peer_on("row", origin_x * zs + zm),
            device_id_type=MESH_IDS,
        ).wait_recv()
        total = total + crossed[k, 0].astype(jnp.float32)
    out_ref[...] = total
    for copy in pending + sends:
        copy.wait_send()


def ring_scatter_sum(part, xs, zs, kernel_id):
    rows = part.shape[0] // (xs * zs)
    width = part.shape[1]
    arranged = part.reshape(xs, zs, rows, width).transpose(1, 0, 2, 3)
    return pl.pallas_call(
        functools.partial(ring_scatter_kernel, zs, xs),
        out_shape=jax.ShapeDtypeStruct((rows, width), jnp.float32),
        in_specs=[pl.BlockSpec(memory_space=pltpu.VMEM)],
        out_specs=pl.BlockSpec(memory_space=pltpu.VMEM),
        scratch_shapes=[
            pltpu.VMEM((2, zs - 1, xs, rows, width // 2), part.dtype),
            pltpu.VMEM((2, zs - 1, xs, rows, width // 2), part.dtype),
            pltpu.VMEM((xs, rows, width), jnp.float32),
            pltpu.VMEM((xs, xs, rows, width), part.dtype),
            pltpu.SemaphoreType.DMA((2, zs - 1)),
            pltpu.SemaphoreType.DMA((2, zs - 1)),
            pltpu.SemaphoreType.DMA((xs,)),
            pltpu.SemaphoreType.DMA((xs,)),
        ],
        compiler_params=pltpu.CompilerParams(
            collective_id=kernel_id, has_side_effects=True, vmem_limit_bytes=56 * 1024 * 1024
        ),
    )(arranged)


def layer_norm(tensor, epsilon):
    average = jnp.mean(tensor, axis=-1, keepdims=True)
    centered = tensor - average
    spread = jnp.mean(centered * centered, axis=-1, keepdims=True)
    return centered * lax.rsqrt(spread + epsilon)


def modulate(tensor, offset, factor):
    return (layer_norm(tensor, 1e-05) * (1.0 + factor) + offset).astype(jnp.bfloat16)


def head_norm(tensor, scaling):
    return (layer_norm(tensor, 1e-06) * scaling).astype(jnp.bfloat16)


def pick_entry(entries, position):
    slot_ids = jnp.arange(entries.shape[0], dtype=jnp.int32)
    return jnp.sum(jnp.where(slot_ids == position, entries, jnp.zeros_like(entries)))


def solver_weights(step_index):
    plan = jnp.linspace(0.00085**0.5, 0.012**0.5, TRAIN_STEPS, dtype=jnp.float32) ** 2
    cumulative = jnp.cumprod(1.0 - plan)
    alpha_now = pick_entry(cumulative, step_index)
    alpha_prev = pick_entry(cumulative, step_index - STRIDE)
    root_now = jnp.sqrt(alpha_now)
    rest_now = jnp.sqrt(1.0 - alpha_now)
    root_prev = jnp.sqrt(alpha_prev)
    rest_prev = jnp.sqrt(1.0 - alpha_prev)
    return (
        root_prev * root_now + rest_prev * rest_now,
        rest_prev * root_now - root_prev * rest_now,
    )


def key_mask(count, owners, grid, text_len, span, block_tokens, tile, text_rows):
    positions = jnp.arange(count, dtype=jnp.int32)
    owner_row = positions // span
    within = positions % span
    is_video = within < block_tokens
    owner_col = within // tile
    local_ids = within % tile
    token_row = owner_row * TR + local_ids // TC % TR
    token_col = owner_col * TC + local_ids % TC
    text_index = owner_row * text_rows + within - block_tokens
    matches = jnp.arange(grid.shape[0], dtype=jnp.int32)[None, :] == owners[:, None]
    rows_live = jnp.sum(jnp.where(matches, grid[None, :, 0], 0), axis=1)
    cols_live = jnp.sum(jnp.where(matches, grid[None, :, 1], 0), axis=1)
    text_lens = jnp.sum(jnp.where(matches, text_len[None, :], 0), axis=1)
    video_live = (token_row[None, :] < rows_live[:, None]) & (
        token_col[None, :] < cols_live[:, None]
    )
    text_live = (text_index[None, :] < text_lens[:, None]) & (within < block_tokens + text_rows)[None, :]
    return jnp.where(is_video[None, :], video_live, text_live).astype(jnp.float32)


def projector(stacked, piece):
    return jnp.einsum("gld,cde->cgle", stacked, piece, preferred_element_type=jnp.float32)


def attention_step(queries, owners, grid, text_len, span, block_tokens, tile, text_rows):
    score_scale = queries.shape[3] ** (-0.5)

    def attend(carry, pieces, start):
        key_piece, value_piece = pieces
        live_keys = key_mask(
            key_piece.shape[1], owners, grid, text_len, span, block_tokens, tile, text_rows
        )
        scores = (
            jnp.einsum("gqhd,gkhd->gqhk", queries, key_piece, preferred_element_type=jnp.float32)
            * score_scale
        )
        raw_weights = jnp.exp(scores) * live_keys[:, None, None, :]
        weighted = jnp.einsum(
            "gqhk,gkhd->gqhd",
            raw_weights.astype(jnp.bfloat16),
            value_piece,
            preferred_element_type=jnp.float32,
        )
        return (weighted, jnp.sum(raw_weights, axis=3))

    return attend


def shards(
    hidden,
    text_hidden,
    text_len,
    grid,
    timestep,
    modulation,
    q_gain,
    k_gain,
    w_qkv,
    w_out,
    w_up,
    w_down,
    w_proj,
    latent,
    conv_w,
):
    col_count = lax.axis_size("col")
    request_id = lax.axis_index("req")
    row_id = lax.axis_index("row")
    col_id = lax.axis_index("col")
    block_tokens = hidden.shape[1]
    tile = block_tokens // col_count
    text_rows = text_hidden.shape[1]
    head_dim = q_gain.shape[0]
    adaptive = modulation[0]
    source = hidden[0].astype(jnp.float32)
    joined = jnp.concatenate(
        [
            modulate(source, adaptive[0], adaptive[1]),
            modulate(text_hidden[0].astype(jnp.float32), adaptive[0], adaptive[1]),
        ],
        axis=0,
    )
    span = joined.shape[0]
    stacked = joined[None]
    owners = jnp.reshape(request_id, (1,))
    half_cols = w_qkv.shape[2] // 2
    own_half = lax.dynamic_slice_in_dim(w_qkv, request_id * half_cols, half_cols, 2)
    gathered_half = lax.all_gather(own_half, "row", axis=1, tiled=True)
    qkv = projector(stacked, lax.all_gather(gathered_half, "req", axis=2, tiled=True))
    groups = stacked.shape[0]
    heads_here = qkv.shape[3] // head_dim
    shaped = qkv.reshape(3, groups, span, heads_here, head_dim)
    queries = head_norm(shaped[0, :, :block_tokens], q_gain)
    key_block = head_norm(shaped[1], k_gain)
    value_block = shaped[2].astype(jnp.bfloat16)
    attend = attention_step(queries, owners, grid, text_len, span, block_tokens, tile, text_rows)
    empty_state = (jnp.zeros(queries.shape, jnp.float32), jnp.zeros(queries.shape[:3], jnp.float32))
    padded_span = 128 * pl.cdiv(span, 128)
    both = jnp.stack([key_block[0], value_block[0]], axis=0).reshape(2, span, heads_here * head_dim)
    both = jnp.pad(both, ((0, 0), (0, padded_span - span), (0, 0)))[None]
    gathered = lax.all_gather(both, "row", axis=0, tiled=True)
    live = key_mask(
        gathered.shape[0] * padded_span, owners, grid, text_len, padded_span, block_tokens, tile, text_rows
    )
    attended = attention(
        queries[0].reshape(block_tokens, heads_here * head_dim),
        gathered,
        live,
        head_dim ** (-0.5),
    )
    partial_out = jnp.dot(attended, w_out, preferred_element_type=jnp.float32)
    projected = scatter_sum(partial_out, "col", 1)
    own_rows = lax.dynamic_slice_in_dim(source, col_id * tile, tile, 0)
    mixed = lax.optimization_barrier(
        (own_rows + adaptive[2] * projected).astype(jnp.bfloat16)
    ).astype(jnp.float32)
    second_norm = modulate(mixed, adaptive[3], adaptive[4])
    hidden_units = jax.nn.gelu(
        jnp.dot(
            lax.all_gather(second_norm, "row", axis=0, tiled=True),
            w_up,
            preferred_element_type=jnp.float32,
        ),
        approximate=True,
    ).astype(jnp.bfloat16)
    feed_terms = jnp.dot(hidden_units, w_down, preferred_element_type=jnp.float32)
    feed_out = ring_scatter_sum(feed_terms.astype(jnp.bfloat16), 4, 8, 0)
    out_hidden = (mixed + adaptive[5] * feed_out).astype(jnp.bfloat16)
    final_norm = modulate(out_hidden.astype(jnp.float32), adaptive[6], adaptive[7])
    velocity = jnp.dot(final_norm, w_proj, preferred_element_type=jnp.float32)
    local_ids = jnp.arange(tile, dtype=jnp.int32)
    token_row = row_id * TR + local_ids // TC % TR
    token_col = col_id * TC + local_ids % TC
    rows_live = pick_entry(grid[:, 0], request_id)
    cols_live = pick_entry(grid[:, 1], request_id)
    live_tokens = ((token_row < rows_live) & (token_col < cols_live)).astype(jnp.float32)
    keep_part, velocity_part = solver_weights(pick_entry(timestep, request_id))
    updated = (keep_part * latent[0] + velocity_part * velocity) * live_tokens[:, None]
    pixels = (
        updated.reshape(FR, TR, TC, CH, 2, 2)
        .transpose(0, 1, 4, 2, 5, 3)
        .reshape(FR, 2 * TR, 2 * TC, CH)
    )
    scaled = (pixels / latent_scale).astype(jnp.bfloat16)
    padded = extended(scaled, (("row", 1), ("col", 2)), 1)
    running = jnp.zeros((FR, 2 * TR, 2 * TC, conv_w.shape[3]), jnp.float32)
    for row_tap in range(3):
        for col_tap in range(3):
            window = padded[:, row_tap : row_tap + 2 * TR, col_tap : col_tap + 2 * TC, :]
            running = running + jnp.einsum(
                "fyxc,cd->fyxd",
                window,
                conv_w[row_tap, col_tap],
                preferred_element_type=jnp.float32,
            )
    return (out_hidden[None], updated[None], running.astype(jnp.bfloat16)[None])


def solution(mesh):
    placed = (
        P("req", "row", None),
        P("req", "row", None),
        P(),
        P(),
        P(),
        P("req", None, None),
        P(),
        P(),
        P(None, "row", "col"),
        P("col", None),
        P(None, "row"),
        P("row", None),
        P(),
        P("req", ("row", "col"), None),
        P(),
    )
    return jax.shard_map(
        shards,
        mesh=mesh,
        in_specs=placed,
        out_specs=(
            P("req", ("row", "col"), None),
            P("req", ("row", "col"), None),
            P("req", None, "row", "col", None),
        ),
        check_vma=False,
    )
```

```python
import functools

import jax
import jax.numpy as jnp
from jax import lax
from jax.sharding import PartitionSpec as P
from jax.experimental import pallas as pl
from jax.experimental.pallas import tpu as pltpu

MESH_IDS = pl.DeviceIdType.MESH

CH = 16
FR = 6
TR = 1
TC = 4
TRAIN_STEPS = 1000
STRIDE = 250


latent_scale = 0.7


def extended(cells, sides, width):
    for axis, dim in sides:
        count = lax.axis_size(axis)
        ends = count - 1
        head = lax.slice_in_dim(cells, 0, width, axis=dim)
        tail = lax.slice_in_dim(cells, cells.shape[dim] - width, cells.shape[dim], axis=dim)
        cells = jnp.concatenate(
            [
                lax.ppermute(tail, axis, [(i, (i + 1) % count) for i in range(ends)]),
                cells,
                lax.ppermute(head, axis, [((i + 1) % count, i) for i in range(ends)]),
            ],
            axis=dim,
        )
    return cells


def peer_on(axis, peer):
    return tuple(peer if name == axis else lax.axis_index(name) for name in ("req", "row", "col"))


def scatter_sum_kernel(axis, count, rows, part_ref, out_ref, landed, send_sems, recv_sems, own_sem):
    me = lax.axis_index(axis)
    barrier = pltpu.get_barrier_semaphore()
    for step in range(1, count):
        peer = lax.rem(me + step, count)
        pl.semaphore_signal(barrier, inc=1, device_id=peer_on(axis, peer), device_id_type=MESH_IDS)
    pl.semaphore_wait(barrier, count - 1)
    own = pltpu.make_async_copy(part_ref.at[pl.ds(me * rows, rows)], landed.at[me], own_sem)
    own.start()
    sends = []
    for step in range(1, count):
        peer = lax.rem(me + step, count)
        copy = pltpu.make_async_remote_copy(
            src_ref=part_ref.at[pl.ds(peer * rows, rows)],
            dst_ref=landed.at[me],
            send_sem=send_sems.at[step],
            recv_sem=recv_sems.at[step],
            device_id=peer_on(axis, peer),
            device_id_type=MESH_IDS,
        )
        copy.start()
        sends.append(copy)
    own.wait()
    for step in range(1, count):
        source = lax.rem(me + count - step, count)
        pltpu.make_async_remote_copy(
            src_ref=part_ref.at[pl.ds(me * rows, rows)],
            dst_ref=landed.at[source],
            send_sem=send_sems.at[step],
            recv_sem=recv_sems.at[step],
            device_id=peer_on(axis, source),
            device_id_type=MESH_IDS,
        ).wait_recv()
    for copy in sends:
        copy.wait_send()
    total = landed[0].astype(jnp.float32)
    for slot in range(1, count):
        total = total + landed[slot].astype(jnp.float32)
    out_ref[...] = total


def scatter_sum(part, axis, kernel_id):
    count = lax.axis_size(axis)
    rows = part.shape[0] // count
    width = part.shape[1]
    return pl.pallas_call(
        functools.partial(scatter_sum_kernel, axis, count, rows),
        out_shape=jax.ShapeDtypeStruct((rows, width), jnp.float32),
        in_specs=[pl.BlockSpec(memory_space=pl.ANY)],
        out_specs=pl.BlockSpec(memory_space=pltpu.VMEM),
        scratch_shapes=[
            pltpu.VMEM((count, rows, width), part.dtype),
            pltpu.SemaphoreType.DMA((count,)),
            pltpu.SemaphoreType.DMA((count,)),
            pltpu.SemaphoreType.DMA(()),
        ],
        compiler_params=pltpu.CompilerParams(
            collective_id=kernel_id, has_side_effects=True, vmem_limit_bytes=48 * 1024 * 1024
        ),
    )(part)


def attention_kernel(scale, q_ref, kv_ref, live_ref, out_ref):
    sources, _, block, width = kv_ref.shape
    lane = lax.broadcasted_iota(jnp.int32, (1, 128), 1)
    first = lane < 64
    live = live_ref[...]
    for pair in range(width // 128):
        cols = slice(pair * 128, (pair + 1) * 128)
        query = q_ref[:, cols]
        keys = kv_ref[:, 0, :, cols].reshape(sources * block, 128)
        values = kv_ref[:, 1, :, cols].reshape(sources * block, 128)
        results = []
        for half in (first, jnp.logical_not(first)):
            picked = jnp.where(half, query, jnp.zeros_like(query))
            scores = lax.dot_general(
                picked, keys, (((1,), (1,)), ((), ())), preferred_element_type=jnp.float32
            ) * scale
            weights = jnp.exp(scores) * live
            totals = jnp.sum(weights, axis=1, keepdims=True)
            summed = jnp.dot(weights.astype(jnp.bfloat16), values, preferred_element_type=jnp.float32)
            results.append(summed / totals)
        out_ref[:, cols] = jnp.where(first, results[0], results[1]).astype(out_ref.dtype)


def attention(queries, gathered, live, scale):
    return pl.pallas_call(
        functools.partial(attention_kernel, scale),
        out_shape=jax.ShapeDtypeStruct(queries.shape, jnp.bfloat16),
        in_specs=[pl.BlockSpec(memory_space=pltpu.VMEM)] * 3,
        out_specs=pl.BlockSpec(memory_space=pltpu.VMEM),
        compiler_params=pltpu.CompilerParams(vmem_limit_bytes=56 * 1024 * 1024),
    )(queries, gathered, live)


def ring_scatter_kernel(zs, xs, part_ref, out_ref, landed, outgoing, own_sum, crossed, ring_send, ring_recv, cross_send, cross_recv):
    me = lax.axis_index("row")
    xm = me // zs
    zm = me % zs
    ahead = xm * zs + lax.rem(zm + 1, zs)
    behind = xm * zs + lax.rem(zm + zs - 1, zs)
    half = part_ref.shape[3] // 2
    barrier = pltpu.get_barrier_semaphore()
    targets = [ahead, behind] + [lax.rem(xm + k, xs) * zs + zm for k in range(1, xs)]
    for peer in targets:
        pl.semaphore_signal(barrier, inc=1, device_id=peer_on("row", peer), device_id_type=MESH_IDS)
    pl.semaphore_wait(barrier, len(targets))
    ways = ((0, ahead, behind, -1), (1, behind, ahead, 1))
    pending = []
    for step in range(zs - 1):
        for way, dest, origin, sign in ways:
            cols = pl.ds(way * half, half)
            chunk = lax.rem(zm + sign * (1 + step) + 2 * zs, zs)
            if step == 0:
                source = part_ref.at[chunk, :, :, cols]
            else:
                arrived = pltpu.make_async_remote_copy(
                    src_ref=outgoing.at[way, step - 1],
                    dst_ref=landed.at[way, step - 1],
                    send_sem=ring_send.at[way, step - 1],
                    recv_sem=ring_recv.at[way, step - 1],
                    device_id=peer_on("row", origin),
                    device_id_type=MESH_IDS,
                )
                arrived.wait_recv()
                outgoing[way, step] = (
                    landed[way, step - 1].astype(jnp.float32)
                    + part_ref[chunk, :, :, cols].astype(jnp.float32)
                ).astype(outgoing.dtype)
                source = outgoing.at[way, step]
            copy = pltpu.make_async_remote_copy(
                src_ref=source,
                dst_ref=landed.at[way, step],
                send_sem=ring_send.at[way, step],
                recv_sem=ring_recv.at[way, step],
                device_id=peer_on("row", dest),
                device_id_type=MESH_IDS,
            )
            copy.start()
            pending.append(copy)
    last = zs - 2
    for way, dest, origin, sign in ways:
        cols = pl.ds(way * half, half)
        pltpu.make_async_remote_copy(
            src_ref=outgoing.at[way, last],
            dst_ref=landed.at[way, last],
            send_sem=ring_send.at[way, last],
            recv_sem=ring_recv.at[way, last],
            device_id=peer_on("row", origin),
            device_id_type=MESH_IDS,
        ).wait_recv()
        own_sum[:, :, cols] = landed[way, last].astype(jnp.float32) + part_ref[zm, :, :, cols].astype(jnp.float32)
    crossed[0] = own_sum[...].astype(crossed.dtype)
    sends = []
    for k in range(1, xs):
        peer_x = lax.rem(xm + k, xs)
        copy = pltpu.make_async_remote_copy(
            src_ref=crossed.at[0, peer_x],
            dst_ref=crossed.at[k, 0],
            send_sem=cross_send.at[k],
            recv_sem=cross_recv.at[k],
            device_id=peer_on("row", peer_x * zs + zm),
            device_id_type=MESH_IDS,
        )
        copy.start()
        sends.append(copy)
    total = own_sum[xm]
    for k in range(1, xs):
        origin_x = lax.rem(xm + xs - k, xs)
        pltpu.make_async_remote_copy(
            src_ref=crossed.at[0, 0],
            dst_ref=crossed.at[k, 0],
            send_sem=cross_send.at[k],
            recv_sem=cross_recv.at[k],
            device_id=peer_on("row", origin_x * zs + zm),
            device_id_type=MESH_IDS,
        ).wait_recv()
        total = total + crossed[k, 0].astype(jnp.float32)
    out_ref[...] = total
    for copy in pending + sends:
        copy.wait_send()


def ring_scatter_sum(part, xs, zs, kernel_id):
    rows = part.shape[0] // (xs * zs)
    width = part.shape[1]
    arranged = part.reshape(zs, xs, rows, width)
    return pl.pallas_call(
        functools.partial(ring_scatter_kernel, zs, xs),
        out_shape=jax.ShapeDtypeStruct((rows, width), jnp.float32),
        in_specs=[pl.BlockSpec(memory_space=pltpu.VMEM)],
        out_specs=pl.BlockSpec(memory_space=pltpu.VMEM),
        scratch_shapes=[
            pltpu.VMEM((2, zs - 1, xs, rows, width // 2), part.dtype),
            pltpu.VMEM((2, zs - 1, xs, rows, width // 2), part.dtype),
            pltpu.VMEM((xs, rows, width), jnp.float32),
            pltpu.VMEM((xs, xs, rows, width), part.dtype),
            pltpu.SemaphoreType.DMA((2, zs - 1)),
            pltpu.SemaphoreType.DMA((2, zs - 1)),
            pltpu.SemaphoreType.DMA((xs,)),
            pltpu.SemaphoreType.DMA((xs,)),
        ],
        compiler_params=pltpu.CompilerParams(
            collective_id=kernel_id, has_side_effects=True, vmem_limit_bytes=56 * 1024 * 1024
        ),
    )(arranged)


def ring_gather_kernel(zs, xs, block_ref, out_ref, held, own_sem, ring_send, ring_recv, cross_send, cross_recv):
    me = lax.axis_index("row")
    xm = me // zs
    zm = me % zs
    ahead = xm * zs + lax.rem(zm + 1, zs)
    behind = xm * zs + lax.rem(zm + zs - 1, zs)
    barrier = pltpu.get_barrier_semaphore()
    targets = [ahead, behind] + [lax.rem(xm + k, xs) * zs + zm for k in range(1, xs)]
    for peer in targets:
        pl.semaphore_signal(barrier, inc=1, device_id=peer_on("row", peer), device_id_type=MESH_IDS)
    pl.semaphore_wait(barrier, len(targets))
    own = pltpu.make_async_copy(block_ref, held.at[zm, xm], own_sem)
    own.start()
    pending = []
    for k in range(1, xs):
        peer_x = lax.rem(xm + k, xs)
        copy = pltpu.make_async_remote_copy(
            src_ref=block_ref,
            dst_ref=held.at[zm, xm],
            send_sem=cross_send.at[k],
            recv_sem=cross_recv.at[k],
            device_id=peer_on("row", peer_x * zs + zm),
            device_id_type=MESH_IDS,
        )
        copy.start()
        pending.append(copy)
    own.wait()
    for k in range(1, xs):
        origin_x = lax.rem(xm + xs - k, xs)
        pltpu.make_async_remote_copy(
            src_ref=block_ref,
            dst_ref=held.at[zm, origin_x],
            send_sem=cross_send.at[k],
            recv_sem=cross_recv.at[k],
            device_id=peer_on("row", origin_x * zs + zm),
            device_id_type=MESH_IDS,
        ).wait_recv()
    split = xs // 2
    ways = ((0, ahead, behind, -1, pl.ds(0, split)), (1, behind, ahead, 1, pl.ds(split, xs - split)))
    for step in range(zs):
        for way, dest, origin, sign, part in ways:
            group = lax.rem(zm + sign * step + zs, zs)
            if step > 0:
                pltpu.make_async_remote_copy(
                    src_ref=held.at[group, part],
                    dst_ref=held.at[group, part],
                    send_sem=ring_send.at[way, step - 1],
                    recv_sem=ring_recv.at[way, step - 1],
                    device_id=peer_on("row", origin),
                    device_id_type=MESH_IDS,
                ).wait_recv()
            if step < zs - 1:
                copy = pltpu.make_async_remote_copy(
                    src_ref=held.at[group, part],
                    dst_ref=held.at[group, part],
                    send_sem=ring_send.at[way, step],
                    recv_sem=ring_recv.at[way, step],
                    device_id=peer_on("row", dest),
                    device_id_type=MESH_IDS,
                )
                copy.start()
                pending.append(copy)
    for copy in pending:
        copy.wait_send()
    out = pltpu.make_async_copy(held, out_ref, own_sem)
    out.start()
    out.wait()


def ring_gather(block, xs, zs, kernel_id):
    return pl.pallas_call(
        functools.partial(ring_gather_kernel, zs, xs),
        out_shape=jax.ShapeDtypeStruct((zs, xs) + block.shape, block.dtype),
        in_specs=[pl.BlockSpec(memory_space=pltpu.VMEM)],
        out_specs=pl.BlockSpec(memory_space=pl.ANY),
        scratch_shapes=[
            pltpu.VMEM((zs, xs) + block.shape, block.dtype),
            pltpu.SemaphoreType.DMA(()),
            pltpu.SemaphoreType.DMA((2, zs - 1)),
            pltpu.SemaphoreType.DMA((2, zs - 1)),
            pltpu.SemaphoreType.DMA((xs,)),
            pltpu.SemaphoreType.DMA((xs,)),
        ],
        compiler_params=pltpu.CompilerParams(
            collective_id=kernel_id, has_side_effects=True, vmem_limit_bytes=56 * 1024 * 1024
        ),
    )(block)


def layer_norm(tensor, epsilon):
    average = jnp.mean(tensor, axis=-1, keepdims=True)
    centered = tensor - average
    spread = jnp.mean(centered * centered, axis=-1, keepdims=True)
    return centered * lax.rsqrt(spread + epsilon)


def modulate(tensor, offset, factor):
    return (layer_norm(tensor, 1e-05) * (1.0 + factor) + offset).astype(jnp.bfloat16)


def head_norm(tensor, scaling):
    return (layer_norm(tensor, 1e-06) * scaling).astype(jnp.bfloat16)


def pick_entry(entries, position):
    slot_ids = jnp.arange(entries.shape[0], dtype=jnp.int32)
    return jnp.sum(jnp.where(slot_ids == position, entries, jnp.zeros_like(entries)))


def solver_weights(step_index):
    plan = jnp.linspace(0.00085**0.5, 0.012**0.5, TRAIN_STEPS, dtype=jnp.float32) ** 2
    cumulative = jnp.cumprod(1.0 - plan)
    alpha_now = pick_entry(cumulative, step_index)
    alpha_prev = pick_entry(cumulative, step_index - STRIDE)
    root_now = jnp.sqrt(alpha_now)
    rest_now = jnp.sqrt(1.0 - alpha_now)
    root_prev = jnp.sqrt(alpha_prev)
    rest_prev = jnp.sqrt(1.0 - alpha_prev)
    return (
        root_prev * root_now + rest_prev * rest_now,
        rest_prev * root_now - root_prev * rest_now,
    )


def key_mask(count, owners, grid, text_len, span, block_tokens, tile, text_rows):
    positions = jnp.arange(count, dtype=jnp.int32)
    owner_row = positions // span
    within = positions % span
    is_video = within < block_tokens
    owner_col = within // tile
    local_ids = within % tile
    token_row = owner_row * TR + local_ids // TC % TR
    token_col = owner_col * TC + local_ids % TC
    text_index = owner_row * text_rows + within - block_tokens
    matches = jnp.arange(grid.shape[0], dtype=jnp.int32)[None, :] == owners[:, None]
    rows_live = jnp.sum(jnp.where(matches, grid[None, :, 0], 0), axis=1)
    cols_live = jnp.sum(jnp.where(matches, grid[None, :, 1], 0), axis=1)
    text_lens = jnp.sum(jnp.where(matches, text_len[None, :], 0), axis=1)
    video_live = (token_row[None, :] < rows_live[:, None]) & (
        token_col[None, :] < cols_live[:, None]
    )
    text_live = (text_index[None, :] < text_lens[:, None]) & (within < block_tokens + text_rows)[None, :]
    return jnp.where(is_video[None, :], video_live, text_live).astype(jnp.float32)


def projector(stacked, piece):
    return jnp.einsum("gld,cde->cgle", stacked, piece, preferred_element_type=jnp.float32)


def attention_step(queries, owners, grid, text_len, span, block_tokens, tile, text_rows):
    score_scale = queries.shape[3] ** (-0.5)

    def attend(carry, pieces, start):
        key_piece, value_piece = pieces
        live_keys = key_mask(
            key_piece.shape[1], owners, grid, text_len, span, block_tokens, tile, text_rows
        )
        scores = (
            jnp.einsum("gqhd,gkhd->gqhk", queries, key_piece, preferred_element_type=jnp.float32)
            * score_scale
        )
        raw_weights = jnp.exp(scores) * live_keys[:, None, None, :]
        weighted = jnp.einsum(
            "gqhk,gkhd->gqhd",
            raw_weights.astype(jnp.bfloat16),
            value_piece,
            preferred_element_type=jnp.float32,
        )
        return (weighted, jnp.sum(raw_weights, axis=3))

    return attend


def shards(
    hidden,
    text_hidden,
    text_len,
    grid,
    timestep,
    modulation,
    q_gain,
    k_gain,
    w_qkv,
    w_out,
    w_up,
    w_down,
    w_proj,
    latent,
    conv_w,
):
    col_count = lax.axis_size("col")
    request_id = lax.axis_index("req")
    row_id = lax.axis_index("row")
    col_id = lax.axis_index("col")
    block_tokens = hidden.shape[1]
    tile = block_tokens // col_count
    text_rows = text_hidden.shape[1]
    head_dim = q_gain.shape[0]
    adaptive = modulation[0]
    source = hidden[0].astype(jnp.float32)
    joined = jnp.concatenate(
        [
            modulate(source, adaptive[0], adaptive[1]),
            modulate(text_hidden[0].astype(jnp.float32), adaptive[0], adaptive[1]),
        ],
        axis=0,
    )
    span = joined.shape[0]
    stacked = joined[None]
    owners = jnp.reshape(request_id, (1,))
    half_cols = w_qkv.shape[2] // 2
    own_half = lax.dynamic_slice_in_dim(w_qkv, request_id * half_cols, half_cols, 2)
    gathered_half = lax.all_gather(own_half, "row", axis=1, tiled=True)
    qkv = projector(stacked, lax.all_gather(gathered_half, "req", axis=2, tiled=True))
    groups = stacked.shape[0]
    heads_here = qkv.shape[3] // head_dim
    shaped = qkv.reshape(3, groups, span, heads_here, head_dim)
    queries = head_norm(shaped[0, :, :block_tokens], q_gain)
    key_block = head_norm(shaped[1], k_gain)
    value_block = shaped[2].astype(jnp.bfloat16)
    attend = attention_step(queries, owners, grid, text_len, span, block_tokens, tile, text_rows)
    empty_state = (jnp.zeros(queries.shape, jnp.float32), jnp.zeros(queries.shape[:3], jnp.float32))
    padded_span = 128 * pl.cdiv(span, 128)
    both = jnp.stack([key_block[0], value_block[0]], axis=0).reshape(2, span, heads_here * head_dim)
    both = jnp.pad(both, ((0, 0), (0, padded_span - span), (0, 0)))[None]
    gathered = lax.all_gather(both, "row", axis=0, tiled=True)
    live = key_mask(
        gathered.shape[0] * padded_span, owners, grid, text_len, padded_span, block_tokens, tile, text_rows
    )
    attended = attention(
        queries[0].reshape(block_tokens, heads_here * head_dim),
        gathered,
        live,
        head_dim ** (-0.5),
    )
    partial_out = jnp.dot(attended, w_out, preferred_element_type=jnp.float32)
    projected = scatter_sum(partial_out, "col", 1)
    own_rows = lax.dynamic_slice_in_dim(source, col_id * tile, tile, 0)
    mixed = lax.optimization_barrier(
        (own_rows + adaptive[2] * projected).astype(jnp.bfloat16)
    ).astype(jnp.float32)
    second_norm = modulate(mixed, adaptive[3], adaptive[4])
    hidden_units = jax.nn.gelu(
        jnp.dot(
            ring_gather(second_norm, 4, 8, 2).reshape(-1, second_norm.shape[1]),
            w_up,
            preferred_element_type=jnp.float32,
        ),
        approximate=True,
    ).astype(jnp.bfloat16)
    feed_terms = jnp.dot(hidden_units, w_down, preferred_element_type=jnp.float32)
    feed_out = ring_scatter_sum(feed_terms.astype(jnp.bfloat16), 4, 8, 0)
    out_hidden = (mixed + adaptive[5] * feed_out).astype(jnp.bfloat16)
    final_norm = modulate(out_hidden.astype(jnp.float32), adaptive[6], adaptive[7])
    velocity = jnp.dot(final_norm, w_proj, preferred_element_type=jnp.float32)
    local_ids = jnp.arange(tile, dtype=jnp.int32)
    token_row = row_id * TR + local_ids // TC % TR
    token_col = col_id * TC + local_ids % TC
    rows_live = pick_entry(grid[:, 0], request_id)
    cols_live = pick_entry(grid[:, 1], request_id)
    live_tokens = ((token_row < rows_live) & (token_col < cols_live)).astype(jnp.float32)
    keep_part, velocity_part = solver_weights(pick_entry(timestep, request_id))
    updated = (keep_part * latent[0] + velocity_part * velocity) * live_tokens[:, None]
    pixels = (
        updated.reshape(FR, TR, TC, CH, 2, 2)
        .transpose(0, 1, 4, 2, 5, 3)
        .reshape(FR, 2 * TR, 2 * TC, CH)
    )
    scaled = (pixels / latent_scale).astype(jnp.bfloat16)
    padded = extended(scaled, (("row", 1), ("col", 2)), 1)
    running = jnp.zeros((FR, 2 * TR, 2 * TC, conv_w.shape[3]), jnp.float32)
    for row_tap in range(3):
        for col_tap in range(3):
            window = padded[:, row_tap : row_tap + 2 * TR, col_tap : col_tap + 2 * TC, :]
            running = running + jnp.einsum(
                "fyxc,cd->fyxd",
                window,
                conv_w[row_tap, col_tap],
                preferred_element_type=jnp.float32,
            )
    return (out_hidden[None], updated[None], running.astype(jnp.bfloat16)[None])


def solution(mesh):
    placed = (
        P("req", "row", None),
        P("req", "row", None),
        P(),
        P(),
        P(),
        P("req", None, None),
        P(),
        P(),
        P(None, "row", "col"),
        P("col", None),
        P(None, "row"),
        P("row", None),
        P(),
        P("req", ("row", "col"), None),
        P(),
    )
    return jax.shard_map(
        shards,
        mesh=mesh,
        in_specs=placed,
        out_specs=(
            P("req", ("row", "col"), None),
            P("req", ("row", "col"), None),
            P("req", None, "row", "col", None),
        ),
        check_vma=False,
    )
```

```python
import functools

import jax
import jax.numpy as jnp
from jax import lax
from jax.sharding import PartitionSpec as P
from jax.experimental import pallas as pl
from jax.experimental.pallas import tpu as pltpu

MESH_IDS = pl.DeviceIdType.MESH

CH = 16
FR = 6
TR = 1
TC = 4
TRAIN_STEPS = 1000
STRIDE = 250


latent_scale = 0.7


def extended(cells, sides, width):
    for axis, dim in sides:
        count = lax.axis_size(axis)
        ends = count - 1
        head = lax.slice_in_dim(cells, 0, width, axis=dim)
        tail = lax.slice_in_dim(cells, cells.shape[dim] - width, cells.shape[dim], axis=dim)
        cells = jnp.concatenate(
            [
                lax.ppermute(tail, axis, [(i, (i + 1) % count) for i in range(ends)]),
                cells,
                lax.ppermute(head, axis, [((i + 1) % count, i) for i in range(ends)]),
            ],
            axis=dim,
        )
    return cells


def peer_on(axis, peer):
    return tuple(peer if name == axis else lax.axis_index(name) for name in ("req", "row", "col"))


def scatter_sum_kernel(axis, count, rows, part_ref, out_ref, landed, send_sems, recv_sems, own_sem):
    me = lax.axis_index(axis)
    barrier = pltpu.get_barrier_semaphore()
    for step in range(1, count):
        peer = lax.rem(me + step, count)
        pl.semaphore_signal(barrier, inc=1, device_id=peer_on(axis, peer), device_id_type=MESH_IDS)
    pl.semaphore_wait(barrier, count - 1)
    own = pltpu.make_async_copy(part_ref.at[pl.ds(me * rows, rows)], landed.at[me], own_sem)
    own.start()
    sends = []
    for step in range(1, count):
        peer = lax.rem(me + step, count)
        copy = pltpu.make_async_remote_copy(
            src_ref=part_ref.at[pl.ds(peer * rows, rows)],
            dst_ref=landed.at[me],
            send_sem=send_sems.at[step],
            recv_sem=recv_sems.at[step],
            device_id=peer_on(axis, peer),
            device_id_type=MESH_IDS,
        )
        copy.start()
        sends.append(copy)
    own.wait()
    for step in range(1, count):
        source = lax.rem(me + count - step, count)
        pltpu.make_async_remote_copy(
            src_ref=part_ref.at[pl.ds(me * rows, rows)],
            dst_ref=landed.at[source],
            send_sem=send_sems.at[step],
            recv_sem=recv_sems.at[step],
            device_id=peer_on(axis, source),
            device_id_type=MESH_IDS,
        ).wait_recv()
    for copy in sends:
        copy.wait_send()
    total = landed[0].astype(jnp.float32)
    for slot in range(1, count):
        total = total + landed[slot].astype(jnp.float32)
    out_ref[...] = total


def scatter_sum(part, axis, kernel_id):
    count = lax.axis_size(axis)
    rows = part.shape[0] // count
    width = part.shape[1]
    return pl.pallas_call(
        functools.partial(scatter_sum_kernel, axis, count, rows),
        out_shape=jax.ShapeDtypeStruct((rows, width), jnp.float32),
        in_specs=[pl.BlockSpec(memory_space=pl.ANY)],
        out_specs=pl.BlockSpec(memory_space=pltpu.VMEM),
        scratch_shapes=[
            pltpu.VMEM((count, rows, width), part.dtype),
            pltpu.SemaphoreType.DMA((count,)),
            pltpu.SemaphoreType.DMA((count,)),
            pltpu.SemaphoreType.DMA(()),
        ],
        compiler_params=pltpu.CompilerParams(
            collective_id=kernel_id, has_side_effects=True, vmem_limit_bytes=48 * 1024 * 1024
        ),
    )(part)


def attention_kernel(scale, q_ref, kv_ref, live_ref, out_ref):
    sources, _, block, width = kv_ref.shape
    lane = lax.broadcasted_iota(jnp.int32, (1, 128), 1)
    first = lane < 64
    live = live_ref[...]
    for pair in range(width // 128):
        cols = slice(pair * 128, (pair + 1) * 128)
        query = q_ref[:, cols]
        keys = kv_ref[:, 0, :, cols].reshape(sources * block, 128)
        values = kv_ref[:, 1, :, cols].reshape(sources * block, 128)
        results = []
        for half in (first, jnp.logical_not(first)):
            picked = jnp.where(half, query, jnp.zeros_like(query))
            scores = lax.dot_general(
                picked, keys, (((1,), (1,)), ((), ())), preferred_element_type=jnp.float32
            ) * scale
            weights = jnp.exp(scores) * live
            totals = jnp.sum(weights, axis=1, keepdims=True)
            summed = jnp.dot(weights.astype(jnp.bfloat16), values, preferred_element_type=jnp.float32)
            results.append(summed / totals)
        out_ref[:, cols] = jnp.where(first, results[0], results[1]).astype(out_ref.dtype)


def attention(queries, gathered, live, scale):
    return pl.pallas_call(
        functools.partial(attention_kernel, scale),
        out_shape=jax.ShapeDtypeStruct(queries.shape, jnp.bfloat16),
        in_specs=[pl.BlockSpec(memory_space=pltpu.VMEM)] * 3,
        out_specs=pl.BlockSpec(memory_space=pltpu.VMEM),
        compiler_params=pltpu.CompilerParams(vmem_limit_bytes=56 * 1024 * 1024),
    )(queries, gathered, live)


def ring_scatter_kernel(zs, xs, part_ref, out_ref, landed, outgoing, own_sum, crossed, ring_send, ring_recv, cross_send, cross_recv):
    me = lax.axis_index("row")
    xm = me // zs
    zm = me % zs
    ahead = xm * zs + lax.rem(zm + 1, zs)
    behind = xm * zs + lax.rem(zm + zs - 1, zs)
    half = part_ref.shape[3] // 2
    barrier = pltpu.get_barrier_semaphore()
    targets = [ahead, behind] + [lax.rem(xm + k, xs) * zs + zm for k in range(1, xs)]
    for peer in targets:
        pl.semaphore_signal(barrier, inc=1, device_id=peer_on("row", peer), device_id_type=MESH_IDS)
    pl.semaphore_wait(barrier, len(targets))
    ways = ((0, ahead, behind, -1), (1, behind, ahead, 1))
    pending = []
    for step in range(zs - 1):
        for way, dest, origin, sign in ways:
            cols = pl.ds(way * half, half)
            chunk = lax.rem(zm + sign * (1 + step) + 2 * zs, zs)
            if step == 0:
                source = part_ref.at[chunk, :, :, cols]
            else:
                arrived = pltpu.make_async_remote_copy(
                    src_ref=outgoing.at[way, step - 1],
                    dst_ref=landed.at[way, step - 1],
                    send_sem=ring_send.at[way, step - 1],
                    recv_sem=ring_recv.at[way, step - 1],
                    device_id=peer_on("row", origin),
                    device_id_type=MESH_IDS,
                )
                arrived.wait_recv()
                outgoing[way, step] = (
                    landed[way, step - 1].astype(jnp.float32)
                    + part_ref[chunk, :, :, cols].astype(jnp.float32)
                ).astype(outgoing.dtype)
                source = outgoing.at[way, step]
            copy = pltpu.make_async_remote_copy(
                src_ref=source,
                dst_ref=landed.at[way, step],
                send_sem=ring_send.at[way, step],
                recv_sem=ring_recv.at[way, step],
                device_id=peer_on("row", dest),
                device_id_type=MESH_IDS,
            )
            copy.start()
            pending.append(copy)
    last = zs - 2
    for way, dest, origin, sign in ways:
        cols = pl.ds(way * half, half)
        pltpu.make_async_remote_copy(
            src_ref=outgoing.at[way, last],
            dst_ref=landed.at[way, last],
            send_sem=ring_send.at[way, last],
            recv_sem=ring_recv.at[way, last],
            device_id=peer_on("row", origin),
            device_id_type=MESH_IDS,
        ).wait_recv()
        own_sum[:, :, cols] = landed[way, last].astype(jnp.float32) + part_ref[zm, :, :, cols].astype(jnp.float32)
    crossed[0] = own_sum[...].astype(crossed.dtype)
    sends = []
    for k in range(1, xs):
        peer_x = lax.rem(xm + k, xs)
        copy = pltpu.make_async_remote_copy(
            src_ref=crossed.at[0, peer_x],
            dst_ref=crossed.at[k, 0],
            send_sem=cross_send.at[k],
            recv_sem=cross_recv.at[k],
            device_id=peer_on("row", peer_x * zs + zm),
            device_id_type=MESH_IDS,
        )
        copy.start()
        sends.append(copy)
    total = own_sum[xm]
    for k in range(1, xs):
        origin_x = lax.rem(xm + xs - k, xs)
        pltpu.make_async_remote_copy(
            src_ref=crossed.at[0, 0],
            dst_ref=crossed.at[k, 0],
            send_sem=cross_send.at[k],
            recv_sem=cross_recv.at[k],
            device_id=peer_on("row", origin_x * zs + zm),
            device_id_type=MESH_IDS,
        ).wait_recv()
        total = total + crossed[k, 0].astype(jnp.float32)
    out_ref[...] = total
    for copy in pending + sends:
        copy.wait_send()


def ring_scatter_sum(part, xs, zs, kernel_id):
    rows = part.shape[0] // (xs * zs)
    width = part.shape[1]
    arranged = part.reshape(zs, xs, rows, width)
    return pl.pallas_call(
        functools.partial(ring_scatter_kernel, zs, xs),
        out_shape=jax.ShapeDtypeStruct((rows, width), jnp.float32),
        in_specs=[pl.BlockSpec(memory_space=pltpu.VMEM)],
        out_specs=pl.BlockSpec(memory_space=pltpu.VMEM),
        scratch_shapes=[
            pltpu.VMEM((2, zs - 1, xs, rows, width // 2), part.dtype),
            pltpu.VMEM((2, zs - 1, xs, rows, width // 2), part.dtype),
            pltpu.VMEM((xs, rows, width), jnp.float32),
            pltpu.VMEM((xs, xs, rows, width), part.dtype),
            pltpu.SemaphoreType.DMA((2, zs - 1)),
            pltpu.SemaphoreType.DMA((2, zs - 1)),
            pltpu.SemaphoreType.DMA((xs,)),
            pltpu.SemaphoreType.DMA((xs,)),
        ],
        compiler_params=pltpu.CompilerParams(
            collective_id=kernel_id, has_side_effects=True, vmem_limit_bytes=56 * 1024 * 1024
        ),
    )(arranged)


def ring_gather_kernel(zs, xs, block_ref, out_ref, held, own_sem, ring_send, ring_recv, cross_send, cross_recv):
    me = lax.axis_index("row")
    xm = me // zs
    zm = me % zs
    ahead = xm * zs + lax.rem(zm + 1, zs)
    behind = xm * zs + lax.rem(zm + zs - 1, zs)
    barrier = pltpu.get_barrier_semaphore()
    targets = [ahead, behind] + [lax.rem(xm + k, xs) * zs + zm for k in range(1, xs)]
    for peer in targets:
        pl.semaphore_signal(barrier, inc=1, device_id=peer_on("row", peer), device_id_type=MESH_IDS)
    pl.semaphore_wait(barrier, len(targets))
    own = pltpu.make_async_copy(block_ref, held.at[zm, xm], own_sem)
    own.start()
    pending = []
    for k in range(1, xs):
        peer_x = lax.rem(xm + k, xs)
        copy = pltpu.make_async_remote_copy(
            src_ref=block_ref,
            dst_ref=held.at[zm, xm],
            send_sem=cross_send.at[k],
            recv_sem=cross_recv.at[k],
            device_id=peer_on("row", peer_x * zs + zm),
            device_id_type=MESH_IDS,
        )
        copy.start()
        pending.append(copy)
    own.wait()
    for k in range(1, xs):
        origin_x = lax.rem(xm + xs - k, xs)
        pltpu.make_async_remote_copy(
            src_ref=block_ref,
            dst_ref=held.at[zm, origin_x],
            send_sem=cross_send.at[k],
            recv_sem=cross_recv.at[k],
            device_id=peer_on("row", origin_x * zs + zm),
            device_id_type=MESH_IDS,
        ).wait_recv()
    split = xs // 2
    ways = ((0, ahead, behind, -1, pl.ds(0, split)), (1, behind, ahead, 1, pl.ds(split, xs - split)))
    for step in range(zs):
        for way, dest, origin, sign, part in ways:
            group = lax.rem(zm + sign * step + zs, zs)
            if step > 0:
                pltpu.make_async_remote_copy(
                    src_ref=held.at[group, part],
                    dst_ref=held.at[group, part],
                    send_sem=ring_send.at[way, step - 1],
                    recv_sem=ring_recv.at[way, step - 1],
                    device_id=peer_on("row", origin),
                    device_id_type=MESH_IDS,
                ).wait_recv()
            if step < zs - 1:
                copy = pltpu.make_async_remote_copy(
                    src_ref=held.at[group, part],
                    dst_ref=held.at[group, part],
                    send_sem=ring_send.at[way, step],
                    recv_sem=ring_recv.at[way, step],
                    device_id=peer_on("row", dest),
                    device_id_type=MESH_IDS,
                )
                copy.start()
                pending.append(copy)
    for copy in pending:
        copy.wait_send()
    out = pltpu.make_async_copy(held, out_ref, own_sem)
    out.start()
    out.wait()


def ring_gather(block, xs, zs, kernel_id):
    return pl.pallas_call(
        functools.partial(ring_gather_kernel, zs, xs),
        out_shape=jax.ShapeDtypeStruct((zs, xs) + block.shape, block.dtype),
        in_specs=[pl.BlockSpec(memory_space=pltpu.VMEM)],
        out_specs=pl.BlockSpec(memory_space=pl.ANY),
        scratch_shapes=[
            pltpu.VMEM((zs, xs) + block.shape, block.dtype),
            pltpu.SemaphoreType.DMA(()),
            pltpu.SemaphoreType.DMA((2, zs - 1)),
            pltpu.SemaphoreType.DMA((2, zs - 1)),
            pltpu.SemaphoreType.DMA((xs,)),
            pltpu.SemaphoreType.DMA((xs,)),
        ],
        compiler_params=pltpu.CompilerParams(
            collective_id=kernel_id, has_side_effects=True, vmem_limit_bytes=56 * 1024 * 1024
        ),
    )(block)


def device_at(**coords):
    return tuple(coords.get(name, lax.axis_index(name)) for name in ("req", "row", "col"))


def paired_gather_kernel(zs, xs, block_ref, out_ref, held, own_sem, ring_send, ring_recv, cross_send, cross_recv, pair_send, pair_recv):
    me = lax.axis_index("row")
    mine = lax.axis_index("req")
    other = 1 - mine
    xm = me // zs
    zm = me % zs
    ahead = xm * zs + lax.rem(zm + 1, zs)
    behind = xm * zs + lax.rem(zm + zs - 1, zs)
    barrier = pltpu.get_barrier_semaphore()
    targets = [device_at(row=ahead), device_at(row=behind)]
    targets += [device_at(row=lax.rem(xm + k, xs) * zs + zm) for k in range(1, xs)]
    targets.append(device_at(req=other))
    for peer in targets:
        pl.semaphore_signal(barrier, inc=1, device_id=peer, device_id_type=MESH_IDS)
    pl.semaphore_wait(barrier, len(targets))
    own = pltpu.make_async_copy(block_ref, held.at[mine, zm, xm], own_sem)
    own.start()
    pending = []
    for k in range(1, xs):
        peer_x = lax.rem(xm + k, xs)
        copy = pltpu.make_async_remote_copy(
            src_ref=block_ref,
            dst_ref=held.at[mine, zm, xm],
            send_sem=cross_send.at[k],
            recv_sem=cross_recv.at[k],
            device_id=device_at(row=peer_x * zs + zm),
            device_id_type=MESH_IDS,
        )
        copy.start()
        pending.append(copy)
    own.wait()
    for k in range(1, xs):
        origin_x = lax.rem(xm + xs - k, xs)
        pltpu.make_async_remote_copy(
            src_ref=block_ref,
            dst_ref=held.at[mine, zm, origin_x],
            send_sem=cross_send.at[k],
            recv_sem=cross_recv.at[k],
            device_id=device_at(row=origin_x * zs + zm),
            device_id_type=MESH_IDS,
        ).wait_recv()
    split = xs // 2
    ways = ((0, ahead, behind, -1, pl.ds(0, split)), (1, behind, ahead, 1, pl.ds(split, xs - split)))
    for step in range(zs):
        for way, dest, origin, sign, part in ways:
            group = lax.rem(zm + sign * step + zs, zs)
            if step > 0:
                pltpu.make_async_remote_copy(
                    src_ref=held.at[mine, group, part],
                    dst_ref=held.at[mine, group, part],
                    send_sem=ring_send.at[way, step - 1],
                    recv_sem=ring_recv.at[way, step - 1],
                    device_id=device_at(row=origin),
                    device_id_type=MESH_IDS,
                ).wait_recv()
            if step < zs - 1:
                copy = pltpu.make_async_remote_copy(
                    src_ref=held.at[mine, group, part],
                    dst_ref=held.at[mine, group, part],
                    send_sem=ring_send.at[way, step],
                    recv_sem=ring_recv.at[way, step],
                    device_id=device_at(row=dest),
                    device_id_type=MESH_IDS,
                )
                copy.start()
                pending.append(copy)
            copy = pltpu.make_async_remote_copy(
                src_ref=held.at[mine, group, part],
                dst_ref=held.at[mine, group, part],
                send_sem=pair_send.at[way, step],
                recv_sem=pair_recv.at[way, step],
                device_id=device_at(req=other),
                device_id_type=MESH_IDS,
            )
            copy.start()
            pending.append(copy)
    for step in range(zs):
        for way, dest, origin, sign, part in ways:
            group = lax.rem(zm + sign * step + zs, zs)
            pltpu.make_async_remote_copy(
                src_ref=held.at[other, group, part],
                dst_ref=held.at[other, group, part],
                send_sem=pair_send.at[way, step],
                recv_sem=pair_recv.at[way, step],
                device_id=device_at(req=other),
                device_id_type=MESH_IDS,
            ).wait_recv()
    for copy in pending:
        copy.wait_send()
    out = pltpu.make_async_copy(held, out_ref, own_sem)
    out.start()
    out.wait()


def paired_gather(block, xs, zs, kernel_id):
    return pl.pallas_call(
        functools.partial(paired_gather_kernel, zs, xs),
        out_shape=jax.ShapeDtypeStruct((2, zs, xs) + block.shape, block.dtype),
        in_specs=[pl.BlockSpec(memory_space=pltpu.VMEM)],
        out_specs=pl.BlockSpec(memory_space=pl.ANY),
        scratch_shapes=[
            pltpu.VMEM((2, zs, xs) + block.shape, block.dtype),
            pltpu.SemaphoreType.DMA(()),
            pltpu.SemaphoreType.DMA((2, zs - 1)),
            pltpu.SemaphoreType.DMA((2, zs - 1)),
            pltpu.SemaphoreType.DMA((xs,)),
            pltpu.SemaphoreType.DMA((xs,)),
            pltpu.SemaphoreType.DMA((2, zs)),
            pltpu.SemaphoreType.DMA((2, zs)),
        ],
        compiler_params=pltpu.CompilerParams(
            collective_id=kernel_id, has_side_effects=True, vmem_limit_bytes=56 * 1024 * 1024
        ),
    )(block)


def layer_norm(tensor, epsilon):
    average = jnp.mean(tensor, axis=-1, keepdims=True)
    centered = tensor - average
    spread = jnp.mean(centered * centered, axis=-1, keepdims=True)
    return centered * lax.rsqrt(spread + epsilon)


def modulate(tensor, offset, factor):
    return (layer_norm(tensor, 1e-05) * (1.0 + factor) + offset).astype(jnp.bfloat16)


def head_norm(tensor, scaling):
    return (layer_norm(tensor, 1e-06) * scaling).astype(jnp.bfloat16)


def pick_entry(entries, position):
    slot_ids = jnp.arange(entries.shape[0], dtype=jnp.int32)
    return jnp.sum(jnp.where(slot_ids == position, entries, jnp.zeros_like(entries)))


def solver_weights(step_index):
    plan = jnp.linspace(0.00085**0.5, 0.012**0.5, TRAIN_STEPS, dtype=jnp.float32) ** 2
    cumulative = jnp.cumprod(1.0 - plan)
    alpha_now = pick_entry(cumulative, step_index)
    alpha_prev = pick_entry(cumulative, step_index - STRIDE)
    root_now = jnp.sqrt(alpha_now)
    rest_now = jnp.sqrt(1.0 - alpha_now)
    root_prev = jnp.sqrt(alpha_prev)
    rest_prev = jnp.sqrt(1.0 - alpha_prev)
    return (
        root_prev * root_now + rest_prev * rest_now,
        rest_prev * root_now - root_prev * rest_now,
    )


def key_mask(count, owners, grid, text_len, span, block_tokens, tile, text_rows):
    positions = jnp.arange(count, dtype=jnp.int32)
    owner_row = positions // span
    within = positions % span
    is_video = within < block_tokens
    owner_col = within // tile
    local_ids = within % tile
    token_row = owner_row * TR + local_ids // TC % TR
    token_col = owner_col * TC + local_ids % TC
    text_index = owner_row * text_rows + within - block_tokens
    matches = jnp.arange(grid.shape[0], dtype=jnp.int32)[None, :] == owners[:, None]
    rows_live = jnp.sum(jnp.where(matches, grid[None, :, 0], 0), axis=1)
    cols_live = jnp.sum(jnp.where(matches, grid[None, :, 1], 0), axis=1)
    text_lens = jnp.sum(jnp.where(matches, text_len[None, :], 0), axis=1)
    video_live = (token_row[None, :] < rows_live[:, None]) & (
        token_col[None, :] < cols_live[:, None]
    )
    text_live = (text_index[None, :] < text_lens[:, None]) & (within < block_tokens + text_rows)[None, :]
    return jnp.where(is_video[None, :], video_live, text_live).astype(jnp.float32)


def projector(stacked, piece):
    return jnp.einsum("gld,cde->cgle", stacked, piece, preferred_element_type=jnp.float32)


def attention_step(queries, owners, grid, text_len, span, block_tokens, tile, text_rows):
    score_scale = queries.shape[3] ** (-0.5)

    def attend(carry, pieces, start):
        key_piece, value_piece = pieces
        live_keys = key_mask(
            key_piece.shape[1], owners, grid, text_len, span, block_tokens, tile, text_rows
        )
        scores = (
            jnp.einsum("gqhd,gkhd->gqhk", queries, key_piece, preferred_element_type=jnp.float32)
            * score_scale
        )
        raw_weights = jnp.exp(scores) * live_keys[:, None, None, :]
        weighted = jnp.einsum(
            "gqhk,gkhd->gqhd",
            raw_weights.astype(jnp.bfloat16),
            value_piece,
            preferred_element_type=jnp.float32,
        )
        return (weighted, jnp.sum(raw_weights, axis=3))

    return attend


def shards(
    hidden,
    text_hidden,
    text_len,
    grid,
    timestep,
    modulation,
    q_gain,
    k_gain,
    w_qkv,
    w_out,
    w_up,
    w_down,
    w_proj,
    latent,
    conv_w,
):
    col_count = lax.axis_size("col")
    request_id = lax.axis_index("req")
    row_id = lax.axis_index("row")
    col_id = lax.axis_index("col")
    block_tokens = hidden.shape[1]
    tile = block_tokens // col_count
    text_rows = text_hidden.shape[1]
    head_dim = q_gain.shape[0]
    adaptive = modulation[0]
    source = hidden[0].astype(jnp.float32)
    joined = jnp.concatenate(
        [
            modulate(source, adaptive[0], adaptive[1]),
            modulate(text_hidden[0].astype(jnp.float32), adaptive[0], adaptive[1]),
        ],
        axis=0,
    )
    span = joined.shape[0]
    stacked = joined[None]
    owners = jnp.reshape(request_id, (1,))
    half_cols = w_qkv.shape[2] // 2
    own_half = lax.dynamic_slice_in_dim(w_qkv, request_id * half_cols, half_cols, 2)
    both_halves = paired_gather(own_half.transpose(1, 0, 2), 4, 8, 3)
    depth = w_qkv.shape[1]
    reordered = joined.reshape(span, 4, 8, depth).transpose(0, 2, 1, 3).reshape(span, -1)
    qkv = jnp.concatenate(
        [
            jnp.einsum(
                "lk,kce->cle",
                reordered,
                both_halves[h].reshape(-1, 3, half_cols),
                preferred_element_type=jnp.float32,
            )
            for h in range(2)
        ],
        axis=2,
    )[:, None]
    groups = stacked.shape[0]
    heads_here = qkv.shape[3] // head_dim
    shaped = qkv.reshape(3, groups, span, heads_here, head_dim)
    queries = head_norm(shaped[0, :, :block_tokens], q_gain)
    key_block = head_norm(shaped[1], k_gain)
    value_block = shaped[2].astype(jnp.bfloat16)
    attend = attention_step(queries, owners, grid, text_len, span, block_tokens, tile, text_rows)
    empty_state = (jnp.zeros(queries.shape, jnp.float32), jnp.zeros(queries.shape[:3], jnp.float32))
    padded_span = 128 * pl.cdiv(span, 128)
    both = jnp.stack([key_block[0], value_block[0]], axis=0).reshape(2, span, heads_here * head_dim)
    both = jnp.pad(both, ((0, 0), (0, padded_span - span), (0, 0)))[None]
    gathered = lax.all_gather(both, "row", axis=0, tiled=True)
    live = key_mask(
        gathered.shape[0] * padded_span, owners, grid, text_len, padded_span, block_tokens, tile, text_rows
    )
    attended = attention(
        queries[0].reshape(block_tokens, heads_here * head_dim),
        gathered,
        live,
        head_dim ** (-0.5),
    )
    partial_out = jnp.dot(attended, w_out, preferred_element_type=jnp.float32)
    projected = scatter_sum(partial_out, "col", 1)
    own_rows = lax.dynamic_slice_in_dim(source, col_id * tile, tile, 0)
    mixed = lax.optimization_barrier(
        (own_rows + adaptive[2] * projected).astype(jnp.bfloat16)
    ).astype(jnp.float32)
    second_norm = modulate(mixed, adaptive[3], adaptive[4])
    hidden_units = jax.nn.gelu(
        jnp.dot(
            ring_gather(second_norm, 4, 8, 2).reshape(-1, second_norm.shape[1]),
            w_up,
            preferred_element_type=jnp.float32,
        ),
        approximate=True,
    ).astype(jnp.bfloat16)
    feed_terms = jnp.dot(hidden_units, w_down, preferred_element_type=jnp.float32)
    feed_out = ring_scatter_sum(feed_terms.astype(jnp.bfloat16), 4, 8, 0)
    out_hidden = (mixed + adaptive[5] * feed_out).astype(jnp.bfloat16)
    final_norm = modulate(out_hidden.astype(jnp.float32), adaptive[6], adaptive[7])
    velocity = jnp.dot(final_norm, w_proj, preferred_element_type=jnp.float32)
    local_ids = jnp.arange(tile, dtype=jnp.int32)
    token_row = row_id * TR + local_ids // TC % TR
    token_col = col_id * TC + local_ids % TC
    rows_live = pick_entry(grid[:, 0], request_id)
    cols_live = pick_entry(grid[:, 1], request_id)
    live_tokens = ((token_row < rows_live) & (token_col < cols_live)).astype(jnp.float32)
    keep_part, velocity_part = solver_weights(pick_entry(timestep, request_id))
    updated = (keep_part * latent[0] + velocity_part * velocity) * live_tokens[:, None]
    pixels = (
        updated.reshape(FR, TR, TC, CH, 2, 2)
        .transpose(0, 1, 4, 2, 5, 3)
        .reshape(FR, 2 * TR, 2 * TC, CH)
    )
    scaled = (pixels / latent_scale).astype(jnp.bfloat16)
    padded = extended(scaled, (("row", 1), ("col", 2)), 1)
    running = jnp.zeros((FR, 2 * TR, 2 * TC, conv_w.shape[3]), jnp.float32)
    for row_tap in range(3):
        for col_tap in range(3):
            window = padded[:, row_tap : row_tap + 2 * TR, col_tap : col_tap + 2 * TC, :]
            running = running + jnp.einsum(
                "fyxc,cd->fyxd",
                window,
                conv_w[row_tap, col_tap],
                preferred_element_type=jnp.float32,
            )
    return (out_hidden[None], updated[None], running.astype(jnp.bfloat16)[None])


def solution(mesh):
    placed = (
        P("req", "row", None),
        P("req", "row", None),
        P(),
        P(),
        P(),
        P("req", None, None),
        P(),
        P(),
        P(None, "row", "col"),
        P("col", None),
        P(None, "row"),
        P("row", None),
        P(),
        P("req", ("row", "col"), None),
        P(),
    )
    return jax.shard_map(
        shards,
        mesh=mesh,
        in_specs=placed,
        out_specs=(
            P("req", ("row", "col"), None),
            P("req", ("row", "col"), None),
            P("req", None, "row", "col", None),
        ),
        check_vma=False,
    )
```

```python
import functools

import jax
import jax.numpy as jnp
from jax import lax
from jax.sharding import PartitionSpec as P
from jax.experimental import pallas as pl
from jax.experimental.pallas import tpu as pltpu

MESH_IDS = pl.DeviceIdType.MESH

CH = 16
FR = 6
TR = 1
TC = 4
TRAIN_STEPS = 1000
STRIDE = 250


latent_scale = 0.7


def extended(cells, sides, width):
    for axis, dim in sides:
        count = lax.axis_size(axis)
        ends = count - 1
        head = lax.slice_in_dim(cells, 0, width, axis=dim)
        tail = lax.slice_in_dim(cells, cells.shape[dim] - width, cells.shape[dim], axis=dim)
        cells = jnp.concatenate(
            [
                lax.ppermute(tail, axis, [(i, (i + 1) % count) for i in range(ends)]),
                cells,
                lax.ppermute(head, axis, [((i + 1) % count, i) for i in range(ends)]),
            ],
            axis=dim,
        )
    return cells


def peer_on(axis, peer):
    return tuple(peer if name == axis else lax.axis_index(name) for name in ("req", "row", "col"))


def scatter_sum_kernel(axis, count, rows, part_ref, out_ref, landed, send_sems, recv_sems, own_sem):
    me = lax.axis_index(axis)
    barrier = pltpu.get_barrier_semaphore()
    for step in range(1, count):
        peer = lax.rem(me + step, count)
        pl.semaphore_signal(barrier, inc=1, device_id=peer_on(axis, peer), device_id_type=MESH_IDS)
    pl.semaphore_wait(barrier, count - 1)
    own = pltpu.make_async_copy(part_ref.at[pl.ds(me * rows, rows)], landed.at[me], own_sem)
    own.start()
    sends = []
    for step in range(1, count):
        peer = lax.rem(me + step, count)
        copy = pltpu.make_async_remote_copy(
            src_ref=part_ref.at[pl.ds(peer * rows, rows)],
            dst_ref=landed.at[me],
            send_sem=send_sems.at[step],
            recv_sem=recv_sems.at[step],
            device_id=peer_on(axis, peer),
            device_id_type=MESH_IDS,
        )
        copy.start()
        sends.append(copy)
    own.wait()
    for step in range(1, count):
        source = lax.rem(me + count - step, count)
        pltpu.make_async_remote_copy(
            src_ref=part_ref.at[pl.ds(me * rows, rows)],
            dst_ref=landed.at[source],
            send_sem=send_sems.at[step],
            recv_sem=recv_sems.at[step],
            device_id=peer_on(axis, source),
            device_id_type=MESH_IDS,
        ).wait_recv()
    for copy in sends:
        copy.wait_send()
    total = landed[0].astype(jnp.float32)
    for slot in range(1, count):
        total = total + landed[slot].astype(jnp.float32)
    out_ref[...] = total


def scatter_sum(part, axis, kernel_id):
    count = lax.axis_size(axis)
    rows = part.shape[0] // count
    width = part.shape[1]
    return pl.pallas_call(
        functools.partial(scatter_sum_kernel, axis, count, rows),
        out_shape=jax.ShapeDtypeStruct((rows, width), jnp.float32),
        in_specs=[pl.BlockSpec(memory_space=pl.ANY)],
        out_specs=pl.BlockSpec(memory_space=pltpu.VMEM),
        scratch_shapes=[
            pltpu.VMEM((count, rows, width), part.dtype),
            pltpu.SemaphoreType.DMA((count,)),
            pltpu.SemaphoreType.DMA((count,)),
            pltpu.SemaphoreType.DMA(()),
        ],
        compiler_params=pltpu.CompilerParams(
            collective_id=kernel_id, has_side_effects=True, vmem_limit_bytes=48 * 1024 * 1024
        ),
    )(part)


def attention_kernel(scale, q_ref, kv_ref, live_ref, out_ref):
    sources, _, block, width = kv_ref.shape
    lane = lax.broadcasted_iota(jnp.int32, (1, 128), 1)
    first = lane < 64
    live = live_ref[...]
    for pair in range(width // 128):
        cols = slice(pair * 128, (pair + 1) * 128)
        query = q_ref[:, cols]
        keys = kv_ref[:, 0, :, cols].reshape(sources * block, 128)
        values = kv_ref[:, 1, :, cols].reshape(sources * block, 128)
        results = []
        for half in (first, jnp.logical_not(first)):
            picked = jnp.where(half, query, jnp.zeros_like(query))
            scores = lax.dot_general(
                picked, keys, (((1,), (1,)), ((), ())), preferred_element_type=jnp.float32
            ) * scale
            weights = jnp.exp(scores) * live
            totals = jnp.sum(weights, axis=1, keepdims=True)
            summed = jnp.dot(weights.astype(jnp.bfloat16), values, preferred_element_type=jnp.float32)
            results.append(summed / totals)
        out_ref[:, cols] = jnp.where(first, results[0], results[1]).astype(out_ref.dtype)


def attention(queries, gathered, live, scale):
    return pl.pallas_call(
        functools.partial(attention_kernel, scale),
        out_shape=jax.ShapeDtypeStruct(queries.shape, jnp.bfloat16),
        in_specs=[pl.BlockSpec(memory_space=pltpu.VMEM)] * 3,
        out_specs=pl.BlockSpec(memory_space=pltpu.VMEM),
        compiler_params=pltpu.CompilerParams(vmem_limit_bytes=56 * 1024 * 1024),
    )(queries, gathered, live)


def ring_scatter_kernel(zs, xs, part_ref, out_ref, landed, outgoing, own_sum, crossed, ring_send, ring_recv, cross_send, cross_recv):
    me = lax.axis_index("row")
    xm = me // zs
    zm = me % zs
    ahead = xm * zs + lax.rem(zm + 1, zs)
    behind = xm * zs + lax.rem(zm + zs - 1, zs)
    half = part_ref.shape[3] // 2
    barrier = pltpu.get_barrier_semaphore()
    targets = [ahead, behind] + [lax.rem(xm + k, xs) * zs + zm for k in range(1, xs)]
    for peer in targets:
        pl.semaphore_signal(barrier, inc=1, device_id=peer_on("row", peer), device_id_type=MESH_IDS)
    pl.semaphore_wait(barrier, len(targets))
    ways = ((0, ahead, behind, -1), (1, behind, ahead, 1))
    pending = []
    for step in range(zs - 1):
        for way, dest, origin, sign in ways:
            cols = pl.ds(way * half, half)
            chunk = lax.rem(zm + sign * (1 + step) + 2 * zs, zs)
            if step == 0:
                source = part_ref.at[chunk, :, :, cols]
            else:
                arrived = pltpu.make_async_remote_copy(
                    src_ref=outgoing.at[way, step - 1],
                    dst_ref=landed.at[way, step - 1],
                    send_sem=ring_send.at[way, step - 1],
                    recv_sem=ring_recv.at[way, step - 1],
                    device_id=peer_on("row", origin),
                    device_id_type=MESH_IDS,
                )
                arrived.wait_recv()
                outgoing[way, step] = (
                    landed[way, step - 1].astype(jnp.float32)
                    + part_ref[chunk, :, :, cols].astype(jnp.float32)
                ).astype(outgoing.dtype)
                source = outgoing.at[way, step]
            copy = pltpu.make_async_remote_copy(
                src_ref=source,
                dst_ref=landed.at[way, step],
                send_sem=ring_send.at[way, step],
                recv_sem=ring_recv.at[way, step],
                device_id=peer_on("row", dest),
                device_id_type=MESH_IDS,
            )
            copy.start()
            pending.append(copy)
    last = zs - 2
    for way, dest, origin, sign in ways:
        cols = pl.ds(way * half, half)
        pltpu.make_async_remote_copy(
            src_ref=outgoing.at[way, last],
            dst_ref=landed.at[way, last],
            send_sem=ring_send.at[way, last],
            recv_sem=ring_recv.at[way, last],
            device_id=peer_on("row", origin),
            device_id_type=MESH_IDS,
        ).wait_recv()
        own_sum[:, :, cols] = landed[way, last].astype(jnp.float32) + part_ref[zm, :, :, cols].astype(jnp.float32)
    crossed[0] = own_sum[...].astype(crossed.dtype)
    sends = []
    for k in range(1, xs):
        peer_x = lax.rem(xm + k, xs)
        copy = pltpu.make_async_remote_copy(
            src_ref=crossed.at[0, peer_x],
            dst_ref=crossed.at[k, 0],
            send_sem=cross_send.at[k],
            recv_sem=cross_recv.at[k],
            device_id=peer_on("row", peer_x * zs + zm),
            device_id_type=MESH_IDS,
        )
        copy.start()
        sends.append(copy)
    total = own_sum[xm]
    for k in range(1, xs):
        origin_x = lax.rem(xm + xs - k, xs)
        pltpu.make_async_remote_copy(
            src_ref=crossed.at[0, 0],
            dst_ref=crossed.at[k, 0],
            send_sem=cross_send.at[k],
            recv_sem=cross_recv.at[k],
            device_id=peer_on("row", origin_x * zs + zm),
            device_id_type=MESH_IDS,
        ).wait_recv()
        total = total + crossed[k, 0].astype(jnp.float32)
    out_ref[...] = total
    for copy in pending + sends:
        copy.wait_send()


def ring_scatter_sum(part, xs, zs, kernel_id):
    rows = part.shape[0] // (xs * zs)
    width = part.shape[1]
    arranged = part.reshape(zs, xs, rows, width)
    return pl.pallas_call(
        functools.partial(ring_scatter_kernel, zs, xs),
        out_shape=jax.ShapeDtypeStruct((rows, width), jnp.float32),
        in_specs=[pl.BlockSpec(memory_space=pltpu.VMEM)],
        out_specs=pl.BlockSpec(memory_space=pltpu.VMEM),
        scratch_shapes=[
            pltpu.VMEM((2, zs - 1, xs, rows, width // 2), part.dtype),
            pltpu.VMEM((2, zs - 1, xs, rows, width // 2), part.dtype),
            pltpu.VMEM((xs, rows, width), jnp.float32),
            pltpu.VMEM((xs, xs, rows, width), part.dtype),
            pltpu.SemaphoreType.DMA((2, zs - 1)),
            pltpu.SemaphoreType.DMA((2, zs - 1)),
            pltpu.SemaphoreType.DMA((xs,)),
            pltpu.SemaphoreType.DMA((xs,)),
        ],
        compiler_params=pltpu.CompilerParams(
            collective_id=kernel_id, has_side_effects=True, vmem_limit_bytes=56 * 1024 * 1024
        ),
    )(arranged)


def ring_gather_kernel(zs, xs, block_ref, out_ref, held, own_sem, ring_send, ring_recv, cross_send, cross_recv):
    me = lax.axis_index("row")
    xm = me // zs
    zm = me % zs
    ahead = xm * zs + lax.rem(zm + 1, zs)
    behind = xm * zs + lax.rem(zm + zs - 1, zs)
    barrier = pltpu.get_barrier_semaphore()
    targets = [ahead, behind] + [lax.rem(xm + k, xs) * zs + zm for k in range(1, xs)]
    for peer in targets:
        pl.semaphore_signal(barrier, inc=1, device_id=peer_on("row", peer), device_id_type=MESH_IDS)
    pl.semaphore_wait(barrier, len(targets))
    own = pltpu.make_async_copy(block_ref, held.at[zm, xm], own_sem)
    own.start()
    pending = []
    for k in range(1, xs):
        peer_x = lax.rem(xm + k, xs)
        copy = pltpu.make_async_remote_copy(
            src_ref=block_ref,
            dst_ref=held.at[zm, xm],
            send_sem=cross_send.at[k],
            recv_sem=cross_recv.at[k],
            device_id=peer_on("row", peer_x * zs + zm),
            device_id_type=MESH_IDS,
        )
        copy.start()
        pending.append(copy)
    own.wait()
    for k in range(1, xs):
        origin_x = lax.rem(xm + xs - k, xs)
        pltpu.make_async_remote_copy(
            src_ref=block_ref,
            dst_ref=held.at[zm, origin_x],
            send_sem=cross_send.at[k],
            recv_sem=cross_recv.at[k],
            device_id=peer_on("row", origin_x * zs + zm),
            device_id_type=MESH_IDS,
        ).wait_recv()
    split = xs // 2
    ways = ((0, ahead, behind, -1, pl.ds(0, split)), (1, behind, ahead, 1, pl.ds(split, xs - split)))
    for step in range(zs):
        for way, dest, origin, sign, part in ways:
            group = lax.rem(zm + sign * step + zs, zs)
            if step > 0:
                pltpu.make_async_remote_copy(
                    src_ref=held.at[group, part],
                    dst_ref=held.at[group, part],
                    send_sem=ring_send.at[way, step - 1],
                    recv_sem=ring_recv.at[way, step - 1],
                    device_id=peer_on("row", origin),
                    device_id_type=MESH_IDS,
                ).wait_recv()
            if step < zs - 1:
                copy = pltpu.make_async_remote_copy(
                    src_ref=held.at[group, part],
                    dst_ref=held.at[group, part],
                    send_sem=ring_send.at[way, step],
                    recv_sem=ring_recv.at[way, step],
                    device_id=peer_on("row", dest),
                    device_id_type=MESH_IDS,
                )
                copy.start()
                pending.append(copy)
    for copy in pending:
        copy.wait_send()
    out = pltpu.make_async_copy(held, out_ref, own_sem)
    out.start()
    out.wait()


def ring_gather(block, xs, zs, kernel_id):
    return pl.pallas_call(
        functools.partial(ring_gather_kernel, zs, xs),
        out_shape=jax.ShapeDtypeStruct((zs, xs) + block.shape, block.dtype),
        in_specs=[pl.BlockSpec(memory_space=pltpu.VMEM)],
        out_specs=pl.BlockSpec(memory_space=pl.ANY),
        scratch_shapes=[
            pltpu.VMEM((zs, xs) + block.shape, block.dtype),
            pltpu.SemaphoreType.DMA(()),
            pltpu.SemaphoreType.DMA((2, zs - 1)),
            pltpu.SemaphoreType.DMA((2, zs - 1)),
            pltpu.SemaphoreType.DMA((xs,)),
            pltpu.SemaphoreType.DMA((xs,)),
        ],
        compiler_params=pltpu.CompilerParams(
            collective_id=kernel_id, has_side_effects=True, vmem_limit_bytes=56 * 1024 * 1024
        ),
    )(block)


def swap_kernel(src_ref, out_ref, landed, sems):
    other = 1 - lax.axis_index("req")
    barrier = pltpu.get_barrier_semaphore()
    pl.semaphore_signal(barrier, inc=1, device_id=peer_on("req", other), device_id_type=MESH_IDS)
    pl.semaphore_wait(barrier, 1)
    copy = pltpu.make_async_remote_copy(
        src_ref=src_ref,
        dst_ref=landed,
        send_sem=sems.at[0],
        recv_sem=sems.at[1],
        device_id=peer_on("req", other),
        device_id_type=MESH_IDS,
    )
    copy.start()
    copy.wait_send()
    copy.wait_recv()
    out_ref[...] = landed[...]


def partner_swap(value, kernel_id):
    return pl.pallas_call(
        swap_kernel,
        out_shape=jax.ShapeDtypeStruct(value.shape, value.dtype),
        in_specs=[pl.BlockSpec(memory_space=pltpu.VMEM)],
        out_specs=pl.BlockSpec(memory_space=pltpu.VMEM),
        scratch_shapes=[pltpu.VMEM(value.shape, value.dtype), pltpu.SemaphoreType.DMA((2,))],
        compiler_params=pltpu.CompilerParams(collective_id=kernel_id, has_side_effects=True),
    )(value)


def layer_norm(tensor, epsilon):
    average = jnp.mean(tensor, axis=-1, keepdims=True)
    centered = tensor - average
    spread = jnp.mean(centered * centered, axis=-1, keepdims=True)
    return centered * lax.rsqrt(spread + epsilon)


def modulate(tensor, offset, factor):
    return (layer_norm(tensor, 1e-05) * (1.0 + factor) + offset).astype(jnp.bfloat16)


def head_norm(tensor, scaling):
    return (layer_norm(tensor, 1e-06) * scaling).astype(jnp.bfloat16)


def pick_entry(entries, position):
    slot_ids = jnp.arange(entries.shape[0], dtype=jnp.int32)
    return jnp.sum(jnp.where(slot_ids == position, entries, jnp.zeros_like(entries)))


def solver_weights(step_index):
    plan = jnp.linspace(0.00085**0.5, 0.012**0.5, TRAIN_STEPS, dtype=jnp.float32) ** 2
    cumulative = jnp.cumprod(1.0 - plan)
    alpha_now = pick_entry(cumulative, step_index)
    alpha_prev = pick_entry(cumulative, step_index - STRIDE)
    root_now = jnp.sqrt(alpha_now)
    rest_now = jnp.sqrt(1.0 - alpha_now)
    root_prev = jnp.sqrt(alpha_prev)
    rest_prev = jnp.sqrt(1.0 - alpha_prev)
    return (
        root_prev * root_now + rest_prev * rest_now,
        rest_prev * root_now - root_prev * rest_now,
    )


def key_mask(count, owners, grid, text_len, span, block_tokens, tile, text_rows):
    positions = jnp.arange(count, dtype=jnp.int32)
    owner_row = positions // span
    within = positions % span
    is_video = within < block_tokens
    owner_col = within // tile
    local_ids = within % tile
    token_row = owner_row * TR + local_ids // TC % TR
    token_col = owner_col * TC + local_ids % TC
    text_index = owner_row * text_rows + within - block_tokens
    matches = jnp.arange(grid.shape[0], dtype=jnp.int32)[None, :] == owners[:, None]
    rows_live = jnp.sum(jnp.where(matches, grid[None, :, 0], 0), axis=1)
    cols_live = jnp.sum(jnp.where(matches, grid[None, :, 1], 0), axis=1)
    text_lens = jnp.sum(jnp.where(matches, text_len[None, :], 0), axis=1)
    video_live = (token_row[None, :] < rows_live[:, None]) & (
        token_col[None, :] < cols_live[:, None]
    )
    text_live = (text_index[None, :] < text_lens[:, None]) & (within < block_tokens + text_rows)[None, :]
    return jnp.where(is_video[None, :], video_live, text_live).astype(jnp.float32)


def projector(stacked, piece):
    return jnp.einsum("gld,cde->cgle", stacked, piece, preferred_element_type=jnp.float32)


def attention_step(queries, owners, grid, text_len, span, block_tokens, tile, text_rows):
    score_scale = queries.shape[3] ** (-0.5)

    def attend(carry, pieces, start):
        key_piece, value_piece = pieces
        live_keys = key_mask(
            key_piece.shape[1], owners, grid, text_len, span, block_tokens, tile, text_rows
        )
        scores = (
            jnp.einsum("gqhd,gkhd->gqhk", queries, key_piece, preferred_element_type=jnp.float32)
            * score_scale
        )
        raw_weights = jnp.exp(scores) * live_keys[:, None, None, :]
        weighted = jnp.einsum(
            "gqhk,gkhd->gqhd",
            raw_weights.astype(jnp.bfloat16),
            value_piece,
            preferred_element_type=jnp.float32,
        )
        return (weighted, jnp.sum(raw_weights, axis=3))

    return attend


def shards(
    hidden,
    text_hidden,
    text_len,
    grid,
    timestep,
    modulation,
    q_gain,
    k_gain,
    w_qkv,
    w_out,
    w_up,
    w_down,
    w_proj,
    latent,
    conv_w,
):
    col_count = lax.axis_size("col")
    request_id = lax.axis_index("req")
    row_id = lax.axis_index("row")
    col_id = lax.axis_index("col")
    block_tokens = hidden.shape[1]
    tile = block_tokens // col_count
    text_rows = text_hidden.shape[1]
    head_dim = q_gain.shape[0]
    adaptive = modulation[0]
    source = hidden[0].astype(jnp.float32)
    joined = jnp.concatenate(
        [
            modulate(source, adaptive[0], adaptive[1]),
            modulate(text_hidden[0].astype(jnp.float32), adaptive[0], adaptive[1]),
        ],
        axis=0,
    )
    span = joined.shape[0]
    stacked = joined[None]
    owners = jnp.reshape(request_id, (1,))
    half_cols = w_qkv.shape[2] // 2
    own_half = lax.dynamic_slice_in_dim(w_qkv, request_id * half_cols, half_cols, 2)
    gathered_half = lax.all_gather(own_half, "row", axis=1, tiled=True)
    half_heads = half_cols // head_dim

    def project(rows):
        mixed_cols = jnp.einsum("ld,cde->cle", rows, gathered_half, preferred_element_type=jnp.float32)
        split = mixed_cols.reshape(3, span, half_heads, head_dim)
        return jnp.stack(
            [head_norm(split[0], q_gain), head_norm(split[1], k_gain), split[2].astype(jnp.bfloat16)]
        )

    mine = project(joined)
    theirs = project(partner_swap(joined, 4))
    received = partner_swap(theirs.reshape(3 * span, half_cols), 5).reshape(theirs.shape)
    full = jnp.concatenate(
        [jnp.where(request_id == 0, mine, received), jnp.where(request_id == 0, received, mine)], axis=2
    )
    groups = 1
    heads_here = full.shape[2]
    queries = full[0, :block_tokens][None]
    key_block = full[1][None]
    value_block = full[2][None]
    attend = attention_step(queries, owners, grid, text_len, span, block_tokens, tile, text_rows)
    empty_state = (jnp.zeros(queries.shape, jnp.float32), jnp.zeros(queries.shape[:3], jnp.float32))
    padded_span = 16 * pl.cdiv(span, 16)
    both = jnp.stack([key_block[0], value_block[0]], axis=0).reshape(2, span, heads_here * head_dim)
    both = jnp.pad(both, ((0, 0), (0, padded_span - span), (0, 0)))[None]
    gathered = lax.all_gather(both, "row", axis=0, tiled=True)
    live = key_mask(
        gathered.shape[0] * padded_span, owners, grid, text_len, padded_span, block_tokens, tile, text_rows
    )
    attended = attention(
        queries[0].reshape(block_tokens, heads_here * head_dim),
        gathered,
        live,
        head_dim ** (-0.5),
    )
    partial_out = jnp.dot(attended, w_out, preferred_element_type=jnp.float32)
    projected = scatter_sum(partial_out, "col", 1)
    own_rows = lax.dynamic_slice_in_dim(source, col_id * tile, tile, 0)
    mixed = lax.optimization_barrier(
        (own_rows + adaptive[2] * projected).astype(jnp.bfloat16)
    ).astype(jnp.float32)
    second_norm = modulate(mixed, adaptive[3], adaptive[4])
    hidden_units = jax.nn.gelu(
        jnp.dot(
            ring_gather(second_norm, 4, 8, 2).reshape(-1, second_norm.shape[1]),
            w_up,
            preferred_element_type=jnp.float32,
        ),
        approximate=True,
    ).astype(jnp.bfloat16)
    feed_terms = jnp.dot(hidden_units, w_down, preferred_element_type=jnp.float32)
    feed_out = ring_scatter_sum(feed_terms.astype(jnp.bfloat16), 4, 8, 0)
    out_hidden = (mixed + adaptive[5] * feed_out).astype(jnp.bfloat16)
    final_norm = modulate(out_hidden.astype(jnp.float32), adaptive[6], adaptive[7])
    velocity = jnp.dot(final_norm, w_proj, preferred_element_type=jnp.float32)
    local_ids = jnp.arange(tile, dtype=jnp.int32)
    token_row = row_id * TR + local_ids // TC % TR
    token_col = col_id * TC + local_ids % TC
    rows_live = pick_entry(grid[:, 0], request_id)
    cols_live = pick_entry(grid[:, 1], request_id)
    live_tokens = ((token_row < rows_live) & (token_col < cols_live)).astype(jnp.float32)
    keep_part, velocity_part = solver_weights(pick_entry(timestep, request_id))
    updated = (keep_part * latent[0] + velocity_part * velocity) * live_tokens[:, None]
    pixels = (
        updated.reshape(FR, TR, TC, CH, 2, 2)
        .transpose(0, 1, 4, 2, 5, 3)
        .reshape(FR, 2 * TR, 2 * TC, CH)
    )
    scaled = (pixels / latent_scale).astype(jnp.bfloat16)
    padded = extended(scaled, (("row", 1), ("col", 2)), 1)
    running = jnp.zeros((FR, 2 * TR, 2 * TC, conv_w.shape[3]), jnp.float32)
    for row_tap in range(3):
        for col_tap in range(3):
            window = padded[:, row_tap : row_tap + 2 * TR, col_tap : col_tap + 2 * TC, :]
            running = running + jnp.einsum(
                "fyxc,cd->fyxd",
                window,
                conv_w[row_tap, col_tap],
                preferred_element_type=jnp.float32,
            )
    return (out_hidden[None], updated[None], running.astype(jnp.bfloat16)[None])


def solution(mesh):
    placed = (
        P("req", "row", None),
        P("req", "row", None),
        P(),
        P(),
        P(),
        P("req", None, None),
        P(),
        P(),
        P(None, "row", "col"),
        P("col", None),
        P(None, "row"),
        P("row", None),
        P(),
        P("req", ("row", "col"), None),
        P(),
    )
    return jax.shard_map(
        shards,
        mesh=mesh,
        in_specs=placed,
        out_specs=(
            P("req", ("row", "col"), None),
            P("req", ("row", "col"), None),
            P("req", None, "row", "col", None),
        ),
        check_vma=False,
    )
```

```python
import functools

import jax
import jax.numpy as jnp
from jax import lax
from jax.sharding import PartitionSpec as P
from jax.experimental import pallas as pl
from jax.experimental.pallas import tpu as pltpu

MESH_IDS = pl.DeviceIdType.MESH

CH = 16
FR = 6
TR = 1
TC = 4
TRAIN_STEPS = 1000
STRIDE = 250


latent_scale = 0.7


def extended(cells, sides, width):
    for axis, dim in sides:
        count = lax.axis_size(axis)
        ends = count - 1
        head = lax.slice_in_dim(cells, 0, width, axis=dim)
        tail = lax.slice_in_dim(cells, cells.shape[dim] - width, cells.shape[dim], axis=dim)
        cells = jnp.concatenate(
            [
                lax.ppermute(tail, axis, [(i, (i + 1) % count) for i in range(ends)]),
                cells,
                lax.ppermute(head, axis, [((i + 1) % count, i) for i in range(ends)]),
            ],
            axis=dim,
        )
    return cells


def peer_on(axis, peer):
    return tuple(peer if name == axis else lax.axis_index(name) for name in ("req", "row", "col"))


def scatter_sum_kernel(axis, count, rows, part_ref, out_ref, landed, send_sems, recv_sems, own_sem):
    me = lax.axis_index(axis)
    barrier = pltpu.get_barrier_semaphore()
    for step in range(1, count):
        peer = lax.rem(me + step, count)
        pl.semaphore_signal(barrier, inc=1, device_id=peer_on(axis, peer), device_id_type=MESH_IDS)
    pl.semaphore_wait(barrier, count - 1)
    own = pltpu.make_async_copy(part_ref.at[pl.ds(me * rows, rows)], landed.at[me], own_sem)
    own.start()
    sends = []
    for step in range(1, count):
        peer = lax.rem(me + step, count)
        copy = pltpu.make_async_remote_copy(
            src_ref=part_ref.at[pl.ds(peer * rows, rows)],
            dst_ref=landed.at[me],
            send_sem=send_sems.at[step],
            recv_sem=recv_sems.at[step],
            device_id=peer_on(axis, peer),
            device_id_type=MESH_IDS,
        )
        copy.start()
        sends.append(copy)
    own.wait()
    for step in range(1, count):
        source = lax.rem(me + count - step, count)
        pltpu.make_async_remote_copy(
            src_ref=part_ref.at[pl.ds(me * rows, rows)],
            dst_ref=landed.at[source],
            send_sem=send_sems.at[step],
            recv_sem=recv_sems.at[step],
            device_id=peer_on(axis, source),
            device_id_type=MESH_IDS,
        ).wait_recv()
    for copy in sends:
        copy.wait_send()
    total = landed[0].astype(jnp.float32)
    for slot in range(1, count):
        total = total + landed[slot].astype(jnp.float32)
    out_ref[...] = total


def scatter_sum(part, axis, kernel_id):
    count = lax.axis_size(axis)
    rows = part.shape[0] // count
    width = part.shape[1]
    return pl.pallas_call(
        functools.partial(scatter_sum_kernel, axis, count, rows),
        out_shape=jax.ShapeDtypeStruct((rows, width), jnp.float32),
        in_specs=[pl.BlockSpec(memory_space=pl.ANY)],
        out_specs=pl.BlockSpec(memory_space=pltpu.VMEM),
        scratch_shapes=[
            pltpu.VMEM((count, rows, width), part.dtype),
            pltpu.SemaphoreType.DMA((count,)),
            pltpu.SemaphoreType.DMA((count,)),
            pltpu.SemaphoreType.DMA(()),
        ],
        compiler_params=pltpu.CompilerParams(
            collective_id=kernel_id, has_side_effects=True, vmem_limit_bytes=48 * 1024 * 1024
        ),
    )(part)


def attention_kernel(scale, q_ref, kv_ref, live_ref, out_ref):
    sources, _, block, width = kv_ref.shape
    lane = lax.broadcasted_iota(jnp.int32, (1, 128), 1)
    first = lane < 64
    live = live_ref[...]
    for pair in range(width // 128):
        cols = slice(pair * 128, (pair + 1) * 128)
        query = q_ref[:, cols]
        keys = kv_ref[:, 0, :, cols].reshape(sources * block, 128)
        values = kv_ref[:, 1, :, cols].reshape(sources * block, 128)
        results = []
        for half in (first, jnp.logical_not(first)):
            picked = jnp.where(half, query, jnp.zeros_like(query))
            scores = lax.dot_general(
                picked, keys, (((1,), (1,)), ((), ())), preferred_element_type=jnp.float32
            ) * scale
            weights = jnp.exp(scores) * live
            totals = jnp.sum(weights, axis=1, keepdims=True)
            summed = jnp.dot(weights.astype(jnp.bfloat16), values, preferred_element_type=jnp.float32)
            results.append(summed / totals)
        out_ref[:, cols] = jnp.where(first, results[0], results[1]).astype(out_ref.dtype)


def attention(queries, gathered, live, scale):
    return pl.pallas_call(
        functools.partial(attention_kernel, scale),
        out_shape=jax.ShapeDtypeStruct(queries.shape, jnp.bfloat16),
        in_specs=[pl.BlockSpec(memory_space=pltpu.VMEM)] * 3,
        out_specs=pl.BlockSpec(memory_space=pltpu.VMEM),
        compiler_params=pltpu.CompilerParams(vmem_limit_bytes=56 * 1024 * 1024),
    )(queries, gathered, live)


def ring_scatter_kernel(zs, xs, part_ref, out_ref, landed, outgoing, own_sum, crossed, ring_send, ring_recv, cross_send, cross_recv):
    me = lax.axis_index("row")
    xm = me // zs
    zm = me % zs
    ahead = xm * zs + lax.rem(zm + 1, zs)
    behind = xm * zs + lax.rem(zm + zs - 1, zs)
    half = part_ref.shape[3] // 2
    barrier = pltpu.get_barrier_semaphore()
    targets = [ahead, behind] + [lax.rem(xm + k, xs) * zs + zm for k in range(1, xs)]
    for peer in targets:
        pl.semaphore_signal(barrier, inc=1, device_id=peer_on("row", peer), device_id_type=MESH_IDS)
    pl.semaphore_wait(barrier, len(targets))
    ways = ((0, ahead, behind, -1), (1, behind, ahead, 1))
    pending = []
    for step in range(zs - 1):
        for way, dest, origin, sign in ways:
            cols = pl.ds(way * half, half)
            chunk = lax.rem(zm + sign * (1 + step) + 2 * zs, zs)
            if step == 0:
                source = part_ref.at[chunk, :, :, cols]
            else:
                arrived = pltpu.make_async_remote_copy(
                    src_ref=outgoing.at[way, step - 1],
                    dst_ref=landed.at[way, step - 1],
                    send_sem=ring_send.at[way, step - 1],
                    recv_sem=ring_recv.at[way, step - 1],
                    device_id=peer_on("row", origin),
                    device_id_type=MESH_IDS,
                )
                arrived.wait_recv()
                outgoing[way, step] = (
                    landed[way, step - 1].astype(jnp.float32)
                    + part_ref[chunk, :, :, cols].astype(jnp.float32)
                ).astype(outgoing.dtype)
                source = outgoing.at[way, step]
            copy = pltpu.make_async_remote_copy(
                src_ref=source,
                dst_ref=landed.at[way, step],
                send_sem=ring_send.at[way, step],
                recv_sem=ring_recv.at[way, step],
                device_id=peer_on("row", dest),
                device_id_type=MESH_IDS,
            )
            copy.start()
            pending.append(copy)
    last = zs - 2
    for way, dest, origin, sign in ways:
        cols = pl.ds(way * half, half)
        pltpu.make_async_remote_copy(
            src_ref=outgoing.at[way, last],
            dst_ref=landed.at[way, last],
            send_sem=ring_send.at[way, last],
            recv_sem=ring_recv.at[way, last],
            device_id=peer_on("row", origin),
            device_id_type=MESH_IDS,
        ).wait_recv()
        own_sum[:, :, cols] = landed[way, last].astype(jnp.float32) + part_ref[zm, :, :, cols].astype(jnp.float32)
    crossed[0] = own_sum[...].astype(crossed.dtype)
    sends = []
    for k in range(1, xs):
        peer_x = lax.rem(xm + k, xs)
        copy = pltpu.make_async_remote_copy(
            src_ref=crossed.at[0, peer_x],
            dst_ref=crossed.at[k, 0],
            send_sem=cross_send.at[k],
            recv_sem=cross_recv.at[k],
            device_id=peer_on("row", peer_x * zs + zm),
            device_id_type=MESH_IDS,
        )
        copy.start()
        sends.append(copy)
    total = own_sum[xm]
    for k in range(1, xs):
        origin_x = lax.rem(xm + xs - k, xs)
        pltpu.make_async_remote_copy(
            src_ref=crossed.at[0, 0],
            dst_ref=crossed.at[k, 0],
            send_sem=cross_send.at[k],
            recv_sem=cross_recv.at[k],
            device_id=peer_on("row", origin_x * zs + zm),
            device_id_type=MESH_IDS,
        ).wait_recv()
        total = total + crossed[k, 0].astype(jnp.float32)
    out_ref[...] = total
    for copy in pending + sends:
        copy.wait_send()


def ring_scatter_sum(part, xs, zs, kernel_id):
    rows = part.shape[0] // (xs * zs)
    width = part.shape[1]
    arranged = part.reshape(zs, xs, rows, width)
    return pl.pallas_call(
        functools.partial(ring_scatter_kernel, zs, xs),
        out_shape=jax.ShapeDtypeStruct((rows, width), jnp.float32),
        in_specs=[pl.BlockSpec(memory_space=pltpu.VMEM)],
        out_specs=pl.BlockSpec(memory_space=pltpu.VMEM),
        scratch_shapes=[
            pltpu.VMEM((2, zs - 1, xs, rows, width // 2), part.dtype),
            pltpu.VMEM((2, zs - 1, xs, rows, width // 2), part.dtype),
            pltpu.VMEM((xs, rows, width), jnp.float32),
            pltpu.VMEM((xs, xs, rows, width), part.dtype),
            pltpu.SemaphoreType.DMA((2, zs - 1)),
            pltpu.SemaphoreType.DMA((2, zs - 1)),
            pltpu.SemaphoreType.DMA((xs,)),
            pltpu.SemaphoreType.DMA((xs,)),
        ],
        compiler_params=pltpu.CompilerParams(
            collective_id=kernel_id, has_side_effects=True, vmem_limit_bytes=56 * 1024 * 1024
        ),
    )(arranged)


def ring_gather_kernel(zs, xs, block_ref, out_ref, held, own_sem, ring_send, ring_recv, cross_send, cross_recv):
    me = lax.axis_index("row")
    xm = me // zs
    zm = me % zs
    ahead = xm * zs + lax.rem(zm + 1, zs)
    behind = xm * zs + lax.rem(zm + zs - 1, zs)
    barrier = pltpu.get_barrier_semaphore()
    targets = [ahead, behind] + [lax.rem(xm + k, xs) * zs + zm for k in range(1, xs)]
    for peer in targets:
        pl.semaphore_signal(barrier, inc=1, device_id=peer_on("row", peer), device_id_type=MESH_IDS)
    pl.semaphore_wait(barrier, len(targets))
    own = pltpu.make_async_copy(block_ref, held.at[zm, xm], own_sem)
    own.start()
    pending = []
    for k in range(1, xs):
        peer_x = lax.rem(xm + k, xs)
        copy = pltpu.make_async_remote_copy(
            src_ref=block_ref,
            dst_ref=held.at[zm, xm],
            send_sem=cross_send.at[k],
            recv_sem=cross_recv.at[k],
            device_id=peer_on("row", peer_x * zs + zm),
            device_id_type=MESH_IDS,
        )
        copy.start()
        pending.append(copy)
    own.wait()
    for k in range(1, xs):
        origin_x = lax.rem(xm + xs - k, xs)
        pltpu.make_async_remote_copy(
            src_ref=block_ref,
            dst_ref=held.at[zm, origin_x],
            send_sem=cross_send.at[k],
            recv_sem=cross_recv.at[k],
            device_id=peer_on("row", origin_x * zs + zm),
            device_id_type=MESH_IDS,
        ).wait_recv()
    split = xs // 2
    ways = ((0, ahead, behind, -1, pl.ds(0, split)), (1, behind, ahead, 1, pl.ds(split, xs - split)))
    for step in range(zs):
        for way, dest, origin, sign, part in ways:
            group = lax.rem(zm + sign * step + zs, zs)
            if step > 0:
                pltpu.make_async_remote_copy(
                    src_ref=held.at[group, part],
                    dst_ref=held.at[group, part],
                    send_sem=ring_send.at[way, step - 1],
                    recv_sem=ring_recv.at[way, step - 1],
                    device_id=peer_on("row", origin),
                    device_id_type=MESH_IDS,
                ).wait_recv()
            if step < zs - 1:
                copy = pltpu.make_async_remote_copy(
                    src_ref=held.at[group, part],
                    dst_ref=held.at[group, part],
                    send_sem=ring_send.at[way, step],
                    recv_sem=ring_recv.at[way, step],
                    device_id=peer_on("row", dest),
                    device_id_type=MESH_IDS,
                )
                copy.start()
                pending.append(copy)
    for copy in pending:
        copy.wait_send()
    out = pltpu.make_async_copy(held, out_ref, own_sem)
    out.start()
    out.wait()


def ring_gather(block, xs, zs, kernel_id):
    return pl.pallas_call(
        functools.partial(ring_gather_kernel, zs, xs),
        out_shape=jax.ShapeDtypeStruct((zs, xs) + block.shape, block.dtype),
        in_specs=[pl.BlockSpec(memory_space=pltpu.VMEM)],
        out_specs=pl.BlockSpec(memory_space=pl.ANY),
        scratch_shapes=[
            pltpu.VMEM((zs, xs) + block.shape, block.dtype),
            pltpu.SemaphoreType.DMA(()),
            pltpu.SemaphoreType.DMA((2, zs - 1)),
            pltpu.SemaphoreType.DMA((2, zs - 1)),
            pltpu.SemaphoreType.DMA((xs,)),
            pltpu.SemaphoreType.DMA((xs,)),
        ],
        compiler_params=pltpu.CompilerParams(
            collective_id=kernel_id, has_side_effects=True, vmem_limit_bytes=56 * 1024 * 1024
        ),
    )(block)


def swap_kernel(src_ref, out_ref, landed, sems):
    other = 1 - lax.axis_index("req")
    barrier = pltpu.get_barrier_semaphore()
    pl.semaphore_signal(barrier, inc=1, device_id=peer_on("req", other), device_id_type=MESH_IDS)
    pl.semaphore_wait(barrier, 1)
    copy = pltpu.make_async_remote_copy(
        src_ref=src_ref,
        dst_ref=landed,
        send_sem=sems.at[0],
        recv_sem=sems.at[1],
        device_id=peer_on("req", other),
        device_id_type=MESH_IDS,
    )
    copy.start()
    copy.wait_send()
    copy.wait_recv()
    out_ref[...] = landed[...]


def partner_swap(value, kernel_id):
    return pl.pallas_call(
        swap_kernel,
        out_shape=jax.ShapeDtypeStruct(value.shape, value.dtype),
        in_specs=[pl.BlockSpec(memory_space=pltpu.VMEM)],
        out_specs=pl.BlockSpec(memory_space=pltpu.VMEM),
        scratch_shapes=[pltpu.VMEM(value.shape, value.dtype), pltpu.SemaphoreType.DMA((2,))],
        compiler_params=pltpu.CompilerParams(collective_id=kernel_id, has_side_effects=True),
    )(value)


def layer_norm(tensor, epsilon):
    average = jnp.mean(tensor, axis=-1, keepdims=True)
    centered = tensor - average
    spread = jnp.mean(centered * centered, axis=-1, keepdims=True)
    return centered * lax.rsqrt(spread + epsilon)


def modulate(tensor, offset, factor):
    return (layer_norm(tensor, 1e-05) * (1.0 + factor) + offset).astype(jnp.bfloat16)


def head_norm(tensor, scaling):
    return (layer_norm(tensor, 1e-06) * scaling).astype(jnp.bfloat16)


def pick_entry(entries, position):
    slot_ids = jnp.arange(entries.shape[0], dtype=jnp.int32)
    return jnp.sum(jnp.where(slot_ids == position, entries, jnp.zeros_like(entries)))


def solver_weights(step_index):
    plan = jnp.linspace(0.00085**0.5, 0.012**0.5, TRAIN_STEPS, dtype=jnp.float32) ** 2
    cumulative = jnp.cumprod(1.0 - plan)
    alpha_now = pick_entry(cumulative, step_index)
    alpha_prev = pick_entry(cumulative, step_index - STRIDE)
    root_now = jnp.sqrt(alpha_now)
    rest_now = jnp.sqrt(1.0 - alpha_now)
    root_prev = jnp.sqrt(alpha_prev)
    rest_prev = jnp.sqrt(1.0 - alpha_prev)
    return (
        root_prev * root_now + rest_prev * rest_now,
        rest_prev * root_now - root_prev * rest_now,
    )


def key_mask(count, owners, grid, text_len, span, block_tokens, tile, text_rows):
    positions = jnp.arange(count, dtype=jnp.int32)
    owner_row = positions // span
    within = positions % span
    is_video = within < block_tokens
    owner_col = within // tile
    local_ids = within % tile
    token_row = owner_row * TR + local_ids // TC % TR
    token_col = owner_col * TC + local_ids % TC
    text_index = owner_row * text_rows + within - block_tokens
    matches = jnp.arange(grid.shape[0], dtype=jnp.int32)[None, :] == owners[:, None]
    rows_live = jnp.sum(jnp.where(matches, grid[None, :, 0], 0), axis=1)
    cols_live = jnp.sum(jnp.where(matches, grid[None, :, 1], 0), axis=1)
    text_lens = jnp.sum(jnp.where(matches, text_len[None, :], 0), axis=1)
    video_live = (token_row[None, :] < rows_live[:, None]) & (
        token_col[None, :] < cols_live[:, None]
    )
    text_live = (text_index[None, :] < text_lens[:, None]) & (within < block_tokens + text_rows)[None, :]
    return jnp.where(is_video[None, :], video_live, text_live).astype(jnp.float32)


def projector(stacked, piece):
    return jnp.einsum("gld,cde->cgle", stacked, piece, preferred_element_type=jnp.float32)


def attention_step(queries, owners, grid, text_len, span, block_tokens, tile, text_rows):
    score_scale = queries.shape[3] ** (-0.5)

    def attend(carry, pieces, start):
        key_piece, value_piece = pieces
        live_keys = key_mask(
            key_piece.shape[1], owners, grid, text_len, span, block_tokens, tile, text_rows
        )
        scores = (
            jnp.einsum("gqhd,gkhd->gqhk", queries, key_piece, preferred_element_type=jnp.float32)
            * score_scale
        )
        raw_weights = jnp.exp(scores) * live_keys[:, None, None, :]
        weighted = jnp.einsum(
            "gqhk,gkhd->gqhd",
            raw_weights.astype(jnp.bfloat16),
            value_piece,
            preferred_element_type=jnp.float32,
        )
        return (weighted, jnp.sum(raw_weights, axis=3))

    return attend


def shards(
    hidden,
    text_hidden,
    text_len,
    grid,
    timestep,
    modulation,
    q_gain,
    k_gain,
    w_qkv,
    w_out,
    w_up,
    w_down,
    w_proj,
    latent,
    conv_w,
):
    col_count = lax.axis_size("col")
    request_id = lax.axis_index("req")
    row_id = lax.axis_index("row")
    col_id = lax.axis_index("col")
    block_tokens = hidden.shape[1]
    tile = block_tokens // col_count
    text_rows = text_hidden.shape[1]
    head_dim = q_gain.shape[0]
    adaptive = modulation[0]
    source = hidden[0].astype(jnp.float32)
    joined = jnp.concatenate(
        [
            modulate(source, adaptive[0], adaptive[1]),
            modulate(text_hidden[0].astype(jnp.float32), adaptive[0], adaptive[1]),
        ],
        axis=0,
    )
    span = joined.shape[0]
    stacked = joined[None]
    owners = jnp.reshape(request_id, (1,))
    half_cols = w_qkv.shape[2] // 2
    own_half = lax.dynamic_slice_in_dim(w_qkv, request_id * half_cols, half_cols, 2)
    gathered_half = lax.all_gather(own_half, "row", axis=1, tiled=True)
    half_heads = half_cols // head_dim

    both_rows = jnp.concatenate([joined, partner_swap(joined, 4)], axis=0)
    projected_rows = jnp.einsum(
        "ld,cde->cle", both_rows, gathered_half, preferred_element_type=jnp.float32
    ).reshape(3, 2 * span, half_heads, head_dim)
    normed_q = head_norm(projected_rows[0], q_gain)
    normed_k = head_norm(projected_rows[1], k_gain)
    plain_v = projected_rows[2].astype(jnp.bfloat16)
    mine = jnp.stack([normed_q[:span], normed_k[:span], plain_v[:span]])
    theirs = jnp.stack([normed_q[span:], normed_k[span:], plain_v[span:]])
    received = partner_swap(theirs.reshape(3 * span, half_cols), 5).reshape(theirs.shape)
    full = jnp.concatenate(
        [jnp.where(request_id == 0, mine, received), jnp.where(request_id == 0, received, mine)], axis=2
    )
    groups = 1
    heads_here = full.shape[2]
    queries = full[0, :block_tokens][None]
    key_block = full[1][None]
    value_block = full[2][None]
    attend = attention_step(queries, owners, grid, text_len, span, block_tokens, tile, text_rows)
    empty_state = (jnp.zeros(queries.shape, jnp.float32), jnp.zeros(queries.shape[:3], jnp.float32))
    padded_span = 16 * pl.cdiv(span, 16)
    both = jnp.stack([key_block[0], value_block[0]], axis=0).reshape(2, span, heads_here * head_dim)
    both = jnp.pad(both, ((0, 0), (0, padded_span - span), (0, 0)))[None]
    gathered = lax.all_gather(both, "row", axis=0, tiled=True)
    live = key_mask(
        gathered.shape[0] * padded_span, owners, grid, text_len, padded_span, block_tokens, tile, text_rows
    )
    attended = attention(
        queries[0].reshape(block_tokens, heads_here * head_dim),
        gathered,
        live,
        head_dim ** (-0.5),
    )
    partial_out = jnp.dot(attended, w_out, preferred_element_type=jnp.float32)
    projected = scatter_sum(partial_out, "col", 1)
    own_rows = lax.dynamic_slice_in_dim(source, col_id * tile, tile, 0)
    mixed = lax.optimization_barrier(
        (own_rows + adaptive[2] * projected).astype(jnp.bfloat16)
    ).astype(jnp.float32)
    second_norm = modulate(mixed, adaptive[3], adaptive[4])
    hidden_units = jax.nn.gelu(
        jnp.dot(
            ring_gather(second_norm, 4, 8, 2).reshape(-1, second_norm.shape[1]),
            w_up,
            preferred_element_type=jnp.float32,
        ),
        approximate=True,
    ).astype(jnp.bfloat16)
    feed_terms = jnp.dot(hidden_units, w_down, preferred_element_type=jnp.float32)
    feed_out = ring_scatter_sum(feed_terms.astype(jnp.bfloat16), 4, 8, 0)
    out_hidden = (mixed + adaptive[5] * feed_out).astype(jnp.bfloat16)
    final_norm = modulate(out_hidden.astype(jnp.float32), adaptive[6], adaptive[7])
    velocity = jnp.dot(final_norm, w_proj, preferred_element_type=jnp.float32)
    local_ids = jnp.arange(tile, dtype=jnp.int32)
    token_row = row_id * TR + local_ids // TC % TR
    token_col = col_id * TC + local_ids % TC
    rows_live = pick_entry(grid[:, 0], request_id)
    cols_live = pick_entry(grid[:, 1], request_id)
    live_tokens = ((token_row < rows_live) & (token_col < cols_live)).astype(jnp.float32)
    keep_part, velocity_part = solver_weights(pick_entry(timestep, request_id))
    updated = (keep_part * latent[0] + velocity_part * velocity) * live_tokens[:, None]
    pixels = (
        updated.reshape(FR, TR, TC, CH, 2, 2)
        .transpose(0, 1, 4, 2, 5, 3)
        .reshape(FR, 2 * TR, 2 * TC, CH)
    )
    scaled = (pixels / latent_scale).astype(jnp.bfloat16)
    padded = extended(scaled, (("row", 1), ("col", 2)), 1)
    running = jnp.zeros((FR, 2 * TR, 2 * TC, conv_w.shape[3]), jnp.float32)
    for row_tap in range(3):
        for col_tap in range(3):
            window = padded[:, row_tap : row_tap + 2 * TR, col_tap : col_tap + 2 * TC, :]
            running = running + jnp.einsum(
                "fyxc,cd->fyxd",
                window,
                conv_w[row_tap, col_tap],
                preferred_element_type=jnp.float32,
            )
    return (out_hidden[None], updated[None], running.astype(jnp.bfloat16)[None])


def solution(mesh):
    placed = (
        P("req", "row", None),
        P("req", "row", None),
        P(),
        P(),
        P(),
        P("req", None, None),
        P(),
        P(),
        P(None, "row", "col"),
        P("col", None),
        P(None, "row"),
        P("row", None),
        P(),
        P("req", ("row", "col"), None),
        P(),
    )
    return jax.shard_map(
        shards,
        mesh=mesh,
        in_specs=placed,
        out_specs=(
            P("req", ("row", "col"), None),
            P("req", ("row", "col"), None),
            P("req", None, "row", "col", None),
        ),
        check_vma=False,
    )
```

```python
import functools

import jax
import jax.numpy as jnp
from jax import lax
from jax.sharding import PartitionSpec as P
from jax.experimental import pallas as pl
from jax.experimental.pallas import tpu as pltpu

MESH_IDS = pl.DeviceIdType.MESH

CH = 16
FR = 6
TR = 1
TC = 4
TRAIN_STEPS = 1000
STRIDE = 250


latent_scale = 0.7


def extended(cells, sides, width):
    for axis, dim in sides:
        count = lax.axis_size(axis)
        ends = count - 1
        head = lax.slice_in_dim(cells, 0, width, axis=dim)
        tail = lax.slice_in_dim(cells, cells.shape[dim] - width, cells.shape[dim], axis=dim)
        cells = jnp.concatenate(
            [
                lax.ppermute(tail, axis, [(i, (i + 1) % count) for i in range(ends)]),
                cells,
                lax.ppermute(head, axis, [((i + 1) % count, i) for i in range(ends)]),
            ],
            axis=dim,
        )
    return cells


def peer_on(axis, peer):
    return tuple(peer if name == axis else lax.axis_index(name) for name in ("req", "row", "col"))


def scatter_sum_kernel(axis, count, rows, part_ref, out_ref, landed, send_sems, recv_sems, own_sem):
    me = lax.axis_index(axis)
    barrier = pltpu.get_barrier_semaphore()
    for step in range(1, count):
        peer = lax.rem(me + step, count)
        pl.semaphore_signal(barrier, inc=1, device_id=peer_on(axis, peer), device_id_type=MESH_IDS)
    pl.semaphore_wait(barrier, count - 1)
    own = pltpu.make_async_copy(part_ref.at[pl.ds(me * rows, rows)], landed.at[me], own_sem)
    own.start()
    sends = []
    for step in range(1, count):
        peer = lax.rem(me + step, count)
        copy = pltpu.make_async_remote_copy(
            src_ref=part_ref.at[pl.ds(peer * rows, rows)],
            dst_ref=landed.at[me],
            send_sem=send_sems.at[step],
            recv_sem=recv_sems.at[step],
            device_id=peer_on(axis, peer),
            device_id_type=MESH_IDS,
        )
        copy.start()
        sends.append(copy)
    own.wait()
    for step in range(1, count):
        source = lax.rem(me + count - step, count)
        pltpu.make_async_remote_copy(
            src_ref=part_ref.at[pl.ds(me * rows, rows)],
            dst_ref=landed.at[source],
            send_sem=send_sems.at[step],
            recv_sem=recv_sems.at[step],
            device_id=peer_on(axis, source),
            device_id_type=MESH_IDS,
        ).wait_recv()
    for copy in sends:
        copy.wait_send()
    total = landed[0].astype(jnp.float32)
    for slot in range(1, count):
        total = total + landed[slot].astype(jnp.float32)
    out_ref[...] = total


def scatter_sum(part, axis, kernel_id):
    count = lax.axis_size(axis)
    rows = part.shape[0] // count
    width = part.shape[1]
    return pl.pallas_call(
        functools.partial(scatter_sum_kernel, axis, count, rows),
        out_shape=jax.ShapeDtypeStruct((rows, width), jnp.float32),
        in_specs=[pl.BlockSpec(memory_space=pl.ANY)],
        out_specs=pl.BlockSpec(memory_space=pltpu.VMEM),
        scratch_shapes=[
            pltpu.VMEM((count, rows, width), part.dtype),
            pltpu.SemaphoreType.DMA((count,)),
            pltpu.SemaphoreType.DMA((count,)),
            pltpu.SemaphoreType.DMA(()),
        ],
        compiler_params=pltpu.CompilerParams(
            collective_id=kernel_id, has_side_effects=True, vmem_limit_bytes=48 * 1024 * 1024
        ),
    )(part)


def attention_kernel(scale, q_ref, kv_ref, live_ref, out_ref):
    sources, _, block, width = kv_ref.shape
    lane = lax.broadcasted_iota(jnp.int32, (1, 128), 1)
    first = lane < 64
    live = live_ref[...]
    for pair in range(width // 128):
        cols = slice(pair * 128, (pair + 1) * 128)
        query = q_ref[:, cols]
        keys = kv_ref[:, 0, :, cols].reshape(sources * block, 128)
        values = kv_ref[:, 1, :, cols].reshape(sources * block, 128)
        results = []
        for half in (first, jnp.logical_not(first)):
            picked = jnp.where(half, query, jnp.zeros_like(query))
            scores = lax.dot_general(
                picked, keys, (((1,), (1,)), ((), ())), preferred_element_type=jnp.float32
            ) * scale
            weights = jnp.exp(scores) * live
            totals = jnp.sum(weights, axis=1, keepdims=True)
            summed = jnp.dot(weights.astype(jnp.bfloat16), values, preferred_element_type=jnp.float32)
            results.append(summed / totals)
        out_ref[:, cols] = jnp.where(first, results[0], results[1]).astype(out_ref.dtype)


def attention(queries, gathered, live, scale):
    return pl.pallas_call(
        functools.partial(attention_kernel, scale),
        out_shape=jax.ShapeDtypeStruct(queries.shape, jnp.bfloat16),
        in_specs=[pl.BlockSpec(memory_space=pltpu.VMEM)] * 3,
        out_specs=pl.BlockSpec(memory_space=pltpu.VMEM),
        compiler_params=pltpu.CompilerParams(vmem_limit_bytes=56 * 1024 * 1024),
    )(queries, gathered, live)


def ring_scatter_kernel(zs, xs, part_ref, out_ref, landed, outgoing, own_sum, crossed, ring_send, ring_recv, cross_send, cross_recv):
    me = lax.axis_index("row")
    xm = me // zs
    zm = me % zs
    ahead = xm * zs + lax.rem(zm + 1, zs)
    behind = xm * zs + lax.rem(zm + zs - 1, zs)
    half = part_ref.shape[3] // 2
    barrier = pltpu.get_barrier_semaphore()
    targets = [ahead, behind] + [lax.rem(xm + k, xs) * zs + zm for k in range(1, xs)]
    for peer in targets:
        pl.semaphore_signal(barrier, inc=1, device_id=peer_on("row", peer), device_id_type=MESH_IDS)
    pl.semaphore_wait(barrier, len(targets))
    ways = ((0, ahead, behind, -1), (1, behind, ahead, 1))
    pending = []
    for step in range(zs - 1):
        for way, dest, origin, sign in ways:
            cols = pl.ds(way * half, half)
            chunk = lax.rem(zm + sign * (1 + step) + 2 * zs, zs)
            if step == 0:
                source = part_ref.at[chunk, :, :, cols]
            else:
                arrived = pltpu.make_async_remote_copy(
                    src_ref=outgoing.at[way, step - 1],
                    dst_ref=landed.at[way, step - 1],
                    send_sem=ring_send.at[way, step - 1],
                    recv_sem=ring_recv.at[way, step - 1],
                    device_id=peer_on("row", origin),
                    device_id_type=MESH_IDS,
                )
                arrived.wait_recv()
                outgoing[way, step] = (
                    landed[way, step - 1].astype(jnp.float32)
                    + part_ref[chunk, :, :, cols].astype(jnp.float32)
                ).astype(outgoing.dtype)
                source = outgoing.at[way, step]
            copy = pltpu.make_async_remote_copy(
                src_ref=source,
                dst_ref=landed.at[way, step],
                send_sem=ring_send.at[way, step],
                recv_sem=ring_recv.at[way, step],
                device_id=peer_on("row", dest),
                device_id_type=MESH_IDS,
            )
            copy.start()
            pending.append(copy)
    last = zs - 2
    for way, dest, origin, sign in ways:
        cols = pl.ds(way * half, half)
        pltpu.make_async_remote_copy(
            src_ref=outgoing.at[way, last],
            dst_ref=landed.at[way, last],
            send_sem=ring_send.at[way, last],
            recv_sem=ring_recv.at[way, last],
            device_id=peer_on("row", origin),
            device_id_type=MESH_IDS,
        ).wait_recv()
        own_sum[:, :, cols] = landed[way, last].astype(jnp.float32) + part_ref[zm, :, :, cols].astype(jnp.float32)
    crossed[0] = own_sum[...].astype(crossed.dtype)
    sends = []
    for k in range(1, xs):
        peer_x = lax.rem(xm + k, xs)
        copy = pltpu.make_async_remote_copy(
            src_ref=crossed.at[0, peer_x],
            dst_ref=crossed.at[k, 0],
            send_sem=cross_send.at[k],
            recv_sem=cross_recv.at[k],
            device_id=peer_on("row", peer_x * zs + zm),
            device_id_type=MESH_IDS,
        )
        copy.start()
        sends.append(copy)
    total = own_sum[xm]
    for k in range(1, xs):
        origin_x = lax.rem(xm + xs - k, xs)
        pltpu.make_async_remote_copy(
            src_ref=crossed.at[0, 0],
            dst_ref=crossed.at[k, 0],
            send_sem=cross_send.at[k],
            recv_sem=cross_recv.at[k],
            device_id=peer_on("row", origin_x * zs + zm),
            device_id_type=MESH_IDS,
        ).wait_recv()
        total = total + crossed[k, 0].astype(jnp.float32)
    out_ref[...] = total
    for copy in pending + sends:
        copy.wait_send()


def ring_scatter_sum(part, xs, zs, kernel_id):
    rows = part.shape[0] // (xs * zs)
    width = part.shape[1]
    arranged = part.reshape(zs, xs, rows, width)
    return pl.pallas_call(
        functools.partial(ring_scatter_kernel, zs, xs),
        out_shape=jax.ShapeDtypeStruct((rows, width), jnp.float32),
        in_specs=[pl.BlockSpec(memory_space=pltpu.VMEM)],
        out_specs=pl.BlockSpec(memory_space=pltpu.VMEM),
        scratch_shapes=[
            pltpu.VMEM((2, zs - 1, xs, rows, width // 2), part.dtype),
            pltpu.VMEM((2, zs - 1, xs, rows, width // 2), part.dtype),
            pltpu.VMEM((xs, rows, width), jnp.float32),
            pltpu.VMEM((xs, xs, rows, width), part.dtype),
            pltpu.SemaphoreType.DMA((2, zs - 1)),
            pltpu.SemaphoreType.DMA((2, zs - 1)),
            pltpu.SemaphoreType.DMA((xs,)),
            pltpu.SemaphoreType.DMA((xs,)),
        ],
        compiler_params=pltpu.CompilerParams(
            collective_id=kernel_id, has_side_effects=True, vmem_limit_bytes=56 * 1024 * 1024
        ),
    )(arranged)


def ring_gather_kernel(zs, xs, block_ref, out_ref, held, own_sem, ring_send, ring_recv, cross_send, cross_recv):
    me = lax.axis_index("row")
    xm = me // zs
    zm = me % zs
    ahead = xm * zs + lax.rem(zm + 1, zs)
    behind = xm * zs + lax.rem(zm + zs - 1, zs)
    barrier = pltpu.get_barrier_semaphore()
    targets = [ahead, behind] + [lax.rem(xm + k, xs) * zs + zm for k in range(1, xs)]
    for peer in targets:
        pl.semaphore_signal(barrier, inc=1, device_id=peer_on("row", peer), device_id_type=MESH_IDS)
    pl.semaphore_wait(barrier, len(targets))
    own = pltpu.make_async_copy(block_ref, held.at[zm, xm], own_sem)
    own.start()
    pending = []
    for k in range(1, xs):
        peer_x = lax.rem(xm + k, xs)
        copy = pltpu.make_async_remote_copy(
            src_ref=block_ref,
            dst_ref=held.at[zm, xm],
            send_sem=cross_send.at[k],
            recv_sem=cross_recv.at[k],
            device_id=peer_on("row", peer_x * zs + zm),
            device_id_type=MESH_IDS,
        )
        copy.start()
        pending.append(copy)
    own.wait()
    for k in range(1, xs):
        origin_x = lax.rem(xm + xs - k, xs)
        pltpu.make_async_remote_copy(
            src_ref=block_ref,
            dst_ref=held.at[zm, origin_x],
            send_sem=cross_send.at[k],
            recv_sem=cross_recv.at[k],
            device_id=peer_on("row", origin_x * zs + zm),
            device_id_type=MESH_IDS,
        ).wait_recv()
    split = xs // 2
    ways = ((0, ahead, behind, -1, pl.ds(0, split)), (1, behind, ahead, 1, pl.ds(split, xs - split)))
    for step in range(zs):
        for way, dest, origin, sign, part in ways:
            group = lax.rem(zm + sign * step + zs, zs)
            if step > 0:
                pltpu.make_async_remote_copy(
                    src_ref=held.at[group, part],
                    dst_ref=held.at[group, part],
                    send_sem=ring_send.at[way, step - 1],
                    recv_sem=ring_recv.at[way, step - 1],
                    device_id=peer_on("row", origin),
                    device_id_type=MESH_IDS,
                ).wait_recv()
            if step < zs - 1:
                copy = pltpu.make_async_remote_copy(
                    src_ref=held.at[group, part],
                    dst_ref=held.at[group, part],
                    send_sem=ring_send.at[way, step],
                    recv_sem=ring_recv.at[way, step],
                    device_id=peer_on("row", dest),
                    device_id_type=MESH_IDS,
                )
                copy.start()
                pending.append(copy)
    for copy in pending:
        copy.wait_send()
    out = pltpu.make_async_copy(held, out_ref, own_sem)
    out.start()
    out.wait()


def ring_gather(block, xs, zs, kernel_id):
    return pl.pallas_call(
        functools.partial(ring_gather_kernel, zs, xs),
        out_shape=jax.ShapeDtypeStruct((zs, xs) + block.shape, block.dtype),
        in_specs=[pl.BlockSpec(memory_space=pltpu.VMEM)],
        out_specs=pl.BlockSpec(memory_space=pl.ANY),
        scratch_shapes=[
            pltpu.VMEM((zs, xs) + block.shape, block.dtype),
            pltpu.SemaphoreType.DMA(()),
            pltpu.SemaphoreType.DMA((2, zs - 1)),
            pltpu.SemaphoreType.DMA((2, zs - 1)),
            pltpu.SemaphoreType.DMA((xs,)),
            pltpu.SemaphoreType.DMA((xs,)),
        ],
        compiler_params=pltpu.CompilerParams(
            collective_id=kernel_id, has_side_effects=True, vmem_limit_bytes=56 * 1024 * 1024
        ),
    )(block)


def swap_kernel(src_ref, out_ref, landed, sems):
    other = 1 - lax.axis_index("req")
    barrier = pltpu.get_barrier_semaphore()
    pl.semaphore_signal(barrier, inc=1, device_id=peer_on("req", other), device_id_type=MESH_IDS)
    pl.semaphore_wait(barrier, 1)
    copy = pltpu.make_async_remote_copy(
        src_ref=src_ref,
        dst_ref=landed,
        send_sem=sems.at[0],
        recv_sem=sems.at[1],
        device_id=peer_on("req", other),
        device_id_type=MESH_IDS,
    )
    copy.start()
    copy.wait_send()
    copy.wait_recv()
    out_ref[...] = landed[...]


def partner_swap(value, kernel_id):
    return pl.pallas_call(
        swap_kernel,
        out_shape=jax.ShapeDtypeStruct(value.shape, value.dtype),
        in_specs=[pl.BlockSpec(memory_space=pltpu.VMEM)],
        out_specs=pl.BlockSpec(memory_space=pltpu.VMEM),
        scratch_shapes=[pltpu.VMEM(value.shape, value.dtype), pltpu.SemaphoreType.DMA((2,))],
        compiler_params=pltpu.CompilerParams(collective_id=kernel_id, has_side_effects=True),
    )(value)


def halo_kernel(tile_ref, out_ref, slots, send_sems, recv_sems):
    req = lax.axis_index("req")
    row = lax.axis_index("row")
    col = lax.axis_index("col")
    rows = lax.axis_size("row")
    cols = lax.axis_size("col")
    offsets = [(a, b) for a in (-1, 0, 1) for b in (-1, 0, 1) if (a, b) != (0, 0)]

    def present(a, b):
        return (row + a >= 0) & (row + a < rows) & (col + b >= 0) & (col + b < cols)

    def link(a, b):
        return pltpu.make_async_remote_copy(
            src_ref=tile_ref,
            dst_ref=slots.at[1 - a, 1 - b],
            send_sem=send_sems.at[1 + a, 1 + b],
            recv_sem=recv_sems.at[1 - a, 1 - b],
            device_id=(req, row + a, col + b),
            device_id_type=MESH_IDS,
        )

    barrier = pltpu.get_barrier_semaphore()
    for a, b in offsets:
        @pl.when(present(a, b))
        def _():
            pl.semaphore_signal(barrier, inc=1, device_id=(req, row + a, col + b), device_id_type=MESH_IDS)
    up = (row + rows - 1) // rows
    down = (2 * rows - 2 - row) // rows
    left = (col + cols - 1) // cols
    right = (2 * cols - 2 - col) // cols
    pl.semaphore_wait(barrier, (1 + up + down) * (1 + left + right) - 1)
    for a, b in offsets:
        @pl.when(present(a, b))
        def _():
            link(a, b).start()
    for a, b in offsets:
        @pl.when(present(a, b))
        def _():
            copy = link(a, b)
            copy.wait_send()
            pltpu.make_async_remote_copy(
                src_ref=tile_ref,
                dst_ref=slots.at[1 + a, 1 + b],
                send_sem=send_sems.at[1 + a, 1 + b],
                recv_sem=recv_sems.at[1 + a, 1 + b],
                device_id=(req, row + a, col + b),
                device_id_type=MESH_IDS,
            ).wait_recv()
            out_ref[1 + a, 1 + b] = slots[1 + a, 1 + b]

        @pl.when(jnp.logical_not(present(a, b)))
        def _():
            out_ref[1 + a, 1 + b] = jnp.zeros(out_ref.shape[2:], out_ref.dtype)
    out_ref[1, 1] = tile_ref[...]


def halo_extend(tile):
    gathered = pl.pallas_call(
        halo_kernel,
        out_shape=jax.ShapeDtypeStruct((3, 3) + tile.shape, tile.dtype),
        in_specs=[pl.BlockSpec(memory_space=pltpu.VMEM)],
        out_specs=pl.BlockSpec(memory_space=pltpu.VMEM),
        scratch_shapes=[
            pltpu.VMEM((3, 3) + tile.shape, tile.dtype),
            pltpu.SemaphoreType.DMA((3, 3)),
            pltpu.SemaphoreType.DMA((3, 3)),
        ],
        compiler_params=pltpu.CompilerParams(collective_id=6, has_side_effects=True),
    )(tile)
    bands = []
    for a, pick_rows in ((0, slice(-1, None)), (1, slice(None)), (2, slice(0, 1))):
        pieces = [
            gathered[a, 0][:, pick_rows, -1:],
            gathered[a, 1][:, pick_rows, :],
            gathered[a, 2][:, pick_rows, :1],
        ]
        bands.append(jnp.concatenate(pieces, axis=2))
    return jnp.concatenate(bands, axis=1)


def layer_norm(tensor, epsilon):
    average = jnp.mean(tensor, axis=-1, keepdims=True)
    centered = tensor - average
    spread = jnp.mean(centered * centered, axis=-1, keepdims=True)
    return centered * lax.rsqrt(spread + epsilon)


def modulate(tensor, offset, factor):
    return (layer_norm(tensor, 1e-05) * (1.0 + factor) + offset).astype(jnp.bfloat16)


def head_norm(tensor, scaling):
    return (layer_norm(tensor, 1e-06) * scaling).astype(jnp.bfloat16)


def pick_entry(entries, position):
    slot_ids = jnp.arange(entries.shape[0], dtype=jnp.int32)
    return jnp.sum(jnp.where(slot_ids == position, entries, jnp.zeros_like(entries)))


def solver_weights(step_index):
    plan = jnp.linspace(0.00085**0.5, 0.012**0.5, TRAIN_STEPS, dtype=jnp.float32) ** 2
    cumulative = jnp.cumprod(1.0 - plan)
    alpha_now = pick_entry(cumulative, step_index)
    alpha_prev = pick_entry(cumulative, step_index - STRIDE)
    root_now = jnp.sqrt(alpha_now)
    rest_now = jnp.sqrt(1.0 - alpha_now)
    root_prev = jnp.sqrt(alpha_prev)
    rest_prev = jnp.sqrt(1.0 - alpha_prev)
    return (
        root_prev * root_now + rest_prev * rest_now,
        rest_prev * root_now - root_prev * rest_now,
    )


def key_mask(count, owners, grid, text_len, span, block_tokens, tile, text_rows):
    positions = jnp.arange(count, dtype=jnp.int32)
    owner_row = positions // span
    within = positions % span
    is_video = within < block_tokens
    owner_col = within // tile
    local_ids = within % tile
    token_row = owner_row * TR + local_ids // TC % TR
    token_col = owner_col * TC + local_ids % TC
    text_index = owner_row * text_rows + within - block_tokens
    matches = jnp.arange(grid.shape[0], dtype=jnp.int32)[None, :] == owners[:, None]
    rows_live = jnp.sum(jnp.where(matches, grid[None, :, 0], 0), axis=1)
    cols_live = jnp.sum(jnp.where(matches, grid[None, :, 1], 0), axis=1)
    text_lens = jnp.sum(jnp.where(matches, text_len[None, :], 0), axis=1)
    video_live = (token_row[None, :] < rows_live[:, None]) & (
        token_col[None, :] < cols_live[:, None]
    )
    text_live = (text_index[None, :] < text_lens[:, None]) & (within < block_tokens + text_rows)[None, :]
    return jnp.where(is_video[None, :], video_live, text_live).astype(jnp.float32)


def projector(stacked, piece):
    return jnp.einsum("gld,cde->cgle", stacked, piece, preferred_element_type=jnp.float32)


def attention_step(queries, owners, grid, text_len, span, block_tokens, tile, text_rows):
    score_scale = queries.shape[3] ** (-0.5)

    def attend(carry, pieces, start):
        key_piece, value_piece = pieces
        live_keys = key_mask(
            key_piece.shape[1], owners, grid, text_len, span, block_tokens, tile, text_rows
        )
        scores = (
            jnp.einsum("gqhd,gkhd->gqhk", queries, key_piece, preferred_element_type=jnp.float32)
            * score_scale
        )
        raw_weights = jnp.exp(scores) * live_keys[:, None, None, :]
        weighted = jnp.einsum(
            "gqhk,gkhd->gqhd",
            raw_weights.astype(jnp.bfloat16),
            value_piece,
            preferred_element_type=jnp.float32,
        )
        return (weighted, jnp.sum(raw_weights, axis=3))

    return attend


def shards(
    hidden,
    text_hidden,
    text_len,
    grid,
    timestep,
    modulation,
    q_gain,
    k_gain,
    w_qkv,
    w_out,
    w_up,
    w_down,
    w_proj,
    latent,
    conv_w,
):
    col_count = lax.axis_size("col")
    request_id = lax.axis_index("req")
    row_id = lax.axis_index("row")
    col_id = lax.axis_index("col")
    block_tokens = hidden.shape[1]
    tile = block_tokens // col_count
    text_rows = text_hidden.shape[1]
    head_dim = q_gain.shape[0]
    adaptive = modulation[0]
    source = hidden[0].astype(jnp.float32)
    joined = jnp.concatenate(
        [
            modulate(source, adaptive[0], adaptive[1]),
            modulate(text_hidden[0].astype(jnp.float32), adaptive[0], adaptive[1]),
        ],
        axis=0,
    )
    span = joined.shape[0]
    stacked = joined[None]
    owners = jnp.reshape(request_id, (1,))
    half_cols = w_qkv.shape[2] // 2
    own_half = lax.dynamic_slice_in_dim(w_qkv, request_id * half_cols, half_cols, 2)
    gathered_half = lax.all_gather(own_half, "row", axis=1, tiled=True)
    half_heads = half_cols // head_dim

    both_rows = jnp.concatenate([joined, partner_swap(joined, 4)], axis=0)
    projected_rows = jnp.einsum(
        "ld,cde->cle", both_rows, gathered_half, preferred_element_type=jnp.float32
    ).reshape(3, 2 * span, half_heads, head_dim)
    normed_q = head_norm(projected_rows[0], q_gain)
    normed_k = head_norm(projected_rows[1], k_gain)
    plain_v = projected_rows[2].astype(jnp.bfloat16)
    mine = jnp.stack([normed_q[:span], normed_k[:span], plain_v[:span]])
    theirs = jnp.stack([normed_q[span:], normed_k[span:], plain_v[span:]])
    received = partner_swap(theirs.reshape(3 * span, half_cols), 5).reshape(theirs.shape)
    full = jnp.concatenate(
        [jnp.where(request_id == 0, mine, received), jnp.where(request_id == 0, received, mine)], axis=2
    )
    groups = 1
    heads_here = full.shape[2]
    queries = full[0, :block_tokens][None]
    key_block = full[1][None]
    value_block = full[2][None]
    attend = attention_step(queries, owners, grid, text_len, span, block_tokens, tile, text_rows)
    empty_state = (jnp.zeros(queries.shape, jnp.float32), jnp.zeros(queries.shape[:3], jnp.float32))
    padded_span = 16 * pl.cdiv(span, 16)
    both = jnp.stack([key_block[0], value_block[0]], axis=0).reshape(2, span, heads_here * head_dim)
    both = jnp.pad(both, ((0, 0), (0, padded_span - span), (0, 0)))[None]
    gathered = lax.all_gather(both, "row", axis=0, tiled=True)
    live = key_mask(
        gathered.shape[0] * padded_span, owners, grid, text_len, padded_span, block_tokens, tile, text_rows
    )
    attended = attention(
        queries[0].reshape(block_tokens, heads_here * head_dim),
        gathered,
        live,
        head_dim ** (-0.5),
    )
    partial_out = jnp.dot(attended, w_out, preferred_element_type=jnp.float32)
    projected = scatter_sum(partial_out, "col", 1)
    own_rows = lax.dynamic_slice_in_dim(source, col_id * tile, tile, 0)
    mixed = lax.optimization_barrier(
        (own_rows + adaptive[2] * projected).astype(jnp.bfloat16)
    ).astype(jnp.float32)
    second_norm = modulate(mixed, adaptive[3], adaptive[4])
    hidden_units = jax.nn.gelu(
        jnp.dot(
            ring_gather(second_norm, 4, 8, 2).reshape(-1, second_norm.shape[1]),
            w_up,
            preferred_element_type=jnp.float32,
        ),
        approximate=True,
    ).astype(jnp.bfloat16)
    feed_terms = jnp.dot(hidden_units, w_down, preferred_element_type=jnp.float32)
    feed_out = ring_scatter_sum(feed_terms.astype(jnp.bfloat16), 4, 8, 0)
    out_hidden = (mixed + adaptive[5] * feed_out).astype(jnp.bfloat16)
    final_norm = modulate(out_hidden.astype(jnp.float32), adaptive[6], adaptive[7])
    velocity = jnp.dot(final_norm, w_proj, preferred_element_type=jnp.float32)
    local_ids = jnp.arange(tile, dtype=jnp.int32)
    token_row = row_id * TR + local_ids // TC % TR
    token_col = col_id * TC + local_ids % TC
    rows_live = pick_entry(grid[:, 0], request_id)
    cols_live = pick_entry(grid[:, 1], request_id)
    live_tokens = ((token_row < rows_live) & (token_col < cols_live)).astype(jnp.float32)
    keep_part, velocity_part = solver_weights(pick_entry(timestep, request_id))
    updated = (keep_part * latent[0] + velocity_part * velocity) * live_tokens[:, None]
    pixels = (
        updated.reshape(FR, TR, TC, CH, 2, 2)
        .transpose(0, 1, 4, 2, 5, 3)
        .reshape(FR, 2 * TR, 2 * TC, CH)
    )
    scaled = (pixels / latent_scale).astype(jnp.bfloat16)
    padded = halo_extend(scaled)
    running = jnp.zeros((FR, 2 * TR, 2 * TC, conv_w.shape[3]), jnp.float32)
    for row_tap in range(3):
        for col_tap in range(3):
            window = padded[:, row_tap : row_tap + 2 * TR, col_tap : col_tap + 2 * TC, :]
            running = running + jnp.einsum(
                "fyxc,cd->fyxd",
                window,
                conv_w[row_tap, col_tap],
                preferred_element_type=jnp.float32,
            )
    return (out_hidden[None], updated[None], running.astype(jnp.bfloat16)[None])


def solution(mesh):
    placed = (
        P("req", "row", None),
        P("req", "row", None),
        P(),
        P(),
        P(),
        P("req", None, None),
        P(),
        P(),
        P(None, "row", "col"),
        P("col", None),
        P(None, "row"),
        P("row", None),
        P(),
        P("req", ("row", "col"), None),
        P(),
    )
    return jax.shard_map(
        shards,
        mesh=mesh,
        in_specs=placed,
        out_specs=(
            P("req", ("row", "col"), None),
            P("req", ("row", "col"), None),
            P("req", None, "row", "col", None),
        ),
        check_vma=False,
    )
```

```python
import functools

import jax
import jax.numpy as jnp
from jax import lax
from jax.sharding import PartitionSpec as P
from jax.experimental import pallas as pl
from jax.experimental.pallas import tpu as pltpu

MESH_IDS = pl.DeviceIdType.MESH

CH = 16
FR = 6
TR = 1
TC = 4
TRAIN_STEPS = 1000
STRIDE = 250


latent_scale = 0.7


def extended(cells, sides, width):
    for axis, dim in sides:
        count = lax.axis_size(axis)
        ends = count - 1
        head = lax.slice_in_dim(cells, 0, width, axis=dim)
        tail = lax.slice_in_dim(cells, cells.shape[dim] - width, cells.shape[dim], axis=dim)
        cells = jnp.concatenate(
            [
                lax.ppermute(tail, axis, [(i, (i + 1) % count) for i in range(ends)]),
                cells,
                lax.ppermute(head, axis, [((i + 1) % count, i) for i in range(ends)]),
            ],
            axis=dim,
        )
    return cells


def peer_on(axis, peer):
    return tuple(peer if name == axis else lax.axis_index(name) for name in ("req", "row", "col"))


def scatter_sum_kernel(axis, count, rows, part_ref, out_ref, landed, send_sems, recv_sems, own_sem):
    me = lax.axis_index(axis)
    barrier = pltpu.get_barrier_semaphore()
    for step in range(1, count):
        peer = lax.rem(me + step, count)
        pl.semaphore_signal(barrier, inc=1, device_id=peer_on(axis, peer), device_id_type=MESH_IDS)
    pl.semaphore_wait(barrier, count - 1)
    own = pltpu.make_async_copy(part_ref.at[pl.ds(me * rows, rows)], landed.at[me], own_sem)
    own.start()
    sends = []
    for step in range(1, count):
        peer = lax.rem(me + step, count)
        copy = pltpu.make_async_remote_copy(
            src_ref=part_ref.at[pl.ds(peer * rows, rows)],
            dst_ref=landed.at[me],
            send_sem=send_sems.at[step],
            recv_sem=recv_sems.at[step],
            device_id=peer_on(axis, peer),
            device_id_type=MESH_IDS,
        )
        copy.start()
        sends.append(copy)
    own.wait()
    for step in range(1, count):
        source = lax.rem(me + count - step, count)
        pltpu.make_async_remote_copy(
            src_ref=part_ref.at[pl.ds(me * rows, rows)],
            dst_ref=landed.at[source],
            send_sem=send_sems.at[step],
            recv_sem=recv_sems.at[step],
            device_id=peer_on(axis, source),
            device_id_type=MESH_IDS,
        ).wait_recv()
    for copy in sends:
        copy.wait_send()
    total = landed[0].astype(jnp.float32)
    for slot in range(1, count):
        total = total + landed[slot].astype(jnp.float32)
    out_ref[...] = total


def scatter_sum(part, axis, kernel_id):
    count = lax.axis_size(axis)
    rows = part.shape[0] // count
    width = part.shape[1]
    return pl.pallas_call(
        functools.partial(scatter_sum_kernel, axis, count, rows),
        out_shape=jax.ShapeDtypeStruct((rows, width), jnp.float32),
        in_specs=[pl.BlockSpec(memory_space=pl.ANY)],
        out_specs=pl.BlockSpec(memory_space=pltpu.VMEM),
        scratch_shapes=[
            pltpu.VMEM((count, rows, width), part.dtype),
            pltpu.SemaphoreType.DMA((count,)),
            pltpu.SemaphoreType.DMA((count,)),
            pltpu.SemaphoreType.DMA(()),
        ],
        compiler_params=pltpu.CompilerParams(
            collective_id=kernel_id, has_side_effects=True, vmem_limit_bytes=48 * 1024 * 1024
        ),
    )(part)


def attention_kernel(scale, q_ref, kv_ref, live_ref, out_ref):
    sources, _, block, width = kv_ref.shape
    lane = lax.broadcasted_iota(jnp.int32, (1, 128), 1)
    first = lane < 64
    live = live_ref[...]
    for pair in range(width // 128):
        cols = slice(pair * 128, (pair + 1) * 128)
        query = q_ref[:, cols]
        keys = kv_ref[:, 0, :, cols].reshape(sources * block, 128)
        values = kv_ref[:, 1, :, cols].reshape(sources * block, 128)
        results = []
        for half in (first, jnp.logical_not(first)):
            picked = jnp.where(half, query, jnp.zeros_like(query))
            scores = lax.dot_general(
                picked, keys, (((1,), (1,)), ((), ())), preferred_element_type=jnp.float32
            ) * scale
            weights = jnp.exp(scores) * live
            totals = jnp.sum(weights, axis=1, keepdims=True)
            summed = jnp.dot(weights.astype(jnp.bfloat16), values, preferred_element_type=jnp.float32)
            results.append(summed / totals)
        out_ref[:, cols] = jnp.where(first, results[0], results[1]).astype(out_ref.dtype)


def attention(queries, gathered, live, scale):
    return pl.pallas_call(
        functools.partial(attention_kernel, scale),
        out_shape=jax.ShapeDtypeStruct(queries.shape, jnp.bfloat16),
        in_specs=[pl.BlockSpec(memory_space=pltpu.VMEM)] * 3,
        out_specs=pl.BlockSpec(memory_space=pltpu.VMEM),
        compiler_params=pltpu.CompilerParams(vmem_limit_bytes=56 * 1024 * 1024),
    )(queries, gathered, live)


def ring_scatter_kernel(zs, xs, part_ref, out_ref, landed, outgoing, own_sum, crossed, ring_send, ring_recv, cross_send, cross_recv):
    me = lax.axis_index("row")
    xm = me // zs
    zm = me % zs
    ahead = xm * zs + lax.rem(zm + 1, zs)
    behind = xm * zs + lax.rem(zm + zs - 1, zs)
    half = part_ref.shape[3] // 2
    barrier = pltpu.get_barrier_semaphore()
    targets = [ahead, behind] + [lax.rem(xm + k, xs) * zs + zm for k in range(1, xs)]
    for peer in targets:
        pl.semaphore_signal(barrier, inc=1, device_id=peer_on("row", peer), device_id_type=MESH_IDS)
    pl.semaphore_wait(barrier, len(targets))
    ways = ((0, ahead, behind, -1), (1, behind, ahead, 1))
    pending = []
    for step in range(zs - 1):
        for way, dest, origin, sign in ways:
            cols = pl.ds(way * half, half)
            chunk = lax.rem(zm + sign * (1 + step) + 2 * zs, zs)
            if step == 0:
                source = part_ref.at[chunk, :, :, cols]
            else:
                arrived = pltpu.make_async_remote_copy(
                    src_ref=outgoing.at[way, step - 1],
                    dst_ref=landed.at[way, step - 1],
                    send_sem=ring_send.at[way, step - 1],
                    recv_sem=ring_recv.at[way, step - 1],
                    device_id=peer_on("row", origin),
                    device_id_type=MESH_IDS,
                )
                arrived.wait_recv()
                outgoing[way, step] = (
                    landed[way, step - 1].astype(jnp.float32)
                    + part_ref[chunk, :, :, cols].astype(jnp.float32)
                ).astype(outgoing.dtype)
                source = outgoing.at[way, step]
            copy = pltpu.make_async_remote_copy(
                src_ref=source,
                dst_ref=landed.at[way, step],
                send_sem=ring_send.at[way, step],
                recv_sem=ring_recv.at[way, step],
                device_id=peer_on("row", dest),
                device_id_type=MESH_IDS,
            )
            copy.start()
            pending.append(copy)
    last = zs - 2
    for way, dest, origin, sign in ways:
        cols = pl.ds(way * half, half)
        pltpu.make_async_remote_copy(
            src_ref=outgoing.at[way, last],
            dst_ref=landed.at[way, last],
            send_sem=ring_send.at[way, last],
            recv_sem=ring_recv.at[way, last],
            device_id=peer_on("row", origin),
            device_id_type=MESH_IDS,
        ).wait_recv()
        own_sum[:, :, cols] = landed[way, last].astype(jnp.float32) + part_ref[zm, :, :, cols].astype(jnp.float32)
    crossed[0] = own_sum[...].astype(crossed.dtype)
    sends = []
    for k in range(1, xs):
        peer_x = lax.rem(xm + k, xs)
        copy = pltpu.make_async_remote_copy(
            src_ref=crossed.at[0, peer_x],
            dst_ref=crossed.at[k, 0],
            send_sem=cross_send.at[k],
            recv_sem=cross_recv.at[k],
            device_id=peer_on("row", peer_x * zs + zm),
            device_id_type=MESH_IDS,
        )
        copy.start()
        sends.append(copy)
    total = own_sum[xm]
    for k in range(1, xs):
        origin_x = lax.rem(xm + xs - k, xs)
        pltpu.make_async_remote_copy(
            src_ref=crossed.at[0, 0],
            dst_ref=crossed.at[k, 0],
            send_sem=cross_send.at[k],
            recv_sem=cross_recv.at[k],
            device_id=peer_on("row", origin_x * zs + zm),
            device_id_type=MESH_IDS,
        ).wait_recv()
        total = total + crossed[k, 0].astype(jnp.float32)
    out_ref[...] = total
    for copy in pending + sends:
        copy.wait_send()


def ring_scatter_sum(part, xs, zs, kernel_id):
    rows = part.shape[0] // (xs * zs)
    width = part.shape[1]
    arranged = part.reshape(zs, xs, rows, width)
    return pl.pallas_call(
        functools.partial(ring_scatter_kernel, zs, xs),
        out_shape=jax.ShapeDtypeStruct((rows, width), jnp.float32),
        in_specs=[pl.BlockSpec(memory_space=pltpu.VMEM)],
        out_specs=pl.BlockSpec(memory_space=pltpu.VMEM),
        scratch_shapes=[
            pltpu.VMEM((2, zs - 1, xs, rows, width // 2), part.dtype),
            pltpu.VMEM((2, zs - 1, xs, rows, width // 2), part.dtype),
            pltpu.VMEM((xs, rows, width), jnp.float32),
            pltpu.VMEM((xs, xs, rows, width), part.dtype),
            pltpu.SemaphoreType.DMA((2, zs - 1)),
            pltpu.SemaphoreType.DMA((2, zs - 1)),
            pltpu.SemaphoreType.DMA((xs,)),
            pltpu.SemaphoreType.DMA((xs,)),
        ],
        compiler_params=pltpu.CompilerParams(
            collective_id=kernel_id, has_side_effects=True, vmem_limit_bytes=56 * 1024 * 1024
        ),
    )(arranged)


def ring_gather_kernel(zs, xs, block_ref, out_ref, held, own_sem, ring_send, ring_recv, cross_send, cross_recv):
    me = lax.axis_index("row")
    xm = me // zs
    zm = me % zs
    ahead = xm * zs + lax.rem(zm + 1, zs)
    behind = xm * zs + lax.rem(zm + zs - 1, zs)
    barrier = pltpu.get_barrier_semaphore()
    targets = [ahead, behind] + [lax.rem(xm + k, xs) * zs + zm for k in range(1, xs)]
    for peer in targets:
        pl.semaphore_signal(barrier, inc=1, device_id=peer_on("row", peer), device_id_type=MESH_IDS)
    pl.semaphore_wait(barrier, len(targets))
    own = pltpu.make_async_copy(block_ref, held.at[zm, xm], own_sem)
    own.start()
    pending = []
    for k in range(1, xs):
        peer_x = lax.rem(xm + k, xs)
        copy = pltpu.make_async_remote_copy(
            src_ref=block_ref,
            dst_ref=held.at[zm, xm],
            send_sem=cross_send.at[k],
            recv_sem=cross_recv.at[k],
            device_id=peer_on("row", peer_x * zs + zm),
            device_id_type=MESH_IDS,
        )
        copy.start()
        pending.append(copy)
    own.wait()
    for k in range(1, xs):
        origin_x = lax.rem(xm + xs - k, xs)
        pltpu.make_async_remote_copy(
            src_ref=block_ref,
            dst_ref=held.at[zm, origin_x],
            send_sem=cross_send.at[k],
            recv_sem=cross_recv.at[k],
            device_id=peer_on("row", origin_x * zs + zm),
            device_id_type=MESH_IDS,
        ).wait_recv()
    split = xs // 2
    ways = ((0, ahead, behind, -1, pl.ds(0, split)), (1, behind, ahead, 1, pl.ds(split, xs - split)))
    for step in range(zs):
        for way, dest, origin, sign, part in ways:
            group = lax.rem(zm + sign * step + zs, zs)
            if step > 0:
                pltpu.make_async_remote_copy(
                    src_ref=held.at[group, part],
                    dst_ref=held.at[group, part],
                    send_sem=ring_send.at[way, step - 1],
                    recv_sem=ring_recv.at[way, step - 1],
                    device_id=peer_on("row", origin),
                    device_id_type=MESH_IDS,
                ).wait_recv()
            if step < zs - 1:
                copy = pltpu.make_async_remote_copy(
                    src_ref=held.at[group, part],
                    dst_ref=held.at[group, part],
                    send_sem=ring_send.at[way, step],
                    recv_sem=ring_recv.at[way, step],
                    device_id=peer_on("row", dest),
                    device_id_type=MESH_IDS,
                )
                copy.start()
                pending.append(copy)
    for copy in pending:
        copy.wait_send()
    out = pltpu.make_async_copy(held, out_ref, own_sem)
    out.start()
    out.wait()


def ring_gather(block, xs, zs, kernel_id):
    return pl.pallas_call(
        functools.partial(ring_gather_kernel, zs, xs),
        out_shape=jax.ShapeDtypeStruct((zs, xs) + block.shape, block.dtype),
        in_specs=[pl.BlockSpec(memory_space=pltpu.VMEM)],
        out_specs=pl.BlockSpec(memory_space=pl.ANY),
        scratch_shapes=[
            pltpu.VMEM((zs, xs) + block.shape, block.dtype),
            pltpu.SemaphoreType.DMA(()),
            pltpu.SemaphoreType.DMA((2, zs - 1)),
            pltpu.SemaphoreType.DMA((2, zs - 1)),
            pltpu.SemaphoreType.DMA((xs,)),
            pltpu.SemaphoreType.DMA((xs,)),
        ],
        compiler_params=pltpu.CompilerParams(
            collective_id=kernel_id, has_side_effects=True, vmem_limit_bytes=56 * 1024 * 1024
        ),
    )(block)


def swap_kernel(src_ref, out_ref, landed, sems):
    other = 1 - lax.axis_index("req")
    barrier = pltpu.get_barrier_semaphore()
    pl.semaphore_signal(barrier, inc=1, device_id=peer_on("req", other), device_id_type=MESH_IDS)
    pl.semaphore_wait(barrier, 1)
    copy = pltpu.make_async_remote_copy(
        src_ref=src_ref,
        dst_ref=landed,
        send_sem=sems.at[0],
        recv_sem=sems.at[1],
        device_id=peer_on("req", other),
        device_id_type=MESH_IDS,
    )
    copy.start()
    copy.wait_send()
    copy.wait_recv()
    out_ref[...] = landed[...]


def partner_swap(value, kernel_id):
    return pl.pallas_call(
        swap_kernel,
        out_shape=jax.ShapeDtypeStruct(value.shape, value.dtype),
        in_specs=[pl.BlockSpec(memory_space=pltpu.VMEM)],
        out_specs=pl.BlockSpec(memory_space=pltpu.VMEM),
        scratch_shapes=[pltpu.VMEM(value.shape, value.dtype), pltpu.SemaphoreType.DMA((2,))],
        compiler_params=pltpu.CompilerParams(collective_id=kernel_id, has_side_effects=True),
    )(value)


def halo_kernel(tile_ref, out_ref, slots, send_sems, recv_sems):
    req = lax.axis_index("req")
    row = lax.axis_index("row")
    col = lax.axis_index("col")
    rows = lax.axis_size("row")
    cols = lax.axis_size("col")
    offsets = [(a, b) for a in (-1, 0, 1) for b in (-1, 0, 1) if (a, b) != (0, 0)]

    def present(a, b):
        return (row + a >= 0) & (row + a < rows) & (col + b >= 0) & (col + b < cols)

    def link(a, b):
        return pltpu.make_async_remote_copy(
            src_ref=tile_ref,
            dst_ref=slots.at[1 - a, 1 - b],
            send_sem=send_sems.at[1 + a, 1 + b],
            recv_sem=recv_sems.at[1 - a, 1 - b],
            device_id=(req, row + a, col + b),
            device_id_type=MESH_IDS,
        )

    barrier = pltpu.get_barrier_semaphore()
    for a, b in offsets:
        @pl.when(present(a, b))
        def _():
            pl.semaphore_signal(barrier, inc=1, device_id=(req, row + a, col + b), device_id_type=MESH_IDS)
    up = (row + rows - 1) // rows
    down = (2 * rows - 2 - row) // rows
    left = (col + cols - 1) // cols
    right = (2 * cols - 2 - col) // cols
    pl.semaphore_wait(barrier, (1 + up + down) * (1 + left + right) - 1)
    for a, b in offsets:
        @pl.when(present(a, b))
        def _():
            link(a, b).start()
    for a, b in offsets:
        @pl.when(present(a, b))
        def _():
            copy = link(a, b)
            copy.wait_send()
            pltpu.make_async_remote_copy(
                src_ref=tile_ref,
                dst_ref=slots.at[1 + a, 1 + b],
                send_sem=send_sems.at[1 + a, 1 + b],
                recv_sem=recv_sems.at[1 + a, 1 + b],
                device_id=(req, row + a, col + b),
                device_id_type=MESH_IDS,
            ).wait_recv()
            out_ref[1 + a, 1 + b] = slots[1 + a, 1 + b]

        @pl.when(jnp.logical_not(present(a, b)))
        def _():
            out_ref[1 + a, 1 + b] = jnp.zeros(out_ref.shape[2:], out_ref.dtype)
    out_ref[1, 1] = tile_ref[...]


def halo_extend(tile):
    gathered = pl.pallas_call(
        halo_kernel,
        out_shape=jax.ShapeDtypeStruct((3, 3) + tile.shape, tile.dtype),
        in_specs=[pl.BlockSpec(memory_space=pltpu.VMEM)],
        out_specs=pl.BlockSpec(memory_space=pltpu.VMEM),
        scratch_shapes=[
            pltpu.VMEM((3, 3) + tile.shape, tile.dtype),
            pltpu.SemaphoreType.DMA((3, 3)),
            pltpu.SemaphoreType.DMA((3, 3)),
        ],
        compiler_params=pltpu.CompilerParams(collective_id=6, has_side_effects=True),
    )(tile)
    bands = []
    for a, pick_rows in ((0, slice(-1, None)), (1, slice(None)), (2, slice(0, 1))):
        pieces = [
            gathered[a, 0][:, pick_rows, -1:],
            gathered[a, 1][:, pick_rows, :],
            gathered[a, 2][:, pick_rows, :1],
        ]
        bands.append(jnp.concatenate(pieces, axis=2))
    return jnp.concatenate(bands, axis=1)


def layer_norm(tensor, epsilon):
    average = jnp.mean(tensor, axis=-1, keepdims=True)
    centered = tensor - average
    spread = jnp.mean(centered * centered, axis=-1, keepdims=True)
    return centered * lax.rsqrt(spread + epsilon)


def modulate(tensor, offset, factor):
    return (layer_norm(tensor, 1e-05) * (1.0 + factor) + offset).astype(jnp.bfloat16)


def head_norm(tensor, scaling):
    return (layer_norm(tensor, 1e-06) * scaling).astype(jnp.bfloat16)


def pick_entry(entries, position):
    slot_ids = jnp.arange(entries.shape[0], dtype=jnp.int32)
    return jnp.sum(jnp.where(slot_ids == position, entries, jnp.zeros_like(entries)))


def solver_weights(step_index):
    plan = jnp.linspace(0.00085**0.5, 0.012**0.5, TRAIN_STEPS, dtype=jnp.float32) ** 2
    cumulative = jnp.cumprod(1.0 - plan)
    alpha_now = pick_entry(cumulative, step_index)
    alpha_prev = pick_entry(cumulative, step_index - STRIDE)
    root_now = jnp.sqrt(alpha_now)
    rest_now = jnp.sqrt(1.0 - alpha_now)
    root_prev = jnp.sqrt(alpha_prev)
    rest_prev = jnp.sqrt(1.0 - alpha_prev)
    return (
        root_prev * root_now + rest_prev * rest_now,
        rest_prev * root_now - root_prev * rest_now,
    )


def key_mask(count, owners, grid, text_len, span, block_tokens, tile, text_rows):
    positions = jnp.arange(count, dtype=jnp.int32)
    owner_row = positions // span
    within = positions % span
    is_video = within < block_tokens
    owner_col = within // tile
    local_ids = within % tile
    token_row = owner_row * TR + local_ids // TC % TR
    token_col = owner_col * TC + local_ids % TC
    text_index = owner_row * text_rows + within - block_tokens
    matches = jnp.arange(grid.shape[0], dtype=jnp.int32)[None, :] == owners[:, None]
    rows_live = jnp.sum(jnp.where(matches, grid[None, :, 0], 0), axis=1)
    cols_live = jnp.sum(jnp.where(matches, grid[None, :, 1], 0), axis=1)
    text_lens = jnp.sum(jnp.where(matches, text_len[None, :], 0), axis=1)
    video_live = (token_row[None, :] < rows_live[:, None]) & (
        token_col[None, :] < cols_live[:, None]
    )
    text_live = (text_index[None, :] < text_lens[:, None]) & (within < block_tokens + text_rows)[None, :]
    return jnp.where(is_video[None, :], video_live, text_live).astype(jnp.float32)


def projector(stacked, piece):
    return jnp.einsum("gld,cde->cgle", stacked, piece, preferred_element_type=jnp.float32)


def attention_step(queries, owners, grid, text_len, span, block_tokens, tile, text_rows):
    score_scale = queries.shape[3] ** (-0.5)

    def attend(carry, pieces, start):
        key_piece, value_piece = pieces
        live_keys = key_mask(
            key_piece.shape[1], owners, grid, text_len, span, block_tokens, tile, text_rows
        )
        scores = (
            jnp.einsum("gqhd,gkhd->gqhk", queries, key_piece, preferred_element_type=jnp.float32)
            * score_scale
        )
        raw_weights = jnp.exp(scores) * live_keys[:, None, None, :]
        weighted = jnp.einsum(
            "gqhk,gkhd->gqhd",
            raw_weights.astype(jnp.bfloat16),
            value_piece,
            preferred_element_type=jnp.float32,
        )
        return (weighted, jnp.sum(raw_weights, axis=3))

    return attend


def shards(
    hidden,
    text_hidden,
    text_len,
    grid,
    timestep,
    modulation,
    q_gain,
    k_gain,
    w_qkv,
    w_out,
    w_up,
    w_down,
    w_proj,
    latent,
    conv_w,
):
    col_count = lax.axis_size("col")
    request_id = lax.axis_index("req")
    row_id = lax.axis_index("row")
    col_id = lax.axis_index("col")
    block_tokens = hidden.shape[1]
    tile = block_tokens // col_count
    text_rows = text_hidden.shape[1]
    head_dim = q_gain.shape[0]
    adaptive = modulation[0]
    source = hidden[0].astype(jnp.float32)
    joined = jnp.concatenate(
        [
            modulate(source, adaptive[0], adaptive[1]),
            modulate(text_hidden[0].astype(jnp.float32), adaptive[0], adaptive[1]),
        ],
        axis=0,
    )
    span = joined.shape[0]
    stacked = joined[None]
    owners = jnp.reshape(request_id, (1,))
    half_cols = w_qkv.shape[2] // 2
    own_half = lax.dynamic_slice_in_dim(w_qkv, request_id * half_cols, half_cols, 2)
    gathered_half = lax.all_gather(own_half, "row", axis=1, tiled=True)
    half_heads = half_cols // head_dim

    both_rows = jnp.concatenate([joined, partner_swap(joined, 4)], axis=0)
    projected_rows = jnp.einsum(
        "ld,cde->cle", both_rows, gathered_half, preferred_element_type=jnp.float32
    ).reshape(3, 2 * span, half_heads, head_dim)
    normed_q = head_norm(projected_rows[0], q_gain)
    normed_k = head_norm(projected_rows[1], k_gain)
    plain_v = projected_rows[2].astype(jnp.bfloat16)
    mine = jnp.stack([normed_q[:span], normed_k[:span], plain_v[:span]])
    theirs = jnp.stack([normed_q[span:], normed_k[span:], plain_v[span:]])
    received = partner_swap(theirs.reshape(3 * span, half_cols), 5).reshape(theirs.shape)
    full = jnp.concatenate(
        [jnp.where(request_id == 0, mine, received), jnp.where(request_id == 0, received, mine)], axis=2
    )
    groups = 1
    heads_here = full.shape[2]
    queries = full[0, :block_tokens][None]
    key_block = full[1][None]
    value_block = full[2][None]
    attend = attention_step(queries, owners, grid, text_len, span, block_tokens, tile, text_rows)
    empty_state = (jnp.zeros(queries.shape, jnp.float32), jnp.zeros(queries.shape[:3], jnp.float32))
    padded_span = 16 * pl.cdiv(span, 16)
    both = jnp.stack([key_block[0], value_block[0]], axis=0).reshape(2, span, heads_here * head_dim)
    both = jnp.pad(both, ((0, 0), (0, padded_span - span), (0, 0)))[None]
    gathered = lax.all_gather(both, "row", axis=0, tiled=True)
    live = key_mask(
        gathered.shape[0] * padded_span, owners, grid, text_len, padded_span, block_tokens, tile, text_rows
    )
    attended = attention(
        queries[0].reshape(block_tokens, heads_here * head_dim),
        gathered,
        live,
        head_dim ** (-0.5),
    )
    partial_out = jnp.dot(attended, w_out, preferred_element_type=jnp.float32)
    projected = scatter_sum(partial_out.astype(jnp.bfloat16), "col", 1)
    own_rows = lax.dynamic_slice_in_dim(source, col_id * tile, tile, 0)
    mixed = lax.optimization_barrier(
        (own_rows + adaptive[2] * projected).astype(jnp.bfloat16)
    ).astype(jnp.float32)
    second_norm = modulate(mixed, adaptive[3], adaptive[4])
    hidden_units = jax.nn.gelu(
        jnp.dot(
            ring_gather(second_norm, 4, 8, 2).reshape(-1, second_norm.shape[1]),
            w_up,
            preferred_element_type=jnp.float32,
        ),
        approximate=True,
    ).astype(jnp.bfloat16)
    feed_terms = jnp.dot(hidden_units, w_down, preferred_element_type=jnp.float32)
    feed_out = ring_scatter_sum(feed_terms.astype(jnp.bfloat16), 4, 8, 0)
    out_hidden = (mixed + adaptive[5] * feed_out).astype(jnp.bfloat16)
    final_norm = modulate(out_hidden.astype(jnp.float32), adaptive[6], adaptive[7])
    velocity = jnp.dot(final_norm, w_proj, preferred_element_type=jnp.float32)
    local_ids = jnp.arange(tile, dtype=jnp.int32)
    token_row = row_id * TR + local_ids // TC % TR
    token_col = col_id * TC + local_ids % TC
    rows_live = pick_entry(grid[:, 0], request_id)
    cols_live = pick_entry(grid[:, 1], request_id)
    live_tokens = ((token_row < rows_live) & (token_col < cols_live)).astype(jnp.float32)
    keep_part, velocity_part = solver_weights(pick_entry(timestep, request_id))
    updated = (keep_part * latent[0] + velocity_part * velocity) * live_tokens[:, None]
    pixels = (
        updated.reshape(FR, TR, TC, CH, 2, 2)
        .transpose(0, 1, 4, 2, 5, 3)
        .reshape(FR, 2 * TR, 2 * TC, CH)
    )
    scaled = (pixels / latent_scale).astype(jnp.bfloat16)
    padded = halo_extend(scaled)
    running = jnp.zeros((FR, 2 * TR, 2 * TC, conv_w.shape[3]), jnp.float32)
    for row_tap in range(3):
        for col_tap in range(3):
            window = padded[:, row_tap : row_tap + 2 * TR, col_tap : col_tap + 2 * TC, :]
            running = running + jnp.einsum(
                "fyxc,cd->fyxd",
                window,
                conv_w[row_tap, col_tap],
                preferred_element_type=jnp.float32,
            )
    return (out_hidden[None], updated[None], running.astype(jnp.bfloat16)[None])


def solution(mesh):
    placed = (
        P("req", "row", None),
        P("req", "row", None),
        P(),
        P(),
        P(),
        P("req", None, None),
        P(),
        P(),
        P(None, "row", "col"),
        P("col", None),
        P(None, "row"),
        P("row", None),
        P(),
        P("req", ("row", "col"), None),
        P(),
    )
    return jax.shard_map(
        shards,
        mesh=mesh,
        in_specs=placed,
        out_specs=(
            P("req", ("row", "col"), None),
            P("req", ("row", "col"), None),
            P("req", None, "row", "col", None),
        ),
        check_vma=False,
    )
```

```python
import functools

import jax
import jax.numpy as jnp
from jax import lax
from jax.sharding import PartitionSpec as P
from jax.experimental import pallas as pl
from jax.experimental.pallas import tpu as pltpu

MESH_IDS = pl.DeviceIdType.MESH

CH = 16
FR = 6
TR = 1
TC = 4
TRAIN_STEPS = 1000
STRIDE = 250


latent_scale = 0.7


def extended(cells, sides, width):
    for axis, dim in sides:
        count = lax.axis_size(axis)
        ends = count - 1
        head = lax.slice_in_dim(cells, 0, width, axis=dim)
        tail = lax.slice_in_dim(cells, cells.shape[dim] - width, cells.shape[dim], axis=dim)
        cells = jnp.concatenate(
            [
                lax.ppermute(tail, axis, [(i, (i + 1) % count) for i in range(ends)]),
                cells,
                lax.ppermute(head, axis, [((i + 1) % count, i) for i in range(ends)]),
            ],
            axis=dim,
        )
    return cells


def peer_on(axis, peer):
    return tuple(peer if name == axis else lax.axis_index(name) for name in ("req", "row", "col"))


def scatter_sum_kernel(axis, count, rows, part_ref, out_ref, landed, send_sems, recv_sems, own_sem):
    me = lax.axis_index(axis)
    barrier = pltpu.get_barrier_semaphore()
    for step in range(1, count):
        peer = lax.rem(me + step, count)
        pl.semaphore_signal(barrier, inc=1, device_id=peer_on(axis, peer), device_id_type=MESH_IDS)
    pl.semaphore_wait(barrier, count - 1)
    own = pltpu.make_async_copy(part_ref.at[pl.ds(me * rows, rows)], landed.at[me], own_sem)
    own.start()
    sends = []
    for step in range(1, count):
        peer = lax.rem(me + step, count)
        copy = pltpu.make_async_remote_copy(
            src_ref=part_ref.at[pl.ds(peer * rows, rows)],
            dst_ref=landed.at[me],
            send_sem=send_sems.at[step],
            recv_sem=recv_sems.at[step],
            device_id=peer_on(axis, peer),
            device_id_type=MESH_IDS,
        )
        copy.start()
        sends.append(copy)
    own.wait()
    for step in range(1, count):
        source = lax.rem(me + count - step, count)
        pltpu.make_async_remote_copy(
            src_ref=part_ref.at[pl.ds(me * rows, rows)],
            dst_ref=landed.at[source],
            send_sem=send_sems.at[step],
            recv_sem=recv_sems.at[step],
            device_id=peer_on(axis, source),
            device_id_type=MESH_IDS,
        ).wait_recv()
    for copy in sends:
        copy.wait_send()
    total = landed[0].astype(jnp.float32)
    for slot in range(1, count):
        total = total + landed[slot].astype(jnp.float32)
    out_ref[...] = total


def scatter_sum(part, axis, kernel_id):
    count = lax.axis_size(axis)
    rows = part.shape[0] // count
    width = part.shape[1]
    return pl.pallas_call(
        functools.partial(scatter_sum_kernel, axis, count, rows),
        out_shape=jax.ShapeDtypeStruct((rows, width), jnp.float32),
        in_specs=[pl.BlockSpec(memory_space=pl.ANY)],
        out_specs=pl.BlockSpec(memory_space=pltpu.VMEM),
        scratch_shapes=[
            pltpu.VMEM((count, rows, width), part.dtype),
            pltpu.SemaphoreType.DMA((count,)),
            pltpu.SemaphoreType.DMA((count,)),
            pltpu.SemaphoreType.DMA(()),
        ],
        compiler_params=pltpu.CompilerParams(
            collective_id=kernel_id, has_side_effects=True, vmem_limit_bytes=48 * 1024 * 1024
        ),
    )(part)


def attention_kernel(scale, q_ref, kv_ref, live_ref, out_ref):
    sources, _, block, width = kv_ref.shape
    lane = lax.broadcasted_iota(jnp.int32, (1, 128), 1)
    first = lane < 64
    live = live_ref[...]
    for pair in range(width // 128):
        cols = slice(pair * 128, (pair + 1) * 128)
        query = q_ref[:, cols]
        keys = kv_ref[:, 0, :, cols].reshape(sources * block, 128)
        values = kv_ref[:, 1, :, cols].reshape(sources * block, 128)
        results = []
        for half in (first, jnp.logical_not(first)):
            picked = jnp.where(half, query, jnp.zeros_like(query))
            scores = lax.dot_general(
                picked, keys, (((1,), (1,)), ((), ())), preferred_element_type=jnp.float32
            ) * scale
            weights = jnp.exp(scores) * live
            totals = jnp.sum(weights, axis=1, keepdims=True)
            summed = jnp.dot(weights.astype(jnp.bfloat16), values, preferred_element_type=jnp.float32)
            results.append(summed / totals)
        out_ref[:, cols] = jnp.where(first, results[0], results[1]).astype(out_ref.dtype)


def attention(queries, gathered, live, scale):
    return pl.pallas_call(
        functools.partial(attention_kernel, scale),
        out_shape=jax.ShapeDtypeStruct(queries.shape, jnp.bfloat16),
        in_specs=[pl.BlockSpec(memory_space=pltpu.VMEM)] * 3,
        out_specs=pl.BlockSpec(memory_space=pltpu.VMEM),
        compiler_params=pltpu.CompilerParams(vmem_limit_bytes=56 * 1024 * 1024),
    )(queries, gathered, live)


def ring_scatter_kernel(zs, xs, part_ref, out_ref, landed, outgoing, own_sum, crossed, ring_send, ring_recv, cross_send, cross_recv):
    me = lax.axis_index("row")
    xm = me // zs
    zm = me % zs
    ahead = xm * zs + lax.rem(zm + 1, zs)
    behind = xm * zs + lax.rem(zm + zs - 1, zs)
    half = part_ref.shape[3] // 2
    barrier = pltpu.get_barrier_semaphore()
    targets = [ahead, behind] + [lax.rem(xm + k, xs) * zs + zm for k in range(1, xs)]
    for peer in targets:
        pl.semaphore_signal(barrier, inc=1, device_id=peer_on("row", peer), device_id_type=MESH_IDS)
    pl.semaphore_wait(barrier, len(targets))
    ways = ((0, ahead, behind, -1), (1, behind, ahead, 1))
    pending = []
    for step in range(zs - 1):
        for way, dest, origin, sign in ways:
            cols = pl.ds(way * half, half)
            chunk = lax.rem(zm + sign * (1 + step) + 2 * zs, zs)
            if step == 0:
                source = part_ref.at[chunk, :, :, cols]
            else:
                arrived = pltpu.make_async_remote_copy(
                    src_ref=outgoing.at[way, step - 1],
                    dst_ref=landed.at[way, step - 1],
                    send_sem=ring_send.at[way, step - 1],
                    recv_sem=ring_recv.at[way, step - 1],
                    device_id=peer_on("row", origin),
                    device_id_type=MESH_IDS,
                )
                arrived.wait_recv()
                outgoing[way, step] = (
                    landed[way, step - 1].astype(jnp.float32)
                    + part_ref[chunk, :, :, cols].astype(jnp.float32)
                ).astype(outgoing.dtype)
                source = outgoing.at[way, step]
            copy = pltpu.make_async_remote_copy(
                src_ref=source,
                dst_ref=landed.at[way, step],
                send_sem=ring_send.at[way, step],
                recv_sem=ring_recv.at[way, step],
                device_id=peer_on("row", dest),
                device_id_type=MESH_IDS,
            )
            copy.start()
            pending.append(copy)
    last = zs - 2
    for way, dest, origin, sign in ways:
        cols = pl.ds(way * half, half)
        pltpu.make_async_remote_copy(
            src_ref=outgoing.at[way, last],
            dst_ref=landed.at[way, last],
            send_sem=ring_send.at[way, last],
            recv_sem=ring_recv.at[way, last],
            device_id=peer_on("row", origin),
            device_id_type=MESH_IDS,
        ).wait_recv()
        own_sum[:, :, cols] = landed[way, last].astype(jnp.float32) + part_ref[zm, :, :, cols].astype(jnp.float32)
    crossed[0] = own_sum[...].astype(crossed.dtype)
    sends = []
    for k in range(1, xs):
        peer_x = lax.rem(xm + k, xs)
        copy = pltpu.make_async_remote_copy(
            src_ref=crossed.at[0, peer_x],
            dst_ref=crossed.at[k, 0],
            send_sem=cross_send.at[k],
            recv_sem=cross_recv.at[k],
            device_id=peer_on("row", peer_x * zs + zm),
            device_id_type=MESH_IDS,
        )
        copy.start()
        sends.append(copy)
    total = own_sum[xm]
    for k in range(1, xs):
        origin_x = lax.rem(xm + xs - k, xs)
        pltpu.make_async_remote_copy(
            src_ref=crossed.at[0, 0],
            dst_ref=crossed.at[k, 0],
            send_sem=cross_send.at[k],
            recv_sem=cross_recv.at[k],
            device_id=peer_on("row", origin_x * zs + zm),
            device_id_type=MESH_IDS,
        ).wait_recv()
        total = total + crossed[k, 0].astype(jnp.float32)
    out_ref[...] = total
    for copy in pending + sends:
        copy.wait_send()


def ring_scatter_sum(part, xs, zs, kernel_id):
    rows = part.shape[0] // (xs * zs)
    width = part.shape[1]
    arranged = part.reshape(zs, xs, rows, width)
    return pl.pallas_call(
        functools.partial(ring_scatter_kernel, zs, xs),
        out_shape=jax.ShapeDtypeStruct((rows, width), jnp.float32),
        in_specs=[pl.BlockSpec(memory_space=pltpu.VMEM)],
        out_specs=pl.BlockSpec(memory_space=pltpu.VMEM),
        scratch_shapes=[
            pltpu.VMEM((2, zs - 1, xs, rows, width // 2), part.dtype),
            pltpu.VMEM((2, zs - 1, xs, rows, width // 2), part.dtype),
            pltpu.VMEM((xs, rows, width), jnp.float32),
            pltpu.VMEM((xs, xs, rows, width), part.dtype),
            pltpu.SemaphoreType.DMA((2, zs - 1)),
            pltpu.SemaphoreType.DMA((2, zs - 1)),
            pltpu.SemaphoreType.DMA((xs,)),
            pltpu.SemaphoreType.DMA((xs,)),
        ],
        compiler_params=pltpu.CompilerParams(
            collective_id=kernel_id, has_side_effects=True, vmem_limit_bytes=56 * 1024 * 1024
        ),
    )(arranged)


def ring_gather_kernel(zs, xs, block_ref, out_ref, held, own_sem, ring_send, ring_recv, cross_send, cross_recv):
    me = lax.axis_index("row")
    xm = me // zs
    zm = me % zs
    ahead = xm * zs + lax.rem(zm + 1, zs)
    behind = xm * zs + lax.rem(zm + zs - 1, zs)
    barrier = pltpu.get_barrier_semaphore()
    targets = [ahead, behind] + [lax.rem(xm + k, xs) * zs + zm for k in range(1, xs)]
    for peer in targets:
        pl.semaphore_signal(barrier, inc=1, device_id=peer_on("row", peer), device_id_type=MESH_IDS)
    pl.semaphore_wait(barrier, len(targets))
    own = pltpu.make_async_copy(block_ref, held.at[zm, xm], own_sem)
    own.start()
    pending = []
    for k in range(1, xs):
        peer_x = lax.rem(xm + k, xs)
        copy = pltpu.make_async_remote_copy(
            src_ref=block_ref,
            dst_ref=held.at[zm, xm],
            send_sem=cross_send.at[k],
            recv_sem=cross_recv.at[k],
            device_id=peer_on("row", peer_x * zs + zm),
            device_id_type=MESH_IDS,
        )
        copy.start()
        pending.append(copy)
    own.wait()
    for k in range(1, xs):
        origin_x = lax.rem(xm + xs - k, xs)
        pltpu.make_async_remote_copy(
            src_ref=block_ref,
            dst_ref=held.at[zm, origin_x],
            send_sem=cross_send.at[k],
            recv_sem=cross_recv.at[k],
            device_id=peer_on("row", origin_x * zs + zm),
            device_id_type=MESH_IDS,
        ).wait_recv()
    split = xs // 2
    ways = ((0, ahead, behind, -1, pl.ds(0, split)), (1, behind, ahead, 1, pl.ds(split, xs - split)))
    for step in range(zs):
        for way, dest, origin, sign, part in ways:
            group = lax.rem(zm + sign * step + zs, zs)
            if step > 0:
                pltpu.make_async_remote_copy(
                    src_ref=held.at[group, part],
                    dst_ref=held.at[group, part],
                    send_sem=ring_send.at[way, step - 1],
                    recv_sem=ring_recv.at[way, step - 1],
                    device_id=peer_on("row", origin),
                    device_id_type=MESH_IDS,
                ).wait_recv()
            if step < zs - 1:
                copy = pltpu.make_async_remote_copy(
                    src_ref=held.at[group, part],
                    dst_ref=held.at[group, part],
                    send_sem=ring_send.at[way, step],
                    recv_sem=ring_recv.at[way, step],
                    device_id=peer_on("row", dest),
                    device_id_type=MESH_IDS,
                )
                copy.start()
                pending.append(copy)
    for copy in pending:
        copy.wait_send()
    out = pltpu.make_async_copy(held, out_ref, own_sem)
    out.start()
    out.wait()


def ring_gather(block, xs, zs, kernel_id):
    return pl.pallas_call(
        functools.partial(ring_gather_kernel, zs, xs),
        out_shape=jax.ShapeDtypeStruct((zs, xs) + block.shape, block.dtype),
        in_specs=[pl.BlockSpec(memory_space=pltpu.VMEM)],
        out_specs=pl.BlockSpec(memory_space=pl.ANY),
        scratch_shapes=[
            pltpu.VMEM((zs, xs) + block.shape, block.dtype),
            pltpu.SemaphoreType.DMA(()),
            pltpu.SemaphoreType.DMA((2, zs - 1)),
            pltpu.SemaphoreType.DMA((2, zs - 1)),
            pltpu.SemaphoreType.DMA((xs,)),
            pltpu.SemaphoreType.DMA((xs,)),
        ],
        compiler_params=pltpu.CompilerParams(
            collective_id=kernel_id, has_side_effects=True, vmem_limit_bytes=56 * 1024 * 1024
        ),
    )(block)


def swap_kernel(src_ref, out_ref, landed, sems):
    other = 1 - lax.axis_index("req")
    barrier = pltpu.get_barrier_semaphore()
    pl.semaphore_signal(barrier, inc=1, device_id=peer_on("req", other), device_id_type=MESH_IDS)
    pl.semaphore_wait(barrier, 1)
    copy = pltpu.make_async_remote_copy(
        src_ref=src_ref,
        dst_ref=landed,
        send_sem=sems.at[0],
        recv_sem=sems.at[1],
        device_id=peer_on("req", other),
        device_id_type=MESH_IDS,
    )
    copy.start()
    copy.wait_send()
    copy.wait_recv()
    out_ref[...] = landed[...]


def partner_swap(value, kernel_id):
    return pl.pallas_call(
        swap_kernel,
        out_shape=jax.ShapeDtypeStruct(value.shape, value.dtype),
        in_specs=[pl.BlockSpec(memory_space=pltpu.VMEM)],
        out_specs=pl.BlockSpec(memory_space=pltpu.VMEM),
        scratch_shapes=[pltpu.VMEM(value.shape, value.dtype), pltpu.SemaphoreType.DMA((2,))],
        compiler_params=pltpu.CompilerParams(collective_id=kernel_id, has_side_effects=True),
    )(value)


def halo_kernel(tile_ref, out_ref, slots, send_sems, recv_sems):
    req = lax.axis_index("req")
    row = lax.axis_index("row")
    col = lax.axis_index("col")
    rows = lax.axis_size("row")
    cols = lax.axis_size("col")
    offsets = [(a, b) for a in (-1, 0, 1) for b in (-1, 0, 1) if (a, b) != (0, 0)]

    def present(a, b):
        return (row + a >= 0) & (row + a < rows) & (col + b >= 0) & (col + b < cols)

    def link(a, b):
        return pltpu.make_async_remote_copy(
            src_ref=tile_ref,
            dst_ref=slots.at[1 - a, 1 - b],
            send_sem=send_sems.at[1 + a, 1 + b],
            recv_sem=recv_sems.at[1 - a, 1 - b],
            device_id=(req, row + a, col + b),
            device_id_type=MESH_IDS,
        )

    barrier = pltpu.get_barrier_semaphore()
    for a, b in offsets:
        @pl.when(present(a, b))
        def _():
            pl.semaphore_signal(barrier, inc=1, device_id=(req, row + a, col + b), device_id_type=MESH_IDS)
    up = (row + rows - 1) // rows
    down = (2 * rows - 2 - row) // rows
    left = (col + cols - 1) // cols
    right = (2 * cols - 2 - col) // cols
    pl.semaphore_wait(barrier, (1 + up + down) * (1 + left + right) - 1)
    for a, b in offsets:
        @pl.when(present(a, b))
        def _():
            link(a, b).start()
    for a, b in offsets:
        @pl.when(present(a, b))
        def _():
            copy = link(a, b)
            copy.wait_send()
            pltpu.make_async_remote_copy(
                src_ref=tile_ref,
                dst_ref=slots.at[1 + a, 1 + b],
                send_sem=send_sems.at[1 + a, 1 + b],
                recv_sem=recv_sems.at[1 + a, 1 + b],
                device_id=(req, row + a, col + b),
                device_id_type=MESH_IDS,
            ).wait_recv()
            out_ref[1 + a, 1 + b] = slots[1 + a, 1 + b]

        @pl.when(jnp.logical_not(present(a, b)))
        def _():
            out_ref[1 + a, 1 + b] = jnp.zeros(out_ref.shape[2:], out_ref.dtype)
    out_ref[1, 1] = tile_ref[...]


def halo_extend(tile):
    gathered = pl.pallas_call(
        halo_kernel,
        out_shape=jax.ShapeDtypeStruct((3, 3) + tile.shape, tile.dtype),
        in_specs=[pl.BlockSpec(memory_space=pltpu.VMEM)],
        out_specs=pl.BlockSpec(memory_space=pltpu.VMEM),
        scratch_shapes=[
            pltpu.VMEM((3, 3) + tile.shape, tile.dtype),
            pltpu.SemaphoreType.DMA((3, 3)),
            pltpu.SemaphoreType.DMA((3, 3)),
        ],
        compiler_params=pltpu.CompilerParams(collective_id=6, has_side_effects=True),
    )(tile)
    bands = []
    for a, pick_rows in ((0, slice(-1, None)), (1, slice(None)), (2, slice(0, 1))):
        pieces = [
            gathered[a, 0][:, pick_rows, -1:],
            gathered[a, 1][:, pick_rows, :],
            gathered[a, 2][:, pick_rows, :1],
        ]
        bands.append(jnp.concatenate(pieces, axis=2))
    return jnp.concatenate(bands, axis=1)


def layer_norm(tensor, epsilon):
    average = jnp.mean(tensor, axis=-1, keepdims=True)
    centered = tensor - average
    spread = jnp.mean(centered * centered, axis=-1, keepdims=True)
    return centered * lax.rsqrt(spread + epsilon)


def modulate(tensor, offset, factor):
    return (layer_norm(tensor, 1e-05) * (1.0 + factor) + offset).astype(jnp.bfloat16)


def head_norm(tensor, scaling):
    return (layer_norm(tensor, 1e-06) * scaling).astype(jnp.bfloat16)


def pick_entry(entries, position):
    slot_ids = jnp.arange(entries.shape[0], dtype=jnp.int32)
    return jnp.sum(jnp.where(slot_ids == position, entries, jnp.zeros_like(entries)))


def solver_weights(step_index):
    plan = jnp.linspace(0.00085**0.5, 0.012**0.5, TRAIN_STEPS, dtype=jnp.float32) ** 2
    cumulative = jnp.cumprod(1.0 - plan)
    alpha_now = pick_entry(cumulative, step_index)
    alpha_prev = pick_entry(cumulative, step_index - STRIDE)
    root_now = jnp.sqrt(alpha_now)
    rest_now = jnp.sqrt(1.0 - alpha_now)
    root_prev = jnp.sqrt(alpha_prev)
    rest_prev = jnp.sqrt(1.0 - alpha_prev)
    return (
        root_prev * root_now + rest_prev * rest_now,
        rest_prev * root_now - root_prev * rest_now,
    )


def key_mask(count, owners, grid, text_len, span, block_tokens, tile, text_rows):
    positions = jnp.arange(count, dtype=jnp.int32)
    owner_row = positions // span
    within = positions % span
    is_video = within < block_tokens
    owner_col = within // tile
    local_ids = within % tile
    token_row = owner_row * TR + local_ids // TC % TR
    token_col = owner_col * TC + local_ids % TC
    text_index = owner_row * text_rows + within - block_tokens
    matches = jnp.arange(grid.shape[0], dtype=jnp.int32)[None, :] == owners[:, None]
    rows_live = jnp.sum(jnp.where(matches, grid[None, :, 0], 0), axis=1)
    cols_live = jnp.sum(jnp.where(matches, grid[None, :, 1], 0), axis=1)
    text_lens = jnp.sum(jnp.where(matches, text_len[None, :], 0), axis=1)
    video_live = (token_row[None, :] < rows_live[:, None]) & (
        token_col[None, :] < cols_live[:, None]
    )
    text_live = (text_index[None, :] < text_lens[:, None]) & (within < block_tokens + text_rows)[None, :]
    return jnp.where(is_video[None, :], video_live, text_live).astype(jnp.float32)


def projector(stacked, piece):
    return jnp.einsum("gld,cde->cgle", stacked, piece, preferred_element_type=jnp.float32)


def attention_step(queries, owners, grid, text_len, span, block_tokens, tile, text_rows):
    score_scale = queries.shape[3] ** (-0.5)

    def attend(carry, pieces, start):
        key_piece, value_piece = pieces
        live_keys = key_mask(
            key_piece.shape[1], owners, grid, text_len, span, block_tokens, tile, text_rows
        )
        scores = (
            jnp.einsum("gqhd,gkhd->gqhk", queries, key_piece, preferred_element_type=jnp.float32)
            * score_scale
        )
        raw_weights = jnp.exp(scores) * live_keys[:, None, None, :]
        weighted = jnp.einsum(
            "gqhk,gkhd->gqhd",
            raw_weights.astype(jnp.bfloat16),
            value_piece,
            preferred_element_type=jnp.float32,
        )
        return (weighted, jnp.sum(raw_weights, axis=3))

    return attend


def shards(
    hidden,
    text_hidden,
    text_len,
    grid,
    timestep,
    modulation,
    q_gain,
    k_gain,
    w_qkv,
    w_out,
    w_up,
    w_down,
    w_proj,
    latent,
    conv_w,
):
    col_count = lax.axis_size("col")
    request_id = lax.axis_index("req")
    row_id = lax.axis_index("row")
    col_id = lax.axis_index("col")
    block_tokens = hidden.shape[1]
    tile = block_tokens // col_count
    text_rows = text_hidden.shape[1]
    head_dim = q_gain.shape[0]
    adaptive = modulation[0]
    source = hidden[0].astype(jnp.float32)
    joined = jnp.concatenate(
        [
            modulate(source, adaptive[0], adaptive[1]),
            modulate(text_hidden[0].astype(jnp.float32), adaptive[0], adaptive[1]),
        ],
        axis=0,
    )
    span = joined.shape[0]
    stacked = joined[None]
    owners = jnp.reshape(request_id, (1,))
    half_cols = w_qkv.shape[2] // 2
    own_half = lax.dynamic_slice_in_dim(w_qkv, request_id * half_cols, half_cols, 2)
    gathered_half = lax.all_gather(own_half, "row", axis=1, tiled=True)
    half_heads = half_cols // head_dim

    both_rows = jnp.concatenate([joined, partner_swap(joined, 4)], axis=0)
    projected_rows = jnp.einsum("ld,cde->cle", both_rows, gathered_half, preferred_element_type=jnp.float32)
    own_raw = projected_rows[:, :span]
    received_raw = partner_swap(projected_rows[:, span:], 5)
    raw = jnp.concatenate(
        [jnp.where(request_id == 0, own_raw, received_raw), jnp.where(request_id == 0, received_raw, own_raw)], axis=2
    ).reshape(3, span, 2 * half_heads, head_dim)
    full = jnp.stack([head_norm(raw[0], q_gain), head_norm(raw[1], k_gain), raw[2].astype(jnp.bfloat16)])
    groups = 1
    heads_here = full.shape[2]
    queries = full[0, :block_tokens][None]
    key_block = full[1][None]
    value_block = full[2][None]
    attend = attention_step(queries, owners, grid, text_len, span, block_tokens, tile, text_rows)
    empty_state = (jnp.zeros(queries.shape, jnp.float32), jnp.zeros(queries.shape[:3], jnp.float32))
    padded_span = 16 * pl.cdiv(span, 16)
    both = jnp.stack([key_block[0], value_block[0]], axis=0).reshape(2, span, heads_here * head_dim)
    both = jnp.pad(both, ((0, 0), (0, padded_span - span), (0, 0)))[None]
    gathered = lax.all_gather(both, "row", axis=0, tiled=True)
    live = key_mask(
        gathered.shape[0] * padded_span, owners, grid, text_len, padded_span, block_tokens, tile, text_rows
    )
    attended = attention(
        queries[0].reshape(block_tokens, heads_here * head_dim),
        gathered,
        live,
        head_dim ** (-0.5),
    )
    partial_out = jnp.dot(attended, w_out, preferred_element_type=jnp.float32)
    projected = scatter_sum(partial_out.astype(jnp.bfloat16), "col", 1)
    own_rows = lax.dynamic_slice_in_dim(source, col_id * tile, tile, 0)
    mixed = lax.optimization_barrier(
        (own_rows + adaptive[2] * projected).astype(jnp.bfloat16)
    ).astype(jnp.float32)
    second_norm = modulate(mixed, adaptive[3], adaptive[4])
    hidden_units = jax.nn.gelu(
        jnp.dot(
            ring_gather(second_norm, 4, 8, 2).reshape(-1, second_norm.shape[1]),
            w_up,
            preferred_element_type=jnp.float32,
        ),
        approximate=True,
    ).astype(jnp.bfloat16)
    feed_terms = jnp.dot(hidden_units, w_down, preferred_element_type=jnp.float32)
    feed_out = ring_scatter_sum(feed_terms.astype(jnp.bfloat16), 4, 8, 0)
    out_hidden = (mixed + adaptive[5] * feed_out).astype(jnp.bfloat16)
    final_norm = modulate(out_hidden.astype(jnp.float32), adaptive[6], adaptive[7])
    velocity = jnp.dot(final_norm, w_proj, preferred_element_type=jnp.float32)
    local_ids = jnp.arange(tile, dtype=jnp.int32)
    token_row = row_id * TR + local_ids // TC % TR
    token_col = col_id * TC + local_ids % TC
    rows_live = pick_entry(grid[:, 0], request_id)
    cols_live = pick_entry(grid[:, 1], request_id)
    live_tokens = ((token_row < rows_live) & (token_col < cols_live)).astype(jnp.float32)
    keep_part, velocity_part = solver_weights(pick_entry(timestep, request_id))
    updated = (keep_part * latent[0] + velocity_part * velocity) * live_tokens[:, None]
    pixels = (
        updated.reshape(FR, TR, TC, CH, 2, 2)
        .transpose(0, 1, 4, 2, 5, 3)
        .reshape(FR, 2 * TR, 2 * TC, CH)
    )
    scaled = (pixels / latent_scale).astype(jnp.bfloat16)
    padded = halo_extend(scaled)
    running = jnp.zeros((FR, 2 * TR, 2 * TC, conv_w.shape[3]), jnp.float32)
    for row_tap in range(3):
        for col_tap in range(3):
            window = padded[:, row_tap : row_tap + 2 * TR, col_tap : col_tap + 2 * TC, :]
            running = running + jnp.einsum(
                "fyxc,cd->fyxd",
                window,
                conv_w[row_tap, col_tap],
                preferred_element_type=jnp.float32,
            )
    return (out_hidden[None], updated[None], running.astype(jnp.bfloat16)[None])


def solution(mesh):
    placed = (
        P("req", "row", None),
        P("req", "row", None),
        P(),
        P(),
        P(),
        P("req", None, None),
        P(),
        P(),
        P(None, "row", "col"),
        P("col", None),
        P(None, "row"),
        P("row", None),
        P(),
        P("req", ("row", "col"), None),
        P(),
    )
    return jax.shard_map(
        shards,
        mesh=mesh,
        in_specs=placed,
        out_specs=(
            P("req", ("row", "col"), None),
            P("req", ("row", "col"), None),
            P("req", None, "row", "col", None),
        ),
        check_vma=False,
    )
```

```python
import functools

import jax
import jax.numpy as jnp
from jax import lax
from jax.sharding import PartitionSpec as P
from jax.experimental import pallas as pl
from jax.experimental.pallas import tpu as pltpu

MESH_IDS = pl.DeviceIdType.MESH

CH = 16
FR = 6
TR = 1
TC = 4
TRAIN_STEPS = 1000
STRIDE = 250


latent_scale = 0.7


def extended(cells, sides, width):
    for axis, dim in sides:
        count = lax.axis_size(axis)
        ends = count - 1
        head = lax.slice_in_dim(cells, 0, width, axis=dim)
        tail = lax.slice_in_dim(cells, cells.shape[dim] - width, cells.shape[dim], axis=dim)
        cells = jnp.concatenate(
            [
                lax.ppermute(tail, axis, [(i, (i + 1) % count) for i in range(ends)]),
                cells,
                lax.ppermute(head, axis, [((i + 1) % count, i) for i in range(ends)]),
            ],
            axis=dim,
        )
    return cells


def peer_on(axis, peer):
    return tuple(peer if name == axis else lax.axis_index(name) for name in ("req", "row", "col"))


def scatter_sum_kernel(axis, count, rows, part_ref, out_ref, landed, send_sems, recv_sems, own_sem):
    me = lax.axis_index(axis)
    barrier = pltpu.get_barrier_semaphore()
    for step in range(1, count):
        peer = lax.rem(me + step, count)
        pl.semaphore_signal(barrier, inc=1, device_id=peer_on(axis, peer), device_id_type=MESH_IDS)
    pl.semaphore_wait(barrier, count - 1)
    own = pltpu.make_async_copy(part_ref.at[pl.ds(me * rows, rows)], landed.at[me], own_sem)
    own.start()
    sends = []
    for step in range(1, count):
        peer = lax.rem(me + step, count)
        copy = pltpu.make_async_remote_copy(
            src_ref=part_ref.at[pl.ds(peer * rows, rows)],
            dst_ref=landed.at[me],
            send_sem=send_sems.at[step],
            recv_sem=recv_sems.at[step],
            device_id=peer_on(axis, peer),
            device_id_type=MESH_IDS,
        )
        copy.start()
        sends.append(copy)
    own.wait()
    for step in range(1, count):
        source = lax.rem(me + count - step, count)
        pltpu.make_async_remote_copy(
            src_ref=part_ref.at[pl.ds(me * rows, rows)],
            dst_ref=landed.at[source],
            send_sem=send_sems.at[step],
            recv_sem=recv_sems.at[step],
            device_id=peer_on(axis, source),
            device_id_type=MESH_IDS,
        ).wait_recv()
    for copy in sends:
        copy.wait_send()
    total = landed[0].astype(jnp.float32)
    for slot in range(1, count):
        total = total + landed[slot].astype(jnp.float32)
    out_ref[...] = total


def scatter_sum(part, axis, kernel_id):
    count = lax.axis_size(axis)
    rows = part.shape[0] // count
    width = part.shape[1]
    return pl.pallas_call(
        functools.partial(scatter_sum_kernel, axis, count, rows),
        out_shape=jax.ShapeDtypeStruct((rows, width), jnp.float32),
        in_specs=[pl.BlockSpec(memory_space=pl.ANY)],
        out_specs=pl.BlockSpec(memory_space=pltpu.VMEM),
        scratch_shapes=[
            pltpu.VMEM((count, rows, width), part.dtype),
            pltpu.SemaphoreType.DMA((count,)),
            pltpu.SemaphoreType.DMA((count,)),
            pltpu.SemaphoreType.DMA(()),
        ],
        compiler_params=pltpu.CompilerParams(
            collective_id=kernel_id, has_side_effects=True, vmem_limit_bytes=48 * 1024 * 1024
        ),
    )(part)


def attention_kernel(scale, q_ref, kv_ref, live_ref, out_ref):
    sources, _, block, width = kv_ref.shape
    lane = lax.broadcasted_iota(jnp.int32, (1, 128), 1)
    first = lane < 64
    live = live_ref[...]
    for pair in range(width // 128):
        cols = slice(pair * 128, (pair + 1) * 128)
        query = q_ref[:, cols]
        keys = kv_ref[:, 0, :, cols].reshape(sources * block, 128)
        values = kv_ref[:, 1, :, cols].reshape(sources * block, 128)
        results = []
        for half in (first, jnp.logical_not(first)):
            picked = jnp.where(half, query, jnp.zeros_like(query))
            scores = lax.dot_general(
                picked, keys, (((1,), (1,)), ((), ())), preferred_element_type=jnp.float32
            ) * scale
            weights = jnp.exp(scores) * live
            totals = jnp.sum(weights, axis=1, keepdims=True)
            summed = jnp.dot(weights.astype(jnp.bfloat16), values, preferred_element_type=jnp.float32)
            results.append(summed / totals)
        out_ref[:, cols] = jnp.where(first, results[0], results[1]).astype(out_ref.dtype)


def attention(queries, gathered, live, scale):
    return pl.pallas_call(
        functools.partial(attention_kernel, scale),
        out_shape=jax.ShapeDtypeStruct(queries.shape, jnp.bfloat16),
        in_specs=[pl.BlockSpec(memory_space=pltpu.VMEM)] * 3,
        out_specs=pl.BlockSpec(memory_space=pltpu.VMEM),
        compiler_params=pltpu.CompilerParams(vmem_limit_bytes=56 * 1024 * 1024),
    )(queries, gathered, live)


def ring_scatter_kernel(zs, xs, part_ref, out_ref, landed, outgoing, own_sum, crossed, ring_send, ring_recv, cross_send, cross_recv):
    me = lax.axis_index("row")
    xm = me // zs
    zm = me % zs
    ahead = xm * zs + lax.rem(zm + 1, zs)
    behind = xm * zs + lax.rem(zm + zs - 1, zs)
    half = part_ref.shape[3] // 2
    barrier = pltpu.get_barrier_semaphore()
    targets = [ahead, behind] + [lax.rem(xm + k, xs) * zs + zm for k in range(1, xs)]
    for peer in targets:
        pl.semaphore_signal(barrier, inc=1, device_id=peer_on("row", peer), device_id_type=MESH_IDS)
    pl.semaphore_wait(barrier, len(targets))
    ways = ((0, ahead, behind, -1), (1, behind, ahead, 1))
    pending = []
    for step in range(zs - 1):
        for way, dest, origin, sign in ways:
            cols = pl.ds(way * half, half)
            chunk = lax.rem(zm + sign * (1 + step) + 2 * zs, zs)
            if step == 0:
                source = part_ref.at[chunk, :, :, cols]
            else:
                arrived = pltpu.make_async_remote_copy(
                    src_ref=outgoing.at[way, step - 1],
                    dst_ref=landed.at[way, step - 1],
                    send_sem=ring_send.at[way, step - 1],
                    recv_sem=ring_recv.at[way, step - 1],
                    device_id=peer_on("row", origin),
                    device_id_type=MESH_IDS,
                )
                arrived.wait_recv()
                outgoing[way, step] = (
                    landed[way, step - 1].astype(jnp.float32)
                    + part_ref[chunk, :, :, cols].astype(jnp.float32)
                ).astype(outgoing.dtype)
                source = outgoing.at[way, step]
            copy = pltpu.make_async_remote_copy(
                src_ref=source,
                dst_ref=landed.at[way, step],
                send_sem=ring_send.at[way, step],
                recv_sem=ring_recv.at[way, step],
                device_id=peer_on("row", dest),
                device_id_type=MESH_IDS,
            )
            copy.start()
            pending.append(copy)
    last = zs - 2
    for way, dest, origin, sign in ways:
        cols = pl.ds(way * half, half)
        pltpu.make_async_remote_copy(
            src_ref=outgoing.at[way, last],
            dst_ref=landed.at[way, last],
            send_sem=ring_send.at[way, last],
            recv_sem=ring_recv.at[way, last],
            device_id=peer_on("row", origin),
            device_id_type=MESH_IDS,
        ).wait_recv()
        own_sum[:, :, cols] = landed[way, last].astype(jnp.float32) + part_ref[zm, :, :, cols].astype(jnp.float32)
    crossed[0] = own_sum[...].astype(crossed.dtype)
    sends = []
    for k in range(1, xs):
        peer_x = lax.rem(xm + k, xs)
        copy = pltpu.make_async_remote_copy(
            src_ref=crossed.at[0, peer_x],
            dst_ref=crossed.at[k, 0],
            send_sem=cross_send.at[k],
            recv_sem=cross_recv.at[k],
            device_id=peer_on("row", peer_x * zs + zm),
            device_id_type=MESH_IDS,
        )
        copy.start()
        sends.append(copy)
    total = own_sum[xm]
    for k in range(1, xs):
        origin_x = lax.rem(xm + xs - k, xs)
        pltpu.make_async_remote_copy(
            src_ref=crossed.at[0, 0],
            dst_ref=crossed.at[k, 0],
            send_sem=cross_send.at[k],
            recv_sem=cross_recv.at[k],
            device_id=peer_on("row", origin_x * zs + zm),
            device_id_type=MESH_IDS,
        ).wait_recv()
        total = total + crossed[k, 0].astype(jnp.float32)
    out_ref[...] = total
    for copy in pending + sends:
        copy.wait_send()


def ring_scatter_sum(part, xs, zs, kernel_id):
    rows = part.shape[0] // (xs * zs)
    width = part.shape[1]
    arranged = part.reshape(zs, xs, rows, width)
    return pl.pallas_call(
        functools.partial(ring_scatter_kernel, zs, xs),
        out_shape=jax.ShapeDtypeStruct((rows, width), jnp.float32),
        in_specs=[pl.BlockSpec(memory_space=pltpu.VMEM)],
        out_specs=pl.BlockSpec(memory_space=pltpu.VMEM),
        scratch_shapes=[
            pltpu.VMEM((2, zs - 1, xs, rows, width // 2), part.dtype),
            pltpu.VMEM((2, zs - 1, xs, rows, width // 2), part.dtype),
            pltpu.VMEM((xs, rows, width), jnp.float32),
            pltpu.VMEM((xs, xs, rows, width), part.dtype),
            pltpu.SemaphoreType.DMA((2, zs - 1)),
            pltpu.SemaphoreType.DMA((2, zs - 1)),
            pltpu.SemaphoreType.DMA((xs,)),
            pltpu.SemaphoreType.DMA((xs,)),
        ],
        compiler_params=pltpu.CompilerParams(
            collective_id=kernel_id, has_side_effects=True, vmem_limit_bytes=56 * 1024 * 1024
        ),
    )(arranged)


def ring_gather_kernel(zs, xs, block_ref, out_ref, held, own_sem, ring_send, ring_recv, cross_send, cross_recv):
    me = lax.axis_index("row")
    xm = me // zs
    zm = me % zs
    ahead = xm * zs + lax.rem(zm + 1, zs)
    behind = xm * zs + lax.rem(zm + zs - 1, zs)
    barrier = pltpu.get_barrier_semaphore()
    targets = [ahead, behind] + [lax.rem(xm + k, xs) * zs + zm for k in range(1, xs)]
    for peer in targets:
        pl.semaphore_signal(barrier, inc=1, device_id=peer_on("row", peer), device_id_type=MESH_IDS)
    pl.semaphore_wait(barrier, len(targets))
    own = pltpu.make_async_copy(block_ref, held.at[zm, xm], own_sem)
    own.start()
    pending = []
    for k in range(1, xs):
        peer_x = lax.rem(xm + k, xs)
        copy = pltpu.make_async_remote_copy(
            src_ref=block_ref,
            dst_ref=held.at[zm, xm],
            send_sem=cross_send.at[k],
            recv_sem=cross_recv.at[k],
            device_id=peer_on("row", peer_x * zs + zm),
            device_id_type=MESH_IDS,
        )
        copy.start()
        pending.append(copy)
    own.wait()
    for k in range(1, xs):
        origin_x = lax.rem(xm + xs - k, xs)
        pltpu.make_async_remote_copy(
            src_ref=block_ref,
            dst_ref=held.at[zm, origin_x],
            send_sem=cross_send.at[k],
            recv_sem=cross_recv.at[k],
            device_id=peer_on("row", origin_x * zs + zm),
            device_id_type=MESH_IDS,
        ).wait_recv()
    split = xs // 2
    ways = ((0, ahead, behind, -1, pl.ds(0, split)), (1, behind, ahead, 1, pl.ds(split, xs - split)))
    for step in range(zs):
        for way, dest, origin, sign, part in ways:
            group = lax.rem(zm + sign * step + zs, zs)
            if step > 0:
                pltpu.make_async_remote_copy(
                    src_ref=held.at[group, part],
                    dst_ref=held.at[group, part],
                    send_sem=ring_send.at[way, step - 1],
                    recv_sem=ring_recv.at[way, step - 1],
                    device_id=peer_on("row", origin),
                    device_id_type=MESH_IDS,
                ).wait_recv()
            if step < zs - 1:
                copy = pltpu.make_async_remote_copy(
                    src_ref=held.at[group, part],
                    dst_ref=held.at[group, part],
                    send_sem=ring_send.at[way, step],
                    recv_sem=ring_recv.at[way, step],
                    device_id=peer_on("row", dest),
                    device_id_type=MESH_IDS,
                )
                copy.start()
                pending.append(copy)
    for copy in pending:
        copy.wait_send()
    out = pltpu.make_async_copy(held, out_ref, own_sem)
    out.start()
    out.wait()


def ring_gather(block, xs, zs, kernel_id):
    return pl.pallas_call(
        functools.partial(ring_gather_kernel, zs, xs),
        out_shape=jax.ShapeDtypeStruct((zs, xs) + block.shape, block.dtype),
        in_specs=[pl.BlockSpec(memory_space=pltpu.VMEM)],
        out_specs=pl.BlockSpec(memory_space=pl.ANY),
        scratch_shapes=[
            pltpu.VMEM((zs, xs) + block.shape, block.dtype),
            pltpu.SemaphoreType.DMA(()),
            pltpu.SemaphoreType.DMA((2, zs - 1)),
            pltpu.SemaphoreType.DMA((2, zs - 1)),
            pltpu.SemaphoreType.DMA((xs,)),
            pltpu.SemaphoreType.DMA((xs,)),
        ],
        compiler_params=pltpu.CompilerParams(
            collective_id=kernel_id, has_side_effects=True, vmem_limit_bytes=56 * 1024 * 1024
        ),
    )(block)


def swap_kernel(src_ref, out_ref, landed, sems):
    other = 1 - lax.axis_index("req")
    barrier = pltpu.get_barrier_semaphore()
    pl.semaphore_signal(barrier, inc=1, device_id=peer_on("req", other), device_id_type=MESH_IDS)
    pl.semaphore_wait(barrier, 1)
    copy = pltpu.make_async_remote_copy(
        src_ref=src_ref,
        dst_ref=landed,
        send_sem=sems.at[0],
        recv_sem=sems.at[1],
        device_id=peer_on("req", other),
        device_id_type=MESH_IDS,
    )
    copy.start()
    copy.wait_send()
    copy.wait_recv()
    out_ref[...] = landed[...]


def partner_swap(value, kernel_id):
    return pl.pallas_call(
        swap_kernel,
        out_shape=jax.ShapeDtypeStruct(value.shape, value.dtype),
        in_specs=[pl.BlockSpec(memory_space=pltpu.VMEM)],
        out_specs=pl.BlockSpec(memory_space=pltpu.VMEM),
        scratch_shapes=[pltpu.VMEM(value.shape, value.dtype), pltpu.SemaphoreType.DMA((2,))],
        compiler_params=pltpu.CompilerParams(collective_id=kernel_id, has_side_effects=True),
    )(value)


def halo_kernel(tile_ref, out_ref, slots, send_sems, recv_sems):
    req = lax.axis_index("req")
    row = lax.axis_index("row")
    col = lax.axis_index("col")
    rows = lax.axis_size("row")
    cols = lax.axis_size("col")
    offsets = [(a, b) for a in (-1, 0, 1) for b in (-1, 0, 1) if (a, b) != (0, 0)]

    def present(a, b):
        return (row + a >= 0) & (row + a < rows) & (col + b >= 0) & (col + b < cols)

    def link(a, b):
        return pltpu.make_async_remote_copy(
            src_ref=tile_ref,
            dst_ref=slots.at[1 - a, 1 - b],
            send_sem=send_sems.at[1 + a, 1 + b],
            recv_sem=recv_sems.at[1 - a, 1 - b],
            device_id=(req, row + a, col + b),
            device_id_type=MESH_IDS,
        )

    barrier = pltpu.get_barrier_semaphore()
    for a, b in offsets:
        @pl.when(present(a, b))
        def _():
            pl.semaphore_signal(barrier, inc=1, device_id=(req, row + a, col + b), device_id_type=MESH_IDS)
    up = (row + rows - 1) // rows
    down = (2 * rows - 2 - row) // rows
    left = (col + cols - 1) // cols
    right = (2 * cols - 2 - col) // cols
    pl.semaphore_wait(barrier, (1 + up + down) * (1 + left + right) - 1)
    for a, b in offsets:
        @pl.when(present(a, b))
        def _():
            link(a, b).start()
    for a, b in offsets:
        @pl.when(present(a, b))
        def _():
            copy = link(a, b)
            copy.wait_send()
            pltpu.make_async_remote_copy(
                src_ref=tile_ref,
                dst_ref=slots.at[1 + a, 1 + b],
                send_sem=send_sems.at[1 + a, 1 + b],
                recv_sem=recv_sems.at[1 + a, 1 + b],
                device_id=(req, row + a, col + b),
                device_id_type=MESH_IDS,
            ).wait_recv()
            out_ref[1 + a, 1 + b] = slots[1 + a, 1 + b]

        @pl.when(jnp.logical_not(present(a, b)))
        def _():
            out_ref[1 + a, 1 + b] = jnp.zeros(out_ref.shape[2:], out_ref.dtype)
    out_ref[1, 1] = tile_ref[...]


def halo_extend(tile):
    gathered = pl.pallas_call(
        halo_kernel,
        out_shape=jax.ShapeDtypeStruct((3, 3) + tile.shape, tile.dtype),
        in_specs=[pl.BlockSpec(memory_space=pltpu.VMEM)],
        out_specs=pl.BlockSpec(memory_space=pltpu.VMEM),
        scratch_shapes=[
            pltpu.VMEM((3, 3) + tile.shape, tile.dtype),
            pltpu.SemaphoreType.DMA((3, 3)),
            pltpu.SemaphoreType.DMA((3, 3)),
        ],
        compiler_params=pltpu.CompilerParams(collective_id=6, has_side_effects=True),
    )(tile)
    bands = []
    for a, pick_rows in ((0, slice(-1, None)), (1, slice(None)), (2, slice(0, 1))):
        pieces = [
            gathered[a, 0][:, pick_rows, -1:],
            gathered[a, 1][:, pick_rows, :],
            gathered[a, 2][:, pick_rows, :1],
        ]
        bands.append(jnp.concatenate(pieces, axis=2))
    return jnp.concatenate(bands, axis=1)


def prep_kernel(eps, raw_ref, q_gain_ref, k_gain_ref, q_ref, kv_ref):
    span = raw_ref.shape[1]
    lane = lax.broadcasted_iota(jnp.int32, (1, 128), 1)
    first = lane < 64
    kv_ref[...] = jnp.zeros(kv_ref.shape, kv_ref.dtype)
    for pair in range(raw_ref.shape[2] // 128):
        cols = slice(pair * 128, (pair + 1) * 128)
        for which, gain_ref in ((0, q_gain_ref), (1, k_gain_ref)):
            piece = raw_ref[which, :, cols]
            low = jnp.sum(jnp.where(first, piece, 0.0), axis=1, keepdims=True)
            high = jnp.sum(jnp.where(first, 0.0, piece), axis=1, keepdims=True)
            centered = piece - jnp.where(first, low, high) / 64.0
            squared = centered * centered
            low = jnp.sum(jnp.where(first, squared, 0.0), axis=1, keepdims=True)
            high = jnp.sum(jnp.where(first, 0.0, squared), axis=1, keepdims=True)
            spread = jnp.where(first, low, high) / 64.0
            normed = (centered * lax.rsqrt(spread + eps) * gain_ref[:, cols]).astype(jnp.bfloat16)
            if which == 0:
                q_ref[:, cols] = normed
            else:
                kv_ref[0, :span, cols] = normed
        kv_ref[1, :span, cols] = raw_ref[2, :, cols].astype(jnp.bfloat16)


def prep_heads(raw, q_gain, k_gain, padded_span):
    width = raw.shape[2]
    tiles = width // q_gain.shape[0]
    return pl.pallas_call(
        functools.partial(prep_kernel, 1e-06),
        out_shape=(
            jax.ShapeDtypeStruct((raw.shape[1], width), jnp.bfloat16),
            jax.ShapeDtypeStruct((2, padded_span, width), jnp.bfloat16),
        ),
        in_specs=[pl.BlockSpec(memory_space=pltpu.VMEM)] * 3,
        out_specs=(pl.BlockSpec(memory_space=pltpu.VMEM), pl.BlockSpec(memory_space=pltpu.VMEM)),
    )(raw, jnp.tile(q_gain, tiles)[None], jnp.tile(k_gain, tiles)[None])


def layer_norm(tensor, epsilon):
    average = jnp.mean(tensor, axis=-1, keepdims=True)
    centered = tensor - average
    spread = jnp.mean(centered * centered, axis=-1, keepdims=True)
    return centered * lax.rsqrt(spread + epsilon)


def modulate(tensor, offset, factor):
    return (layer_norm(tensor, 1e-05) * (1.0 + factor) + offset).astype(jnp.bfloat16)


def head_norm(tensor, scaling):
    return (layer_norm(tensor, 1e-06) * scaling).astype(jnp.bfloat16)


def pick_entry(entries, position):
    slot_ids = jnp.arange(entries.shape[0], dtype=jnp.int32)
    return jnp.sum(jnp.where(slot_ids == position, entries, jnp.zeros_like(entries)))


def solver_weights(step_index):
    plan = jnp.linspace(0.00085**0.5, 0.012**0.5, TRAIN_STEPS, dtype=jnp.float32) ** 2
    cumulative = jnp.cumprod(1.0 - plan)
    alpha_now = pick_entry(cumulative, step_index)
    alpha_prev = pick_entry(cumulative, step_index - STRIDE)
    root_now = jnp.sqrt(alpha_now)
    rest_now = jnp.sqrt(1.0 - alpha_now)
    root_prev = jnp.sqrt(alpha_prev)
    rest_prev = jnp.sqrt(1.0 - alpha_prev)
    return (
        root_prev * root_now + rest_prev * rest_now,
        rest_prev * root_now - root_prev * rest_now,
    )


def key_mask(count, owners, grid, text_len, span, block_tokens, tile, text_rows):
    positions = jnp.arange(count, dtype=jnp.int32)
    owner_row = positions // span
    within = positions % span
    is_video = within < block_tokens
    owner_col = within // tile
    local_ids = within % tile
    token_row = owner_row * TR + local_ids // TC % TR
    token_col = owner_col * TC + local_ids % TC
    text_index = owner_row * text_rows + within - block_tokens
    matches = jnp.arange(grid.shape[0], dtype=jnp.int32)[None, :] == owners[:, None]
    rows_live = jnp.sum(jnp.where(matches, grid[None, :, 0], 0), axis=1)
    cols_live = jnp.sum(jnp.where(matches, grid[None, :, 1], 0), axis=1)
    text_lens = jnp.sum(jnp.where(matches, text_len[None, :], 0), axis=1)
    video_live = (token_row[None, :] < rows_live[:, None]) & (
        token_col[None, :] < cols_live[:, None]
    )
    text_live = (text_index[None, :] < text_lens[:, None]) & (within < block_tokens + text_rows)[None, :]
    return jnp.where(is_video[None, :], video_live, text_live).astype(jnp.float32)


def projector(stacked, piece):
    return jnp.einsum("gld,cde->cgle", stacked, piece, preferred_element_type=jnp.float32)


def attention_step(queries, owners, grid, text_len, span, block_tokens, tile, text_rows):
    score_scale = queries.shape[3] ** (-0.5)

    def attend(carry, pieces, start):
        key_piece, value_piece = pieces
        live_keys = key_mask(
            key_piece.shape[1], owners, grid, text_len, span, block_tokens, tile, text_rows
        )
        scores = (
            jnp.einsum("gqhd,gkhd->gqhk", queries, key_piece, preferred_element_type=jnp.float32)
            * score_scale
        )
        raw_weights = jnp.exp(scores) * live_keys[:, None, None, :]
        weighted = jnp.einsum(
            "gqhk,gkhd->gqhd",
            raw_weights.astype(jnp.bfloat16),
            value_piece,
            preferred_element_type=jnp.float32,
        )
        return (weighted, jnp.sum(raw_weights, axis=3))

    return attend


def shards(
    hidden,
    text_hidden,
    text_len,
    grid,
    timestep,
    modulation,
    q_gain,
    k_gain,
    w_qkv,
    w_out,
    w_up,
    w_down,
    w_proj,
    latent,
    conv_w,
):
    col_count = lax.axis_size("col")
    request_id = lax.axis_index("req")
    row_id = lax.axis_index("row")
    col_id = lax.axis_index("col")
    block_tokens = hidden.shape[1]
    tile = block_tokens // col_count
    text_rows = text_hidden.shape[1]
    head_dim = q_gain.shape[0]
    adaptive = modulation[0]
    source = hidden[0].astype(jnp.float32)
    joined = jnp.concatenate(
        [
            modulate(source, adaptive[0], adaptive[1]),
            modulate(text_hidden[0].astype(jnp.float32), adaptive[0], adaptive[1]),
        ],
        axis=0,
    )
    span = joined.shape[0]
    stacked = joined[None]
    owners = jnp.reshape(request_id, (1,))
    half_cols = w_qkv.shape[2] // 2
    own_half = lax.dynamic_slice_in_dim(w_qkv, request_id * half_cols, half_cols, 2)
    gathered_half = lax.all_gather(own_half, "row", axis=1, tiled=True)
    half_heads = half_cols // head_dim

    both_rows = jnp.concatenate([joined, partner_swap(joined, 4)], axis=0)
    projected_rows = jnp.einsum("ld,cde->cle", both_rows, gathered_half, preferred_element_type=jnp.float32)
    own_raw = projected_rows[:, :span]
    received_raw = partner_swap(projected_rows[:, span:], 5)
    raw = jnp.concatenate(
        [jnp.where(request_id == 0, own_raw, received_raw), jnp.where(request_id == 0, received_raw, own_raw)], axis=2
    )
    heads_here = raw.shape[2] // head_dim
    padded_span = 16 * pl.cdiv(span, 16)
    all_queries, both = prep_heads(raw, q_gain, k_gain, padded_span)
    gathered = lax.all_gather(both[None], "row", axis=0, tiled=True)
    live = key_mask(
        gathered.shape[0] * padded_span, owners, grid, text_len, padded_span, block_tokens, tile, text_rows
    )
    attended = attention(all_queries[:block_tokens], gathered, live, head_dim ** (-0.5))
    partial_out = jnp.dot(attended, w_out, preferred_element_type=jnp.float32)
    projected = scatter_sum(partial_out.astype(jnp.bfloat16), "col", 1)
    own_rows = lax.dynamic_slice_in_dim(source, col_id * tile, tile, 0)
    mixed = lax.optimization_barrier(
        (own_rows + adaptive[2] * projected).astype(jnp.bfloat16)
    ).astype(jnp.float32)
    second_norm = modulate(mixed, adaptive[3], adaptive[4])
    hidden_units = jax.nn.gelu(
        jnp.dot(
            ring_gather(second_norm, 4, 8, 2).reshape(-1, second_norm.shape[1]),
            w_up,
            preferred_element_type=jnp.float32,
        ),
        approximate=True,
    ).astype(jnp.bfloat16)
    feed_terms = jnp.dot(hidden_units, w_down, preferred_element_type=jnp.float32)
    feed_out = ring_scatter_sum(feed_terms.astype(jnp.bfloat16), 4, 8, 0)
    out_hidden = (mixed + adaptive[5] * feed_out).astype(jnp.bfloat16)
    final_norm = modulate(out_hidden.astype(jnp.float32), adaptive[6], adaptive[7])
    velocity = jnp.dot(final_norm, w_proj, preferred_element_type=jnp.float32)
    local_ids = jnp.arange(tile, dtype=jnp.int32)
    token_row = row_id * TR + local_ids // TC % TR
    token_col = col_id * TC + local_ids % TC
    rows_live = pick_entry(grid[:, 0], request_id)
    cols_live = pick_entry(grid[:, 1], request_id)
    live_tokens = ((token_row < rows_live) & (token_col < cols_live)).astype(jnp.float32)
    keep_part, velocity_part = solver_weights(pick_entry(timestep, request_id))
    updated = (keep_part * latent[0] + velocity_part * velocity) * live_tokens[:, None]
    pixels = (
        updated.reshape(FR, TR, TC, CH, 2, 2)
        .transpose(0, 1, 4, 2, 5, 3)
        .reshape(FR, 2 * TR, 2 * TC, CH)
    )
    scaled = (pixels / latent_scale).astype(jnp.bfloat16)
    padded = halo_extend(scaled)
    running = jnp.zeros((FR, 2 * TR, 2 * TC, conv_w.shape[3]), jnp.float32)
    for row_tap in range(3):
        for col_tap in range(3):
            window = padded[:, row_tap : row_tap + 2 * TR, col_tap : col_tap + 2 * TC, :]
            running = running + jnp.einsum(
                "fyxc,cd->fyxd",
                window,
                conv_w[row_tap, col_tap],
                preferred_element_type=jnp.float32,
            )
    return (out_hidden[None], updated[None], running.astype(jnp.bfloat16)[None])


def solution(mesh):
    placed = (
        P("req", "row", None),
        P("req", "row", None),
        P(),
        P(),
        P(),
        P("req", None, None),
        P(),
        P(),
        P(None, "row", "col"),
        P("col", None),
        P(None, "row"),
        P("row", None),
        P(),
        P("req", ("row", "col"), None),
        P(),
    )
    return jax.shard_map(
        shards,
        mesh=mesh,
        in_specs=placed,
        out_specs=(
            P("req", ("row", "col"), None),
            P("req", ("row", "col"), None),
            P("req", None, "row", "col", None),
        ),
        check_vma=False,
    )
```

```python
import functools

import jax
import jax.numpy as jnp
from jax import lax
from jax.sharding import PartitionSpec as P
from jax.experimental import pallas as pl
from jax.experimental.pallas import tpu as pltpu

MESH_IDS = pl.DeviceIdType.MESH

CH = 16
FR = 6
TR = 1
TC = 4
TRAIN_STEPS = 1000
STRIDE = 250


latent_scale = 0.7


def extended(cells, sides, width):
    for axis, dim in sides:
        count = lax.axis_size(axis)
        ends = count - 1
        head = lax.slice_in_dim(cells, 0, width, axis=dim)
        tail = lax.slice_in_dim(cells, cells.shape[dim] - width, cells.shape[dim], axis=dim)
        cells = jnp.concatenate(
            [
                lax.ppermute(tail, axis, [(i, (i + 1) % count) for i in range(ends)]),
                cells,
                lax.ppermute(head, axis, [((i + 1) % count, i) for i in range(ends)]),
            ],
            axis=dim,
        )
    return cells


def peer_on(axis, peer):
    return tuple(peer if name == axis else lax.axis_index(name) for name in ("req", "row", "col"))


def scatter_sum_kernel(axis, count, rows, part_ref, out_ref, landed, send_sems, recv_sems, own_sem):
    me = lax.axis_index(axis)
    barrier = pltpu.get_barrier_semaphore()
    for step in range(1, count):
        peer = lax.rem(me + step, count)
        pl.semaphore_signal(barrier, inc=1, device_id=peer_on(axis, peer), device_id_type=MESH_IDS)
    pl.semaphore_wait(barrier, count - 1)
    own = pltpu.make_async_copy(part_ref.at[pl.ds(me * rows, rows)], landed.at[me], own_sem)
    own.start()
    sends = []
    for step in range(1, count):
        peer = lax.rem(me + step, count)
        copy = pltpu.make_async_remote_copy(
            src_ref=part_ref.at[pl.ds(peer * rows, rows)],
            dst_ref=landed.at[me],
            send_sem=send_sems.at[step],
            recv_sem=recv_sems.at[step],
            device_id=peer_on(axis, peer),
            device_id_type=MESH_IDS,
        )
        copy.start()
        sends.append(copy)
    own.wait()
    for step in range(1, count):
        source = lax.rem(me + count - step, count)
        pltpu.make_async_remote_copy(
            src_ref=part_ref.at[pl.ds(me * rows, rows)],
            dst_ref=landed.at[source],
            send_sem=send_sems.at[step],
            recv_sem=recv_sems.at[step],
            device_id=peer_on(axis, source),
            device_id_type=MESH_IDS,
        ).wait_recv()
    for copy in sends:
        copy.wait_send()
    total = landed[0].astype(jnp.float32)
    for slot in range(1, count):
        total = total + landed[slot].astype(jnp.float32)
    out_ref[...] = total


def scatter_sum(part, axis, kernel_id):
    count = lax.axis_size(axis)
    rows = part.shape[0] // count
    width = part.shape[1]
    return pl.pallas_call(
        functools.partial(scatter_sum_kernel, axis, count, rows),
        out_shape=jax.ShapeDtypeStruct((rows, width), jnp.float32),
        in_specs=[pl.BlockSpec(memory_space=pl.ANY)],
        out_specs=pl.BlockSpec(memory_space=pltpu.VMEM),
        scratch_shapes=[
            pltpu.VMEM((count, rows, width), part.dtype),
            pltpu.SemaphoreType.DMA((count,)),
            pltpu.SemaphoreType.DMA((count,)),
            pltpu.SemaphoreType.DMA(()),
        ],
        compiler_params=pltpu.CompilerParams(
            collective_id=kernel_id, has_side_effects=True, vmem_limit_bytes=48 * 1024 * 1024
        ),
    )(part)


def attention_kernel(scale, q_ref, first_kv, second_kv, first_live, second_live, out_ref):
    lane = lax.broadcasted_iota(jnp.int32, (1, 128), 1)
    first = lane < 64
    per_half = first_kv.shape[3] // 128
    for pair in range(2 * per_half):
        kv_ref, live_ref = (first_kv, first_live) if pair < per_half else (second_kv, second_live)
        sources, _, block, width = kv_ref.shape
        live = live_ref[...]
        cols = slice(pair * 128, (pair + 1) * 128)
        local = slice((pair % per_half) * 128, (pair % per_half + 1) * 128)
        query = q_ref[:, cols]
        keys = kv_ref[:, 0, :, local].reshape(sources * block, 128)
        values = kv_ref[:, 1, :, local].reshape(sources * block, 128)
        results = []
        for half in (first, jnp.logical_not(first)):
            picked = jnp.where(half, query, jnp.zeros_like(query))
            scores = lax.dot_general(
                picked, keys, (((1,), (1,)), ((), ())), preferred_element_type=jnp.float32
            ) * scale
            weights = jnp.exp(scores) * live
            totals = jnp.sum(weights, axis=1, keepdims=True)
            summed = jnp.dot(weights.astype(jnp.bfloat16), values, preferred_element_type=jnp.float32)
            results.append(summed / totals)
        out_ref[:, cols] = jnp.where(first, results[0], results[1]).astype(out_ref.dtype)


def attention(queries, first_kv, second_kv, first_live, second_live, scale):
    return pl.pallas_call(
        functools.partial(attention_kernel, scale),
        out_shape=jax.ShapeDtypeStruct(queries.shape, jnp.bfloat16),
        in_specs=[pl.BlockSpec(memory_space=pltpu.VMEM)] * 5,
        out_specs=pl.BlockSpec(memory_space=pltpu.VMEM),
        compiler_params=pltpu.CompilerParams(vmem_limit_bytes=56 * 1024 * 1024),
    )(queries, first_kv, second_kv, first_live, second_live)


def ring_scatter_kernel(zs, xs, part_ref, out_ref, landed, outgoing, own_sum, crossed, ring_send, ring_recv, cross_send, cross_recv):
    me = lax.axis_index("row")
    xm = me // zs
    zm = me % zs
    ahead = xm * zs + lax.rem(zm + 1, zs)
    behind = xm * zs + lax.rem(zm + zs - 1, zs)
    half = part_ref.shape[3] // 2
    barrier = pltpu.get_barrier_semaphore()
    targets = [ahead, behind] + [lax.rem(xm + k, xs) * zs + zm for k in range(1, xs)]
    for peer in targets:
        pl.semaphore_signal(barrier, inc=1, device_id=peer_on("row", peer), device_id_type=MESH_IDS)
    pl.semaphore_wait(barrier, len(targets))
    ways = ((0, ahead, behind, -1), (1, behind, ahead, 1))
    pending = []
    for step in range(zs - 1):
        for way, dest, origin, sign in ways:
            cols = pl.ds(way * half, half)
            chunk = lax.rem(zm + sign * (1 + step) + 2 * zs, zs)
            if step == 0:
                source = part_ref.at[chunk, :, :, cols]
            else:
                arrived = pltpu.make_async_remote_copy(
                    src_ref=outgoing.at[way, step - 1],
                    dst_ref=landed.at[way, step - 1],
                    send_sem=ring_send.at[way, step - 1],
                    recv_sem=ring_recv.at[way, step - 1],
                    device_id=peer_on("row", origin),
                    device_id_type=MESH_IDS,
                )
                arrived.wait_recv()
                outgoing[way, step] = (
                    landed[way, step - 1].astype(jnp.float32)
                    + part_ref[chunk, :, :, cols].astype(jnp.float32)
                ).astype(outgoing.dtype)
                source = outgoing.at[way, step]
            copy = pltpu.make_async_remote_copy(
                src_ref=source,
                dst_ref=landed.at[way, step],
                send_sem=ring_send.at[way, step],
                recv_sem=ring_recv.at[way, step],
                device_id=peer_on("row", dest),
                device_id_type=MESH_IDS,
            )
            copy.start()
            pending.append(copy)
    last = zs - 2
    for way, dest, origin, sign in ways:
        cols = pl.ds(way * half, half)
        pltpu.make_async_remote_copy(
            src_ref=outgoing.at[way, last],
            dst_ref=landed.at[way, last],
            send_sem=ring_send.at[way, last],
            recv_sem=ring_recv.at[way, last],
            device_id=peer_on("row", origin),
            device_id_type=MESH_IDS,
        ).wait_recv()
        own_sum[:, :, cols] = landed[way, last].astype(jnp.float32) + part_ref[zm, :, :, cols].astype(jnp.float32)
    crossed[0] = own_sum[...].astype(crossed.dtype)
    sends = []
    for k in range(1, xs):
        peer_x = lax.rem(xm + k, xs)
        copy = pltpu.make_async_remote_copy(
            src_ref=crossed.at[0, peer_x],
            dst_ref=crossed.at[k, 0],
            send_sem=cross_send.at[k],
            recv_sem=cross_recv.at[k],
            device_id=peer_on("row", peer_x * zs + zm),
            device_id_type=MESH_IDS,
        )
        copy.start()
        sends.append(copy)
    total = own_sum[xm]
    for k in range(1, xs):
        origin_x = lax.rem(xm + xs - k, xs)
        pltpu.make_async_remote_copy(
            src_ref=crossed.at[0, 0],
            dst_ref=crossed.at[k, 0],
            send_sem=cross_send.at[k],
            recv_sem=cross_recv.at[k],
            device_id=peer_on("row", origin_x * zs + zm),
            device_id_type=MESH_IDS,
        ).wait_recv()
        total = total + crossed[k, 0].astype(jnp.float32)
    out_ref[...] = total
    for copy in pending + sends:
        copy.wait_send()


def ring_scatter_sum(part, xs, zs, kernel_id):
    rows = part.shape[0] // (xs * zs)
    width = part.shape[1]
    arranged = part.reshape(zs, xs, rows, width)
    return pl.pallas_call(
        functools.partial(ring_scatter_kernel, zs, xs),
        out_shape=jax.ShapeDtypeStruct((rows, width), jnp.float32),
        in_specs=[pl.BlockSpec(memory_space=pltpu.VMEM)],
        out_specs=pl.BlockSpec(memory_space=pltpu.VMEM),
        scratch_shapes=[
            pltpu.VMEM((2, zs - 1, xs, rows, width // 2), part.dtype),
            pltpu.VMEM((2, zs - 1, xs, rows, width // 2), part.dtype),
            pltpu.VMEM((xs, rows, width), jnp.float32),
            pltpu.VMEM((xs, xs, rows, width), part.dtype),
            pltpu.SemaphoreType.DMA((2, zs - 1)),
            pltpu.SemaphoreType.DMA((2, zs - 1)),
            pltpu.SemaphoreType.DMA((xs,)),
            pltpu.SemaphoreType.DMA((xs,)),
        ],
        compiler_params=pltpu.CompilerParams(
            collective_id=kernel_id, has_side_effects=True, vmem_limit_bytes=56 * 1024 * 1024
        ),
    )(arranged)


def ring_gather_kernel(zs, xs, block_ref, out_ref, held, own_sem, ring_send, ring_recv, cross_send, cross_recv):
    me = lax.axis_index("row")
    xm = me // zs
    zm = me % zs
    ahead = xm * zs + lax.rem(zm + 1, zs)
    behind = xm * zs + lax.rem(zm + zs - 1, zs)
    barrier = pltpu.get_barrier_semaphore()
    targets = [ahead, behind] + [lax.rem(xm + k, xs) * zs + zm for k in range(1, xs)]
    for peer in targets:
        pl.semaphore_signal(barrier, inc=1, device_id=peer_on("row", peer), device_id_type=MESH_IDS)
    pl.semaphore_wait(barrier, len(targets))
    own = pltpu.make_async_copy(block_ref, held.at[zm, xm], own_sem)
    own.start()
    pending = []
    for k in range(1, xs):
        peer_x = lax.rem(xm + k, xs)
        copy = pltpu.make_async_remote_copy(
            src_ref=block_ref,
            dst_ref=held.at[zm, xm],
            send_sem=cross_send.at[k],
            recv_sem=cross_recv.at[k],
            device_id=peer_on("row", peer_x * zs + zm),
            device_id_type=MESH_IDS,
        )
        copy.start()
        pending.append(copy)
    own.wait()
    for k in range(1, xs):
        origin_x = lax.rem(xm + xs - k, xs)
        pltpu.make_async_remote_copy(
            src_ref=block_ref,
            dst_ref=held.at[zm, origin_x],
            send_sem=cross_send.at[k],
            recv_sem=cross_recv.at[k],
            device_id=peer_on("row", origin_x * zs + zm),
            device_id_type=MESH_IDS,
        ).wait_recv()
    split = xs // 2
    ways = ((0, ahead, behind, -1, pl.ds(0, split)), (1, behind, ahead, 1, pl.ds(split, xs - split)))
    for step in range(zs):
        for way, dest, origin, sign, part in ways:
            group = lax.rem(zm + sign * step + zs, zs)
            if step > 0:
                pltpu.make_async_remote_copy(
                    src_ref=held.at[group, part],
                    dst_ref=held.at[group, part],
                    send_sem=ring_send.at[way, step - 1],
                    recv_sem=ring_recv.at[way, step - 1],
                    device_id=peer_on("row", origin),
                    device_id_type=MESH_IDS,
                ).wait_recv()
            if step < zs - 1:
                copy = pltpu.make_async_remote_copy(
                    src_ref=held.at[group, part],
                    dst_ref=held.at[group, part],
                    send_sem=ring_send.at[way, step],
                    recv_sem=ring_recv.at[way, step],
                    device_id=peer_on("row", dest),
                    device_id_type=MESH_IDS,
                )
                copy.start()
                pending.append(copy)
    for copy in pending:
        copy.wait_send()
    out = pltpu.make_async_copy(held, out_ref, own_sem)
    out.start()
    out.wait()


def ring_gather(block, xs, zs, kernel_id):
    return pl.pallas_call(
        functools.partial(ring_gather_kernel, zs, xs),
        out_shape=jax.ShapeDtypeStruct((zs, xs) + block.shape, block.dtype),
        in_specs=[pl.BlockSpec(memory_space=pltpu.VMEM)],
        out_specs=pl.BlockSpec(memory_space=pl.ANY),
        scratch_shapes=[
            pltpu.VMEM((zs, xs) + block.shape, block.dtype),
            pltpu.SemaphoreType.DMA(()),
            pltpu.SemaphoreType.DMA((2, zs - 1)),
            pltpu.SemaphoreType.DMA((2, zs - 1)),
            pltpu.SemaphoreType.DMA((xs,)),
            pltpu.SemaphoreType.DMA((xs,)),
        ],
        compiler_params=pltpu.CompilerParams(
            collective_id=kernel_id, has_side_effects=True, vmem_limit_bytes=56 * 1024 * 1024
        ),
    )(block)


def swap_kernel(src_ref, out_ref, landed, sems):
    other = 1 - lax.axis_index("req")
    barrier = pltpu.get_barrier_semaphore()
    pl.semaphore_signal(barrier, inc=1, device_id=peer_on("req", other), device_id_type=MESH_IDS)
    pl.semaphore_wait(barrier, 1)
    copy = pltpu.make_async_remote_copy(
        src_ref=src_ref,
        dst_ref=landed,
        send_sem=sems.at[0],
        recv_sem=sems.at[1],
        device_id=peer_on("req", other),
        device_id_type=MESH_IDS,
    )
    copy.start()
    copy.wait_send()
    copy.wait_recv()
    out_ref[...] = landed[...]


def partner_swap(value, kernel_id):
    return pl.pallas_call(
        swap_kernel,
        out_shape=jax.ShapeDtypeStruct(value.shape, value.dtype),
        in_specs=[pl.BlockSpec(memory_space=pltpu.VMEM)],
        out_specs=pl.BlockSpec(memory_space=pltpu.VMEM),
        scratch_shapes=[pltpu.VMEM(value.shape, value.dtype), pltpu.SemaphoreType.DMA((2,))],
        compiler_params=pltpu.CompilerParams(collective_id=kernel_id, has_side_effects=True),
    )(value)


def halo_kernel(tile_ref, out_ref, slots, send_sems, recv_sems):
    req = lax.axis_index("req")
    row = lax.axis_index("row")
    col = lax.axis_index("col")
    rows = lax.axis_size("row")
    cols = lax.axis_size("col")
    offsets = [(a, b) for a in (-1, 0, 1) for b in (-1, 0, 1) if (a, b) != (0, 0)]

    def present(a, b):
        return (row + a >= 0) & (row + a < rows) & (col + b >= 0) & (col + b < cols)

    def link(a, b):
        return pltpu.make_async_remote_copy(
            src_ref=tile_ref,
            dst_ref=slots.at[1 - a, 1 - b],
            send_sem=send_sems.at[1 + a, 1 + b],
            recv_sem=recv_sems.at[1 - a, 1 - b],
            device_id=(req, row + a, col + b),
            device_id_type=MESH_IDS,
        )

    barrier = pltpu.get_barrier_semaphore()
    for a, b in offsets:
        @pl.when(present(a, b))
        def _():
            pl.semaphore_signal(barrier, inc=1, device_id=(req, row + a, col + b), device_id_type=MESH_IDS)
    up = (row + rows - 1) // rows
    down = (2 * rows - 2 - row) // rows
    left = (col + cols - 1) // cols
    right = (2 * cols - 2 - col) // cols
    pl.semaphore_wait(barrier, (1 + up + down) * (1 + left + right) - 1)
    for a, b in offsets:
        @pl.when(present(a, b))
        def _():
            link(a, b).start()
    for a, b in offsets:
        @pl.when(present(a, b))
        def _():
            copy = link(a, b)
            copy.wait_send()
            pltpu.make_async_remote_copy(
                src_ref=tile_ref,
                dst_ref=slots.at[1 + a, 1 + b],
                send_sem=send_sems.at[1 + a, 1 + b],
                recv_sem=recv_sems.at[1 + a, 1 + b],
                device_id=(req, row + a, col + b),
                device_id_type=MESH_IDS,
            ).wait_recv()
            out_ref[1 + a, 1 + b] = slots[1 + a, 1 + b]

        @pl.when(jnp.logical_not(present(a, b)))
        def _():
            out_ref[1 + a, 1 + b] = jnp.zeros(out_ref.shape[2:], out_ref.dtype)
    out_ref[1, 1] = tile_ref[...]


def halo_extend(tile):
    gathered = pl.pallas_call(
        halo_kernel,
        out_shape=jax.ShapeDtypeStruct((3, 3) + tile.shape, tile.dtype),
        in_specs=[pl.BlockSpec(memory_space=pltpu.VMEM)],
        out_specs=pl.BlockSpec(memory_space=pltpu.VMEM),
        scratch_shapes=[
            pltpu.VMEM((3, 3) + tile.shape, tile.dtype),
            pltpu.SemaphoreType.DMA((3, 3)),
            pltpu.SemaphoreType.DMA((3, 3)),
        ],
        compiler_params=pltpu.CompilerParams(collective_id=6, has_side_effects=True),
    )(tile)
    bands = []
    for a, pick_rows in ((0, slice(-1, None)), (1, slice(None)), (2, slice(0, 1))):
        pieces = [
            gathered[a, 0][:, pick_rows, -1:],
            gathered[a, 1][:, pick_rows, :],
            gathered[a, 2][:, pick_rows, :1],
        ]
        bands.append(jnp.concatenate(pieces, axis=2))
    return jnp.concatenate(bands, axis=1)


def prep_kernel(eps, raw_ref, q_gain_ref, k_gain_ref, q_ref, kv_ref):
    span = raw_ref.shape[1]
    lane = lax.broadcasted_iota(jnp.int32, (1, 128), 1)
    first = lane < 64
    kv_ref[...] = jnp.zeros(kv_ref.shape, kv_ref.dtype)
    for pair in range(raw_ref.shape[2] // 128):
        cols = slice(pair * 128, (pair + 1) * 128)
        for which, gain_ref in ((0, q_gain_ref), (1, k_gain_ref)):
            piece = raw_ref[which, :, cols]
            low = jnp.sum(jnp.where(first, piece, 0.0), axis=1, keepdims=True)
            high = jnp.sum(jnp.where(first, 0.0, piece), axis=1, keepdims=True)
            centered = piece - jnp.where(first, low, high) / 64.0
            squared = centered * centered
            low = jnp.sum(jnp.where(first, squared, 0.0), axis=1, keepdims=True)
            high = jnp.sum(jnp.where(first, 0.0, squared), axis=1, keepdims=True)
            spread = jnp.where(first, low, high) / 64.0
            normed = (centered * lax.rsqrt(spread + eps) * gain_ref[:, cols]).astype(jnp.bfloat16)
            if which == 0:
                q_ref[:, cols] = normed
            else:
                kv_ref[0, :span, cols] = normed
        kv_ref[1, :span, cols] = raw_ref[2, :, cols].astype(jnp.bfloat16)


def prep_heads(raw, q_gain, k_gain, padded_span):
    width = raw.shape[2]
    tiles = width // q_gain.shape[0]
    return pl.pallas_call(
        functools.partial(prep_kernel, 1e-06),
        out_shape=(
            jax.ShapeDtypeStruct((raw.shape[1], width), jnp.bfloat16),
            jax.ShapeDtypeStruct((2, padded_span, width), jnp.bfloat16),
        ),
        in_specs=[pl.BlockSpec(memory_space=pltpu.VMEM)] * 3,
        out_specs=(pl.BlockSpec(memory_space=pltpu.VMEM), pl.BlockSpec(memory_space=pltpu.VMEM)),
    )(raw, jnp.tile(q_gain, tiles)[None], jnp.tile(k_gain, tiles)[None])


def layer_norm(tensor, epsilon):
    average = jnp.mean(tensor, axis=-1, keepdims=True)
    centered = tensor - average
    spread = jnp.mean(centered * centered, axis=-1, keepdims=True)
    return centered * lax.rsqrt(spread + epsilon)


def modulate(tensor, offset, factor):
    return (layer_norm(tensor, 1e-05) * (1.0 + factor) + offset).astype(jnp.bfloat16)


def head_norm(tensor, scaling):
    return (layer_norm(tensor, 1e-06) * scaling).astype(jnp.bfloat16)


def pick_entry(entries, position):
    slot_ids = jnp.arange(entries.shape[0], dtype=jnp.int32)
    return jnp.sum(jnp.where(slot_ids == position, entries, jnp.zeros_like(entries)))


def solver_weights(step_index):
    plan = jnp.linspace(0.00085**0.5, 0.012**0.5, TRAIN_STEPS, dtype=jnp.float32) ** 2
    cumulative = jnp.cumprod(1.0 - plan)
    alpha_now = pick_entry(cumulative, step_index)
    alpha_prev = pick_entry(cumulative, step_index - STRIDE)
    root_now = jnp.sqrt(alpha_now)
    rest_now = jnp.sqrt(1.0 - alpha_now)
    root_prev = jnp.sqrt(alpha_prev)
    rest_prev = jnp.sqrt(1.0 - alpha_prev)
    return (
        root_prev * root_now + rest_prev * rest_now,
        rest_prev * root_now - root_prev * rest_now,
    )


def key_mask(count, owners, grid, text_len, span, block_tokens, tile, text_rows):
    positions = jnp.arange(count, dtype=jnp.int32)
    owner_row = positions // span
    within = positions % span
    is_video = within < block_tokens
    owner_col = within // tile
    local_ids = within % tile
    token_row = owner_row * TR + local_ids // TC % TR
    token_col = owner_col * TC + local_ids % TC
    text_index = owner_row * text_rows + within - block_tokens
    matches = jnp.arange(grid.shape[0], dtype=jnp.int32)[None, :] == owners[:, None]
    rows_live = jnp.sum(jnp.where(matches, grid[None, :, 0], 0), axis=1)
    cols_live = jnp.sum(jnp.where(matches, grid[None, :, 1], 0), axis=1)
    text_lens = jnp.sum(jnp.where(matches, text_len[None, :], 0), axis=1)
    video_live = (token_row[None, :] < rows_live[:, None]) & (
        token_col[None, :] < cols_live[:, None]
    )
    text_live = (text_index[None, :] < text_lens[:, None]) & (within < block_tokens + text_rows)[None, :]
    return jnp.where(is_video[None, :], video_live, text_live).astype(jnp.float32)


def projector(stacked, piece):
    return jnp.einsum("gld,cde->cgle", stacked, piece, preferred_element_type=jnp.float32)


def attention_step(queries, owners, grid, text_len, span, block_tokens, tile, text_rows):
    score_scale = queries.shape[3] ** (-0.5)

    def attend(carry, pieces, start):
        key_piece, value_piece = pieces
        live_keys = key_mask(
            key_piece.shape[1], owners, grid, text_len, span, block_tokens, tile, text_rows
        )
        scores = (
            jnp.einsum("gqhd,gkhd->gqhk", queries, key_piece, preferred_element_type=jnp.float32)
            * score_scale
        )
        raw_weights = jnp.exp(scores) * live_keys[:, None, None, :]
        weighted = jnp.einsum(
            "gqhk,gkhd->gqhd",
            raw_weights.astype(jnp.bfloat16),
            value_piece,
            preferred_element_type=jnp.float32,
        )
        return (weighted, jnp.sum(raw_weights, axis=3))

    return attend


def shards(
    hidden,
    text_hidden,
    text_len,
    grid,
    timestep,
    modulation,
    q_gain,
    k_gain,
    w_qkv,
    w_out,
    w_up,
    w_down,
    w_proj,
    latent,
    conv_w,
):
    col_count = lax.axis_size("col")
    request_id = lax.axis_index("req")
    row_id = lax.axis_index("row")
    col_id = lax.axis_index("col")
    block_tokens = hidden.shape[1]
    tile = block_tokens // col_count
    text_rows = text_hidden.shape[1]
    head_dim = q_gain.shape[0]
    adaptive = modulation[0]
    source = hidden[0].astype(jnp.float32)
    joined = jnp.concatenate(
        [
            modulate(source, adaptive[0], adaptive[1]),
            modulate(text_hidden[0].astype(jnp.float32), adaptive[0], adaptive[1]),
        ],
        axis=0,
    )
    span = joined.shape[0]
    stacked = joined[None]
    owners = jnp.reshape(request_id, (1,))
    half_cols = w_qkv.shape[2] // 2
    own_half = lax.dynamic_slice_in_dim(w_qkv, request_id * half_cols, half_cols, 2)
    gathered_half = lax.all_gather(own_half, "row", axis=1, tiled=True)
    half_heads = half_cols // head_dim

    both_rows = jnp.concatenate([joined, partner_swap(joined, 4)], axis=0)
    projected_rows = jnp.einsum("ld,cde->cle", both_rows, gathered_half, preferred_element_type=jnp.float32)
    own_raw = projected_rows[:, :span]
    received_raw = partner_swap(projected_rows[:, span:], 5)
    raw = jnp.concatenate(
        [jnp.where(request_id == 0, own_raw, received_raw), jnp.where(request_id == 0, received_raw, own_raw)], axis=2
    )
    heads_here = raw.shape[2] // head_dim
    padded_span = 16 * pl.cdiv(span, 16)
    all_queries, both = prep_heads(raw, q_gain, k_gain, padded_span)
    split_cols = both.shape[2] // 2
    first_kv = lax.all_gather(both[None, :, :, :split_cols], "row", axis=0, tiled=True)
    second_kv = ring_gather(both[:, :, split_cols:], 4, 8, 7)
    second_kv = second_kv.reshape((-1,) + second_kv.shape[2:])
    sources = first_kv.shape[0]
    live = key_mask(sources * padded_span, owners, grid, text_len, padded_span, block_tokens, tile, text_rows)
    second_live = live.reshape(4, sources // 4, padded_span).transpose(1, 0, 2).reshape(1, -1)
    attended = attention(all_queries[:block_tokens], first_kv, second_kv, live, second_live, head_dim ** (-0.5))
    partial_out = jnp.dot(attended, w_out, preferred_element_type=jnp.float32)
    projected = scatter_sum(partial_out.astype(jnp.bfloat16), "col", 1)
    own_rows = lax.dynamic_slice_in_dim(source, col_id * tile, tile, 0)
    mixed = lax.optimization_barrier(
        (own_rows + adaptive[2] * projected).astype(jnp.bfloat16)
    ).astype(jnp.float32)
    second_norm = modulate(mixed, adaptive[3], adaptive[4])
    hidden_units = jax.nn.gelu(
        jnp.dot(
            ring_gather(second_norm, 4, 8, 2).reshape(-1, second_norm.shape[1]),
            w_up,
            preferred_element_type=jnp.float32,
        ),
        approximate=True,
    ).astype(jnp.bfloat16)
    feed_terms = jnp.dot(hidden_units, w_down, preferred_element_type=jnp.float32)
    feed_out = ring_scatter_sum(feed_terms.astype(jnp.bfloat16), 4, 8, 0)
    out_hidden = (mixed + adaptive[5] * feed_out).astype(jnp.bfloat16)
    final_norm = modulate(out_hidden.astype(jnp.float32), adaptive[6], adaptive[7])
    velocity = jnp.dot(final_norm, w_proj, preferred_element_type=jnp.float32)
    local_ids = jnp.arange(tile, dtype=jnp.int32)
    token_row = row_id * TR + local_ids // TC % TR
    token_col = col_id * TC + local_ids % TC
    rows_live = pick_entry(grid[:, 0], request_id)
    cols_live = pick_entry(grid[:, 1], request_id)
    live_tokens = ((token_row < rows_live) & (token_col < cols_live)).astype(jnp.float32)
    keep_part, velocity_part = solver_weights(pick_entry(timestep, request_id))
    updated = (keep_part * latent[0] + velocity_part * velocity) * live_tokens[:, None]
    pixels = (
        updated.reshape(FR, TR, TC, CH, 2, 2)
        .transpose(0, 1, 4, 2, 5, 3)
        .reshape(FR, 2 * TR, 2 * TC, CH)
    )
    scaled = (pixels / latent_scale).astype(jnp.bfloat16)
    padded = halo_extend(scaled)
    running = jnp.zeros((FR, 2 * TR, 2 * TC, conv_w.shape[3]), jnp.float32)
    for row_tap in range(3):
        for col_tap in range(3):
            window = padded[:, row_tap : row_tap + 2 * TR, col_tap : col_tap + 2 * TC, :]
            running = running + jnp.einsum(
                "fyxc,cd->fyxd",
                window,
                conv_w[row_tap, col_tap],
                preferred_element_type=jnp.float32,
            )
    return (out_hidden[None], updated[None], running.astype(jnp.bfloat16)[None])


def solution(mesh):
    placed = (
        P("req", "row", None),
        P("req", "row", None),
        P(),
        P(),
        P(),
        P("req", None, None),
        P(),
        P(),
        P(None, "row", "col"),
        P("col", None),
        P(None, "row"),
        P("row", None),
        P(),
        P("req", ("row", "col"), None),
        P(),
    )
    return jax.shard_map(
        shards,
        mesh=mesh,
        in_specs=placed,
        out_specs=(
            P("req", ("row", "col"), None),
            P("req", ("row", "col"), None),
            P("req", None, "row", "col", None),
        ),
        check_vma=False,
    )
```

```python
import functools

import jax
import jax.numpy as jnp
from jax import lax
from jax.sharding import PartitionSpec as P
from jax.experimental import pallas as pl
from jax.experimental.pallas import tpu as pltpu

MESH_IDS = pl.DeviceIdType.MESH

CH = 16
FR = 6
TR = 1
TC = 4
TRAIN_STEPS = 1000
STRIDE = 250


latent_scale = 0.7


def extended(cells, sides, width):
    for axis, dim in sides:
        count = lax.axis_size(axis)
        ends = count - 1
        head = lax.slice_in_dim(cells, 0, width, axis=dim)
        tail = lax.slice_in_dim(cells, cells.shape[dim] - width, cells.shape[dim], axis=dim)
        cells = jnp.concatenate(
            [
                lax.ppermute(tail, axis, [(i, (i + 1) % count) for i in range(ends)]),
                cells,
                lax.ppermute(head, axis, [((i + 1) % count, i) for i in range(ends)]),
            ],
            axis=dim,
        )
    return cells


def peer_on(axis, peer):
    return tuple(peer if name == axis else lax.axis_index(name) for name in ("req", "row", "col"))


def scatter_sum_kernel(axis, count, rows, part_ref, out_ref, landed, send_sems, recv_sems, own_sem):
    me = lax.axis_index(axis)
    barrier = pltpu.get_barrier_semaphore()
    for step in range(1, count):
        peer = lax.rem(me + step, count)
        pl.semaphore_signal(barrier, inc=1, device_id=peer_on(axis, peer), device_id_type=MESH_IDS)
    pl.semaphore_wait(barrier, count - 1)
    own = pltpu.make_async_copy(part_ref.at[pl.ds(me * rows, rows)], landed.at[me], own_sem)
    own.start()
    sends = []
    for step in range(1, count):
        peer = lax.rem(me + step, count)
        copy = pltpu.make_async_remote_copy(
            src_ref=part_ref.at[pl.ds(peer * rows, rows)],
            dst_ref=landed.at[me],
            send_sem=send_sems.at[step],
            recv_sem=recv_sems.at[step],
            device_id=peer_on(axis, peer),
            device_id_type=MESH_IDS,
        )
        copy.start()
        sends.append(copy)
    own.wait()
    for step in range(1, count):
        source = lax.rem(me + count - step, count)
        pltpu.make_async_remote_copy(
            src_ref=part_ref.at[pl.ds(me * rows, rows)],
            dst_ref=landed.at[source],
            send_sem=send_sems.at[step],
            recv_sem=recv_sems.at[step],
            device_id=peer_on(axis, source),
            device_id_type=MESH_IDS,
        ).wait_recv()
    for copy in sends:
        copy.wait_send()
    total = landed[0].astype(jnp.float32)
    for slot in range(1, count):
        total = total + landed[slot].astype(jnp.float32)
    out_ref[...] = total


def scatter_sum(part, axis, kernel_id):
    count = lax.axis_size(axis)
    rows = part.shape[0] // count
    width = part.shape[1]
    return pl.pallas_call(
        functools.partial(scatter_sum_kernel, axis, count, rows),
        out_shape=jax.ShapeDtypeStruct((rows, width), jnp.float32),
        in_specs=[pl.BlockSpec(memory_space=pl.ANY)],
        out_specs=pl.BlockSpec(memory_space=pltpu.VMEM),
        scratch_shapes=[
            pltpu.VMEM((count, rows, width), part.dtype),
            pltpu.SemaphoreType.DMA((count,)),
            pltpu.SemaphoreType.DMA((count,)),
            pltpu.SemaphoreType.DMA(()),
        ],
        compiler_params=pltpu.CompilerParams(
            collective_id=kernel_id, has_side_effects=True, vmem_limit_bytes=48 * 1024 * 1024
        ),
    )(part)


def attention_kernel(scale, q_ref, kv_ref, live_ref, out_ref):
    sources, _, block, width = kv_ref.shape
    lane = lax.broadcasted_iota(jnp.int32, (1, 128), 1)
    first = lane < 64
    live = live_ref[...]
    for pair in range(width // 128):
        cols = slice(pair * 128, (pair + 1) * 128)
        query = q_ref[:, cols]
        keys = kv_ref[:, 0, :, cols].reshape(sources * block, 128)
        values = kv_ref[:, 1, :, cols].reshape(sources * block, 128)
        rows = query.shape[0]
        zeros = jnp.zeros_like(query)
        picked = jnp.concatenate([jnp.where(first, query, zeros), jnp.where(first, zeros, query)], axis=0)
        scores = lax.dot_general(
            picked, keys, (((1,), (1,)), ((), ())), preferred_element_type=jnp.float32
        ) * scale
        weights = jnp.exp(scores) * live
        totals = jnp.sum(weights, axis=1, keepdims=True)
        summed = jnp.dot(weights.astype(jnp.bfloat16), values, preferred_element_type=jnp.float32) / totals
        out_ref[:, cols] = jnp.where(first, summed[:rows], summed[rows:]).astype(out_ref.dtype)


def attention(queries, gathered, live, scale):
    return pl.pallas_call(
        functools.partial(attention_kernel, scale),
        out_shape=jax.ShapeDtypeStruct(queries.shape, jnp.bfloat16),
        in_specs=[pl.BlockSpec(memory_space=pltpu.VMEM)] * 3,
        out_specs=pl.BlockSpec(memory_space=pltpu.VMEM),
        compiler_params=pltpu.CompilerParams(vmem_limit_bytes=56 * 1024 * 1024),
    )(queries, gathered, live)


def ring_scatter_kernel(zs, xs, part_ref, out_ref, landed, outgoing, own_sum, crossed, ring_send, ring_recv, cross_send, cross_recv):
    me = lax.axis_index("row")
    xm = me // zs
    zm = me % zs
    ahead = xm * zs + lax.rem(zm + 1, zs)
    behind = xm * zs + lax.rem(zm + zs - 1, zs)
    half = part_ref.shape[3] // 2
    barrier = pltpu.get_barrier_semaphore()
    targets = [ahead, behind] + [lax.rem(xm + k, xs) * zs + zm for k in range(1, xs)]
    for peer in targets:
        pl.semaphore_signal(barrier, inc=1, device_id=peer_on("row", peer), device_id_type=MESH_IDS)
    pl.semaphore_wait(barrier, len(targets))
    ways = ((0, ahead, behind, -1), (1, behind, ahead, 1))
    pending = []
    for step in range(zs - 1):
        for way, dest, origin, sign in ways:
            cols = pl.ds(way * half, half)
            chunk = lax.rem(zm + sign * (1 + step) + 2 * zs, zs)
            if step == 0:
                source = part_ref.at[chunk, :, :, cols]
            else:
                arrived = pltpu.make_async_remote_copy(
                    src_ref=outgoing.at[way, step - 1],
                    dst_ref=landed.at[way, step - 1],
                    send_sem=ring_send.at[way, step - 1],
                    recv_sem=ring_recv.at[way, step - 1],
                    device_id=peer_on("row", origin),
                    device_id_type=MESH_IDS,
                )
                arrived.wait_recv()
                outgoing[way, step] = (
                    landed[way, step - 1].astype(jnp.float32)
                    + part_ref[chunk, :, :, cols].astype(jnp.float32)
                ).astype(outgoing.dtype)
                source = outgoing.at[way, step]
            copy = pltpu.make_async_remote_copy(
                src_ref=source,
                dst_ref=landed.at[way, step],
                send_sem=ring_send.at[way, step],
                recv_sem=ring_recv.at[way, step],
                device_id=peer_on("row", dest),
                device_id_type=MESH_IDS,
            )
            copy.start()
            pending.append(copy)
    last = zs - 2
    for way, dest, origin, sign in ways:
        cols = pl.ds(way * half, half)
        pltpu.make_async_remote_copy(
            src_ref=outgoing.at[way, last],
            dst_ref=landed.at[way, last],
            send_sem=ring_send.at[way, last],
            recv_sem=ring_recv.at[way, last],
            device_id=peer_on("row", origin),
            device_id_type=MESH_IDS,
        ).wait_recv()
        own_sum[:, :, cols] = landed[way, last].astype(jnp.float32) + part_ref[zm, :, :, cols].astype(jnp.float32)
    crossed[0] = own_sum[...].astype(crossed.dtype)
    sends = []
    for k in range(1, xs):
        peer_x = lax.rem(xm + k, xs)
        copy = pltpu.make_async_remote_copy(
            src_ref=crossed.at[0, peer_x],
            dst_ref=crossed.at[k, 0],
            send_sem=cross_send.at[k],
            recv_sem=cross_recv.at[k],
            device_id=peer_on("row", peer_x * zs + zm),
            device_id_type=MESH_IDS,
        )
        copy.start()
        sends.append(copy)
    total = own_sum[xm]
    for k in range(1, xs):
        origin_x = lax.rem(xm + xs - k, xs)
        pltpu.make_async_remote_copy(
            src_ref=crossed.at[0, 0],
            dst_ref=crossed.at[k, 0],
            send_sem=cross_send.at[k],
            recv_sem=cross_recv.at[k],
            device_id=peer_on("row", origin_x * zs + zm),
            device_id_type=MESH_IDS,
        ).wait_recv()
        total = total + crossed[k, 0].astype(jnp.float32)
    out_ref[...] = total
    for copy in pending + sends:
        copy.wait_send()


def ring_scatter_sum(part, xs, zs, kernel_id):
    rows = part.shape[0] // (xs * zs)
    width = part.shape[1]
    arranged = part.reshape(zs, xs, rows, width)
    return pl.pallas_call(
        functools.partial(ring_scatter_kernel, zs, xs),
        out_shape=jax.ShapeDtypeStruct((rows, width), jnp.float32),
        in_specs=[pl.BlockSpec(memory_space=pltpu.VMEM)],
        out_specs=pl.BlockSpec(memory_space=pltpu.VMEM),
        scratch_shapes=[
            pltpu.VMEM((2, zs - 1, xs, rows, width // 2), part.dtype),
            pltpu.VMEM((2, zs - 1, xs, rows, width // 2), part.dtype),
            pltpu.VMEM((xs, rows, width), jnp.float32),
            pltpu.VMEM((xs, xs, rows, width), part.dtype),
            pltpu.SemaphoreType.DMA((2, zs - 1)),
            pltpu.SemaphoreType.DMA((2, zs - 1)),
            pltpu.SemaphoreType.DMA((xs,)),
            pltpu.SemaphoreType.DMA((xs,)),
        ],
        compiler_params=pltpu.CompilerParams(
            collective_id=kernel_id, has_side_effects=True, vmem_limit_bytes=56 * 1024 * 1024
        ),
    )(arranged)


def ring_gather_kernel(zs, xs, block_ref, out_ref, held, own_sem, ring_send, ring_recv, cross_send, cross_recv):
    me = lax.axis_index("row")
    xm = me // zs
    zm = me % zs
    ahead = xm * zs + lax.rem(zm + 1, zs)
    behind = xm * zs + lax.rem(zm + zs - 1, zs)
    barrier = pltpu.get_barrier_semaphore()
    targets = [ahead, behind] + [lax.rem(xm + k, xs) * zs + zm for k in range(1, xs)]
    for peer in targets:
        pl.semaphore_signal(barrier, inc=1, device_id=peer_on("row", peer), device_id_type=MESH_IDS)
    pl.semaphore_wait(barrier, len(targets))
    own = pltpu.make_async_copy(block_ref, held.at[zm, xm], own_sem)
    own.start()
    pending = []
    for k in range(1, xs):
        peer_x = lax.rem(xm + k, xs)
        copy = pltpu.make_async_remote_copy(
            src_ref=block_ref,
            dst_ref=held.at[zm, xm],
            send_sem=cross_send.at[k],
            recv_sem=cross_recv.at[k],
            device_id=peer_on("row", peer_x * zs + zm),
            device_id_type=MESH_IDS,
        )
        copy.start()
        pending.append(copy)
    own.wait()
    for k in range(1, xs):
        origin_x = lax.rem(xm + xs - k, xs)
        pltpu.make_async_remote_copy(
            src_ref=block_ref,
            dst_ref=held.at[zm, origin_x],
            send_sem=cross_send.at[k],
            recv_sem=cross_recv.at[k],
            device_id=peer_on("row", origin_x * zs + zm),
            device_id_type=MESH_IDS,
        ).wait_recv()
    split = xs // 2
    ways = ((0, ahead, behind, -1, pl.ds(0, split)), (1, behind, ahead, 1, pl.ds(split, xs - split)))
    for step in range(zs):
        for way, dest, origin, sign, part in ways:
            group = lax.rem(zm + sign * step + zs, zs)
            if step > 0:
                pltpu.make_async_remote_copy(
                    src_ref=held.at[group, part],
                    dst_ref=held.at[group, part],
                    send_sem=ring_send.at[way, step - 1],
                    recv_sem=ring_recv.at[way, step - 1],
                    device_id=peer_on("row", origin),
                    device_id_type=MESH_IDS,
                ).wait_recv()
            if step < zs - 1:
                copy = pltpu.make_async_remote_copy(
                    src_ref=held.at[group, part],
                    dst_ref=held.at[group, part],
                    send_sem=ring_send.at[way, step],
                    recv_sem=ring_recv.at[way, step],
                    device_id=peer_on("row", dest),
                    device_id_type=MESH_IDS,
                )
                copy.start()
                pending.append(copy)
    for copy in pending:
        copy.wait_send()
    out = pltpu.make_async_copy(held, out_ref, own_sem)
    out.start()
    out.wait()


def ring_gather(block, xs, zs, kernel_id):
    return pl.pallas_call(
        functools.partial(ring_gather_kernel, zs, xs),
        out_shape=jax.ShapeDtypeStruct((zs, xs) + block.shape, block.dtype),
        in_specs=[pl.BlockSpec(memory_space=pltpu.VMEM)],
        out_specs=pl.BlockSpec(memory_space=pl.ANY),
        scratch_shapes=[
            pltpu.VMEM((zs, xs) + block.shape, block.dtype),
            pltpu.SemaphoreType.DMA(()),
            pltpu.SemaphoreType.DMA((2, zs - 1)),
            pltpu.SemaphoreType.DMA((2, zs - 1)),
            pltpu.SemaphoreType.DMA((xs,)),
            pltpu.SemaphoreType.DMA((xs,)),
        ],
        compiler_params=pltpu.CompilerParams(
            collective_id=kernel_id, has_side_effects=True, vmem_limit_bytes=56 * 1024 * 1024
        ),
    )(block)


def swap_kernel(src_ref, out_ref, landed, sems):
    other = 1 - lax.axis_index("req")
    barrier = pltpu.get_barrier_semaphore()
    pl.semaphore_signal(barrier, inc=1, device_id=peer_on("req", other), device_id_type=MESH_IDS)
    pl.semaphore_wait(barrier, 1)
    copy = pltpu.make_async_remote_copy(
        src_ref=src_ref,
        dst_ref=landed,
        send_sem=sems.at[0],
        recv_sem=sems.at[1],
        device_id=peer_on("req", other),
        device_id_type=MESH_IDS,
    )
    copy.start()
    copy.wait_send()
    copy.wait_recv()
    out_ref[...] = landed[...]


def partner_swap(value, kernel_id):
    return pl.pallas_call(
        swap_kernel,
        out_shape=jax.ShapeDtypeStruct(value.shape, value.dtype),
        in_specs=[pl.BlockSpec(memory_space=pltpu.VMEM)],
        out_specs=pl.BlockSpec(memory_space=pltpu.VMEM),
        scratch_shapes=[pltpu.VMEM(value.shape, value.dtype), pltpu.SemaphoreType.DMA((2,))],
        compiler_params=pltpu.CompilerParams(collective_id=kernel_id, has_side_effects=True),
    )(value)


def halo_kernel(tile_ref, out_ref, slots, send_sems, recv_sems):
    req = lax.axis_index("req")
    row = lax.axis_index("row")
    col = lax.axis_index("col")
    rows = lax.axis_size("row")
    cols = lax.axis_size("col")
    offsets = [(a, b) for a in (-1, 0, 1) for b in (-1, 0, 1) if (a, b) != (0, 0)]

    def present(a, b):
        return (row + a >= 0) & (row + a < rows) & (col + b >= 0) & (col + b < cols)

    def link(a, b):
        return pltpu.make_async_remote_copy(
            src_ref=tile_ref,
            dst_ref=slots.at[1 - a, 1 - b],
            send_sem=send_sems.at[1 + a, 1 + b],
            recv_sem=recv_sems.at[1 - a, 1 - b],
            device_id=(req, row + a, col + b),
            device_id_type=MESH_IDS,
        )

    barrier = pltpu.get_barrier_semaphore()
    for a, b in offsets:
        @pl.when(present(a, b))
        def _():
            pl.semaphore_signal(barrier, inc=1, device_id=(req, row + a, col + b), device_id_type=MESH_IDS)
    up = (row + rows - 1) // rows
    down = (2 * rows - 2 - row) // rows
    left = (col + cols - 1) // cols
    right = (2 * cols - 2 - col) // cols
    pl.semaphore_wait(barrier, (1 + up + down) * (1 + left + right) - 1)
    for a, b in offsets:
        @pl.when(present(a, b))
        def _():
            link(a, b).start()
    for a, b in offsets:
        @pl.when(present(a, b))
        def _():
            copy = link(a, b)
            copy.wait_send()
            pltpu.make_async_remote_copy(
                src_ref=tile_ref,
                dst_ref=slots.at[1 + a, 1 + b],
                send_sem=send_sems.at[1 + a, 1 + b],
                recv_sem=recv_sems.at[1 + a, 1 + b],
                device_id=(req, row + a, col + b),
                device_id_type=MESH_IDS,
            ).wait_recv()
            out_ref[1 + a, 1 + b] = slots[1 + a, 1 + b]

        @pl.when(jnp.logical_not(present(a, b)))
        def _():
            out_ref[1 + a, 1 + b] = jnp.zeros(out_ref.shape[2:], out_ref.dtype)
    out_ref[1, 1] = tile_ref[...]


def halo_extend(tile):
    gathered = pl.pallas_call(
        halo_kernel,
        out_shape=jax.ShapeDtypeStruct((3, 3) + tile.shape, tile.dtype),
        in_specs=[pl.BlockSpec(memory_space=pltpu.VMEM)],
        out_specs=pl.BlockSpec(memory_space=pltpu.VMEM),
        scratch_shapes=[
            pltpu.VMEM((3, 3) + tile.shape, tile.dtype),
            pltpu.SemaphoreType.DMA((3, 3)),
            pltpu.SemaphoreType.DMA((3, 3)),
        ],
        compiler_params=pltpu.CompilerParams(collective_id=6, has_side_effects=True),
    )(tile)
    bands = []
    for a, pick_rows in ((0, slice(-1, None)), (1, slice(None)), (2, slice(0, 1))):
        pieces = [
            gathered[a, 0][:, pick_rows, -1:],
            gathered[a, 1][:, pick_rows, :],
            gathered[a, 2][:, pick_rows, :1],
        ]
        bands.append(jnp.concatenate(pieces, axis=2))
    return jnp.concatenate(bands, axis=1)


def prep_kernel(eps, raw_ref, q_gain_ref, k_gain_ref, q_ref, kv_ref):
    span = raw_ref.shape[1]
    lane = lax.broadcasted_iota(jnp.int32, (1, 128), 1)
    first = lane < 64
    kv_ref[...] = jnp.zeros(kv_ref.shape, kv_ref.dtype)
    for pair in range(raw_ref.shape[2] // 128):
        cols = slice(pair * 128, (pair + 1) * 128)
        for which, gain_ref in ((0, q_gain_ref), (1, k_gain_ref)):
            piece = raw_ref[which, :, cols]
            low = jnp.sum(jnp.where(first, piece, 0.0), axis=1, keepdims=True)
            high = jnp.sum(jnp.where(first, 0.0, piece), axis=1, keepdims=True)
            centered = piece - jnp.where(first, low, high) / 64.0
            squared = centered * centered
            low = jnp.sum(jnp.where(first, squared, 0.0), axis=1, keepdims=True)
            high = jnp.sum(jnp.where(first, 0.0, squared), axis=1, keepdims=True)
            spread = jnp.where(first, low, high) / 64.0
            normed = (centered * lax.rsqrt(spread + eps) * gain_ref[:, cols]).astype(jnp.bfloat16)
            if which == 0:
                q_ref[:, cols] = normed
            else:
                kv_ref[0, :span, cols] = normed
        kv_ref[1, :span, cols] = raw_ref[2, :, cols].astype(jnp.bfloat16)


def prep_heads(raw, q_gain, k_gain, padded_span):
    width = raw.shape[2]
    tiles = width // q_gain.shape[0]
    return pl.pallas_call(
        functools.partial(prep_kernel, 1e-06),
        out_shape=(
            jax.ShapeDtypeStruct((raw.shape[1], width), jnp.bfloat16),
            jax.ShapeDtypeStruct((2, padded_span, width), jnp.bfloat16),
        ),
        in_specs=[pl.BlockSpec(memory_space=pltpu.VMEM)] * 3,
        out_specs=(pl.BlockSpec(memory_space=pltpu.VMEM), pl.BlockSpec(memory_space=pltpu.VMEM)),
    )(raw, jnp.tile(q_gain, tiles)[None], jnp.tile(k_gain, tiles)[None])


def layer_norm(tensor, epsilon):
    average = jnp.mean(tensor, axis=-1, keepdims=True)
    centered = tensor - average
    spread = jnp.mean(centered * centered, axis=-1, keepdims=True)
    return centered * lax.rsqrt(spread + epsilon)


def modulate(tensor, offset, factor):
    return (layer_norm(tensor, 1e-05) * (1.0 + factor) + offset).astype(jnp.bfloat16)


def head_norm(tensor, scaling):
    return (layer_norm(tensor, 1e-06) * scaling).astype(jnp.bfloat16)


def pick_entry(entries, position):
    slot_ids = jnp.arange(entries.shape[0], dtype=jnp.int32)
    return jnp.sum(jnp.where(slot_ids == position, entries, jnp.zeros_like(entries)))


def solver_weights(step_index):
    plan = jnp.linspace(0.00085**0.5, 0.012**0.5, TRAIN_STEPS, dtype=jnp.float32) ** 2
    cumulative = jnp.cumprod(1.0 - plan)
    alpha_now = pick_entry(cumulative, step_index)
    alpha_prev = pick_entry(cumulative, step_index - STRIDE)
    root_now = jnp.sqrt(alpha_now)
    rest_now = jnp.sqrt(1.0 - alpha_now)
    root_prev = jnp.sqrt(alpha_prev)
    rest_prev = jnp.sqrt(1.0 - alpha_prev)
    return (
        root_prev * root_now + rest_prev * rest_now,
        rest_prev * root_now - root_prev * rest_now,
    )


def key_mask(count, owners, grid, text_len, span, block_tokens, tile, text_rows):
    positions = jnp.arange(count, dtype=jnp.int32)
    owner_row = positions // span
    within = positions % span
    is_video = within < block_tokens
    owner_col = within // tile
    local_ids = within % tile
    token_row = owner_row * TR + local_ids // TC % TR
    token_col = owner_col * TC + local_ids % TC
    text_index = owner_row * text_rows + within - block_tokens
    matches = jnp.arange(grid.shape[0], dtype=jnp.int32)[None, :] == owners[:, None]
    rows_live = jnp.sum(jnp.where(matches, grid[None, :, 0], 0), axis=1)
    cols_live = jnp.sum(jnp.where(matches, grid[None, :, 1], 0), axis=1)
    text_lens = jnp.sum(jnp.where(matches, text_len[None, :], 0), axis=1)
    video_live = (token_row[None, :] < rows_live[:, None]) & (
        token_col[None, :] < cols_live[:, None]
    )
    text_live = (text_index[None, :] < text_lens[:, None]) & (within < block_tokens + text_rows)[None, :]
    return jnp.where(is_video[None, :], video_live, text_live).astype(jnp.float32)


def projector(stacked, piece):
    return jnp.einsum("gld,cde->cgle", stacked, piece, preferred_element_type=jnp.float32)


def attention_step(queries, owners, grid, text_len, span, block_tokens, tile, text_rows):
    score_scale = queries.shape[3] ** (-0.5)

    def attend(carry, pieces, start):
        key_piece, value_piece = pieces
        live_keys = key_mask(
            key_piece.shape[1], owners, grid, text_len, span, block_tokens, tile, text_rows
        )
        scores = (
            jnp.einsum("gqhd,gkhd->gqhk", queries, key_piece, preferred_element_type=jnp.float32)
            * score_scale
        )
        raw_weights = jnp.exp(scores) * live_keys[:, None, None, :]
        weighted = jnp.einsum(
            "gqhk,gkhd->gqhd",
            raw_weights.astype(jnp.bfloat16),
            value_piece,
            preferred_element_type=jnp.float32,
        )
        return (weighted, jnp.sum(raw_weights, axis=3))

    return attend


def shards(
    hidden,
    text_hidden,
    text_len,
    grid,
    timestep,
    modulation,
    q_gain,
    k_gain,
    w_qkv,
    w_out,
    w_up,
    w_down,
    w_proj,
    latent,
    conv_w,
):
    col_count = lax.axis_size("col")
    request_id = lax.axis_index("req")
    row_id = lax.axis_index("row")
    col_id = lax.axis_index("col")
    block_tokens = hidden.shape[1]
    tile = block_tokens // col_count
    text_rows = text_hidden.shape[1]
    head_dim = q_gain.shape[0]
    adaptive = modulation[0]
    source = hidden[0].astype(jnp.float32)
    joined = jnp.concatenate(
        [
            modulate(source, adaptive[0], adaptive[1]),
            modulate(text_hidden[0].astype(jnp.float32), adaptive[0], adaptive[1]),
        ],
        axis=0,
    )
    span = joined.shape[0]
    stacked = joined[None]
    owners = jnp.reshape(request_id, (1,))
    half_cols = w_qkv.shape[2] // 2
    own_half = lax.dynamic_slice_in_dim(w_qkv, request_id * half_cols, half_cols, 2)
    gathered_half = lax.all_gather(own_half, "row", axis=1, tiled=True)
    half_heads = half_cols // head_dim

    both_rows = jnp.concatenate([joined, partner_swap(joined, 4)], axis=0)
    projected_rows = jnp.einsum("ld,cde->cle", both_rows, gathered_half, preferred_element_type=jnp.float32)
    own_raw = projected_rows[:, :span]
    received_raw = partner_swap(projected_rows[:, span:], 5)
    raw = jnp.concatenate(
        [jnp.where(request_id == 0, own_raw, received_raw), jnp.where(request_id == 0, received_raw, own_raw)], axis=2
    )
    heads_here = raw.shape[2] // head_dim
    padded_span = 16 * pl.cdiv(span, 16)
    all_queries, both = prep_heads(raw, q_gain, k_gain, padded_span)
    gathered = lax.all_gather(both[None], "row", axis=0, tiled=True)
    live = key_mask(
        gathered.shape[0] * padded_span, owners, grid, text_len, padded_span, block_tokens, tile, text_rows
    )
    attended = attention(all_queries[:block_tokens], gathered, live, head_dim ** (-0.5))
    partial_out = jnp.dot(attended, w_out, preferred_element_type=jnp.float32)
    projected = scatter_sum(partial_out.astype(jnp.bfloat16), "col", 1)
    own_rows = lax.dynamic_slice_in_dim(source, col_id * tile, tile, 0)
    mixed = lax.optimization_barrier(
        (own_rows + adaptive[2] * projected).astype(jnp.bfloat16)
    ).astype(jnp.float32)
    second_norm = modulate(mixed, adaptive[3], adaptive[4])
    hidden_units = jax.nn.gelu(
        jnp.dot(
            ring_gather(second_norm, 4, 8, 2).reshape(-1, second_norm.shape[1]),
            w_up,
            preferred_element_type=jnp.float32,
        ),
        approximate=True,
    ).astype(jnp.bfloat16)
    feed_terms = jnp.dot(hidden_units, w_down, preferred_element_type=jnp.float32)
    feed_out = ring_scatter_sum(feed_terms.astype(jnp.bfloat16), 4, 8, 0)
    out_hidden = (mixed + adaptive[5] * feed_out).astype(jnp.bfloat16)
    final_norm = modulate(out_hidden.astype(jnp.float32), adaptive[6], adaptive[7])
    velocity = jnp.dot(final_norm, w_proj, preferred_element_type=jnp.float32)
    local_ids = jnp.arange(tile, dtype=jnp.int32)
    token_row = row_id * TR + local_ids // TC % TR
    token_col = col_id * TC + local_ids % TC
    rows_live = pick_entry(grid[:, 0], request_id)
    cols_live = pick_entry(grid[:, 1], request_id)
    live_tokens = ((token_row < rows_live) & (token_col < cols_live)).astype(jnp.float32)
    keep_part, velocity_part = solver_weights(pick_entry(timestep, request_id))
    updated = (keep_part * latent[0] + velocity_part * velocity) * live_tokens[:, None]
    pixels = (
        updated.reshape(FR, TR, TC, CH, 2, 2)
        .transpose(0, 1, 4, 2, 5, 3)
        .reshape(FR, 2 * TR, 2 * TC, CH)
    )
    scaled = (pixels / latent_scale).astype(jnp.bfloat16)
    padded = halo_extend(scaled)
    running = jnp.zeros((FR, 2 * TR, 2 * TC, conv_w.shape[3]), jnp.float32)
    for row_tap in range(3):
        for col_tap in range(3):
            window = padded[:, row_tap : row_tap + 2 * TR, col_tap : col_tap + 2 * TC, :]
            running = running + jnp.einsum(
                "fyxc,cd->fyxd",
                window,
                conv_w[row_tap, col_tap],
                preferred_element_type=jnp.float32,
            )
    return (out_hidden[None], updated[None], running.astype(jnp.bfloat16)[None])


def solution(mesh):
    placed = (
        P("req", "row", None),
        P("req", "row", None),
        P(),
        P(),
        P(),
        P("req", None, None),
        P(),
        P(),
        P(None, "row", "col"),
        P("col", None),
        P(None, "row"),
        P("row", None),
        P(),
        P("req", ("row", "col"), None),
        P(),
    )
    return jax.shard_map(
        shards,
        mesh=mesh,
        in_specs=placed,
        out_specs=(
            P("req", ("row", "col"), None),
            P("req", ("row", "col"), None),
            P("req", None, "row", "col", None),
        ),
        check_vma=False,
    )
```

```python
import functools

import jax
import jax.numpy as jnp
from jax import lax
from jax.sharding import PartitionSpec as P
from jax.experimental import pallas as pl
from jax.experimental.pallas import tpu as pltpu

MESH_IDS = pl.DeviceIdType.MESH

CH = 16
FR = 6
TR = 1
TC = 4
TRAIN_STEPS = 1000
STRIDE = 250


latent_scale = 0.7


def extended(cells, sides, width):
    for axis, dim in sides:
        count = lax.axis_size(axis)
        ends = count - 1
        head = lax.slice_in_dim(cells, 0, width, axis=dim)
        tail = lax.slice_in_dim(cells, cells.shape[dim] - width, cells.shape[dim], axis=dim)
        cells = jnp.concatenate(
            [
                lax.ppermute(tail, axis, [(i, (i + 1) % count) for i in range(ends)]),
                cells,
                lax.ppermute(head, axis, [((i + 1) % count, i) for i in range(ends)]),
            ],
            axis=dim,
        )
    return cells


def peer_on(axis, peer):
    return tuple(peer if name == axis else lax.axis_index(name) for name in ("req", "row", "col"))


def scatter_sum_kernel(axis, count, rows, part_ref, out_ref, landed, send_sems, recv_sems, own_sem):
    me = lax.axis_index(axis)
    barrier = pltpu.get_barrier_semaphore()
    for step in range(1, count):
        peer = lax.rem(me + step, count)
        pl.semaphore_signal(barrier, inc=1, device_id=peer_on(axis, peer), device_id_type=MESH_IDS)
    pl.semaphore_wait(barrier, count - 1)
    own = pltpu.make_async_copy(part_ref.at[pl.ds(me * rows, rows)], landed.at[me], own_sem)
    own.start()
    sends = []
    for step in range(1, count):
        peer = lax.rem(me + step, count)
        copy = pltpu.make_async_remote_copy(
            src_ref=part_ref.at[pl.ds(peer * rows, rows)],
            dst_ref=landed.at[me],
            send_sem=send_sems.at[step],
            recv_sem=recv_sems.at[step],
            device_id=peer_on(axis, peer),
            device_id_type=MESH_IDS,
        )
        copy.start()
        sends.append(copy)
    own.wait()
    for step in range(1, count):
        source = lax.rem(me + count - step, count)
        pltpu.make_async_remote_copy(
            src_ref=part_ref.at[pl.ds(me * rows, rows)],
            dst_ref=landed.at[source],
            send_sem=send_sems.at[step],
            recv_sem=recv_sems.at[step],
            device_id=peer_on(axis, source),
            device_id_type=MESH_IDS,
        ).wait_recv()
    for copy in sends:
        copy.wait_send()
    total = landed[0].astype(jnp.float32)
    for slot in range(1, count):
        total = total + landed[slot].astype(jnp.float32)
    out_ref[...] = total


def scatter_sum(part, axis, kernel_id):
    count = lax.axis_size(axis)
    rows = part.shape[0] // count
    width = part.shape[1]
    return pl.pallas_call(
        functools.partial(scatter_sum_kernel, axis, count, rows),
        out_shape=jax.ShapeDtypeStruct((rows, width), jnp.float32),
        in_specs=[pl.BlockSpec(memory_space=pltpu.VMEM)],
        out_specs=pl.BlockSpec(memory_space=pltpu.VMEM),
        scratch_shapes=[
            pltpu.VMEM((count, rows, width), part.dtype),
            pltpu.SemaphoreType.DMA((count,)),
            pltpu.SemaphoreType.DMA((count,)),
            pltpu.SemaphoreType.DMA(()),
        ],
        compiler_params=pltpu.CompilerParams(
            collective_id=kernel_id, has_side_effects=True, vmem_limit_bytes=48 * 1024 * 1024
        ),
    )(part)


def attention_kernel(scale, q_ref, kv_ref, live_ref, out_ref):
    sources, _, block, width = kv_ref.shape
    lane = lax.broadcasted_iota(jnp.int32, (1, 128), 1)
    first = lane < 64
    live = live_ref[...]
    for pair in range(width // 128):
        cols = slice(pair * 128, (pair + 1) * 128)
        query = q_ref[:, cols]
        keys = kv_ref[:, 0, :, cols].reshape(sources * block, 128)
        values = kv_ref[:, 1, :, cols].reshape(sources * block, 128)
        rows = query.shape[0]
        zeros = jnp.zeros_like(query)
        picked = jnp.concatenate([jnp.where(first, query, zeros), jnp.where(first, zeros, query)], axis=0)
        scores = lax.dot_general(
            picked, keys, (((1,), (1,)), ((), ())), preferred_element_type=jnp.float32
        ) * scale
        weights = jnp.exp(scores) * live
        totals = jnp.sum(weights, axis=1, keepdims=True)
        summed = jnp.dot(weights.astype(jnp.bfloat16), values, preferred_element_type=jnp.float32) / totals
        out_ref[:, cols] = jnp.where(first, summed[:rows], summed[rows:]).astype(out_ref.dtype)


def attention(queries, gathered, live, scale):
    return pl.pallas_call(
        functools.partial(attention_kernel, scale),
        out_shape=jax.ShapeDtypeStruct(queries.shape, jnp.bfloat16),
        in_specs=[pl.BlockSpec(memory_space=pltpu.VMEM)] * 3,
        out_specs=pl.BlockSpec(memory_space=pltpu.VMEM),
        compiler_params=pltpu.CompilerParams(vmem_limit_bytes=56 * 1024 * 1024),
    )(queries, gathered, live)


def ring_scatter_kernel(zs, xs, part_ref, out_ref, landed, outgoing, own_sum, crossed, ring_send, ring_recv, cross_send, cross_recv):
    me = lax.axis_index("row")
    xm = me // zs
    zm = me % zs
    ahead = xm * zs + lax.rem(zm + 1, zs)
    behind = xm * zs + lax.rem(zm + zs - 1, zs)
    half = part_ref.shape[3] // 2
    barrier = pltpu.get_barrier_semaphore()
    targets = [ahead, behind] + [lax.rem(xm + k, xs) * zs + zm for k in range(1, xs)]
    for peer in targets:
        pl.semaphore_signal(barrier, inc=1, device_id=peer_on("row", peer), device_id_type=MESH_IDS)
    pl.semaphore_wait(barrier, len(targets))
    ways = ((0, ahead, behind, -1), (1, behind, ahead, 1))
    pending = []
    for step in range(zs - 1):
        for way, dest, origin, sign in ways:
            cols = pl.ds(way * half, half)
            chunk = lax.rem(zm + sign * (1 + step) + 2 * zs, zs)
            if step == 0:
                source = part_ref.at[chunk, :, :, cols]
            else:
                arrived = pltpu.make_async_remote_copy(
                    src_ref=outgoing.at[way, step - 1],
                    dst_ref=landed.at[way, step - 1],
                    send_sem=ring_send.at[way, step - 1],
                    recv_sem=ring_recv.at[way, step - 1],
                    device_id=peer_on("row", origin),
                    device_id_type=MESH_IDS,
                )
                arrived.wait_recv()
                outgoing[way, step] = (
                    landed[way, step - 1].astype(jnp.float32)
                    + part_ref[chunk, :, :, cols].astype(jnp.float32)
                ).astype(outgoing.dtype)
                source = outgoing.at[way, step]
            copy = pltpu.make_async_remote_copy(
                src_ref=source,
                dst_ref=landed.at[way, step],
                send_sem=ring_send.at[way, step],
                recv_sem=ring_recv.at[way, step],
                device_id=peer_on("row", dest),
                device_id_type=MESH_IDS,
            )
            copy.start()
            pending.append(copy)
    last = zs - 2
    for way, dest, origin, sign in ways:
        cols = pl.ds(way * half, half)
        pltpu.make_async_remote_copy(
            src_ref=outgoing.at[way, last],
            dst_ref=landed.at[way, last],
            send_sem=ring_send.at[way, last],
            recv_sem=ring_recv.at[way, last],
            device_id=peer_on("row", origin),
            device_id_type=MESH_IDS,
        ).wait_recv()
        own_sum[:, :, cols] = landed[way, last].astype(jnp.float32) + part_ref[zm, :, :, cols].astype(jnp.float32)
    crossed[0] = own_sum[...].astype(crossed.dtype)
    sends = []
    for k in range(1, xs):
        peer_x = lax.rem(xm + k, xs)
        copy = pltpu.make_async_remote_copy(
            src_ref=crossed.at[0, peer_x],
            dst_ref=crossed.at[k, 0],
            send_sem=cross_send.at[k],
            recv_sem=cross_recv.at[k],
            device_id=peer_on("row", peer_x * zs + zm),
            device_id_type=MESH_IDS,
        )
        copy.start()
        sends.append(copy)
    total = own_sum[xm]
    for k in range(1, xs):
        origin_x = lax.rem(xm + xs - k, xs)
        pltpu.make_async_remote_copy(
            src_ref=crossed.at[0, 0],
            dst_ref=crossed.at[k, 0],
            send_sem=cross_send.at[k],
            recv_sem=cross_recv.at[k],
            device_id=peer_on("row", origin_x * zs + zm),
            device_id_type=MESH_IDS,
        ).wait_recv()
        total = total + crossed[k, 0].astype(jnp.float32)
    out_ref[...] = total
    for copy in pending + sends:
        copy.wait_send()


def ring_scatter_sum(part, xs, zs, kernel_id):
    rows = part.shape[0] // (xs * zs)
    width = part.shape[1]
    arranged = part.reshape(zs, xs, rows, width)
    return pl.pallas_call(
        functools.partial(ring_scatter_kernel, zs, xs),
        out_shape=jax.ShapeDtypeStruct((rows, width), jnp.float32),
        in_specs=[pl.BlockSpec(memory_space=pltpu.VMEM)],
        out_specs=pl.BlockSpec(memory_space=pltpu.VMEM),
        scratch_shapes=[
            pltpu.VMEM((2, zs - 1, xs, rows, width // 2), part.dtype),
            pltpu.VMEM((2, zs - 1, xs, rows, width // 2), part.dtype),
            pltpu.VMEM((xs, rows, width), jnp.float32),
            pltpu.VMEM((xs, xs, rows, width), part.dtype),
            pltpu.SemaphoreType.DMA((2, zs - 1)),
            pltpu.SemaphoreType.DMA((2, zs - 1)),
            pltpu.SemaphoreType.DMA((xs,)),
            pltpu.SemaphoreType.DMA((xs,)),
        ],
        compiler_params=pltpu.CompilerParams(
            collective_id=kernel_id, has_side_effects=True, vmem_limit_bytes=56 * 1024 * 1024
        ),
    )(arranged)


def ring_gather_kernel(zs, xs, block_ref, out_ref, held, own_sem, ring_send, ring_recv, cross_send, cross_recv):
    me = lax.axis_index("row")
    xm = me // zs
    zm = me % zs
    ahead = xm * zs + lax.rem(zm + 1, zs)
    behind = xm * zs + lax.rem(zm + zs - 1, zs)
    barrier = pltpu.get_barrier_semaphore()
    targets = [ahead, behind] + [lax.rem(xm + k, xs) * zs + zm for k in range(1, xs)]
    for peer in targets:
        pl.semaphore_signal(barrier, inc=1, device_id=peer_on("row", peer), device_id_type=MESH_IDS)
    pl.semaphore_wait(barrier, len(targets))
    own = pltpu.make_async_copy(block_ref, held.at[zm, xm], own_sem)
    own.start()
    pending = []
    for k in range(1, xs):
        peer_x = lax.rem(xm + k, xs)
        copy = pltpu.make_async_remote_copy(
            src_ref=block_ref,
            dst_ref=held.at[zm, xm],
            send_sem=cross_send.at[k],
            recv_sem=cross_recv.at[k],
            device_id=peer_on("row", peer_x * zs + zm),
            device_id_type=MESH_IDS,
        )
        copy.start()
        pending.append(copy)
    own.wait()
    for k in range(1, xs):
        origin_x = lax.rem(xm + xs - k, xs)
        pltpu.make_async_remote_copy(
            src_ref=block_ref,
            dst_ref=held.at[zm, origin_x],
            send_sem=cross_send.at[k],
            recv_sem=cross_recv.at[k],
            device_id=peer_on("row", origin_x * zs + zm),
            device_id_type=MESH_IDS,
        ).wait_recv()
    split = xs // 2
    ways = ((0, ahead, behind, -1, pl.ds(0, split)), (1, behind, ahead, 1, pl.ds(split, xs - split)))
    for step in range(zs):
        for way, dest, origin, sign, part in ways:
            group = lax.rem(zm + sign * step + zs, zs)
            if step > 0:
                pltpu.make_async_remote_copy(
                    src_ref=held.at[group, part],
                    dst_ref=held.at[group, part],
                    send_sem=ring_send.at[way, step - 1],
                    recv_sem=ring_recv.at[way, step - 1],
                    device_id=peer_on("row", origin),
                    device_id_type=MESH_IDS,
                ).wait_recv()
            if step < zs - 1:
                copy = pltpu.make_async_remote_copy(
                    src_ref=held.at[group, part],
                    dst_ref=held.at[group, part],
                    send_sem=ring_send.at[way, step],
                    recv_sem=ring_recv.at[way, step],
                    device_id=peer_on("row", dest),
                    device_id_type=MESH_IDS,
                )
                copy.start()
                pending.append(copy)
    for copy in pending:
        copy.wait_send()
    out = pltpu.make_async_copy(held, out_ref, own_sem)
    out.start()
    out.wait()


def ring_gather(block, xs, zs, kernel_id):
    return pl.pallas_call(
        functools.partial(ring_gather_kernel, zs, xs),
        out_shape=jax.ShapeDtypeStruct((zs, xs) + block.shape, block.dtype),
        in_specs=[pl.BlockSpec(memory_space=pltpu.VMEM)],
        out_specs=pl.BlockSpec(memory_space=pl.ANY),
        scratch_shapes=[
            pltpu.VMEM((zs, xs) + block.shape, block.dtype),
            pltpu.SemaphoreType.DMA(()),
            pltpu.SemaphoreType.DMA((2, zs - 1)),
            pltpu.SemaphoreType.DMA((2, zs - 1)),
            pltpu.SemaphoreType.DMA((xs,)),
            pltpu.SemaphoreType.DMA((xs,)),
        ],
        compiler_params=pltpu.CompilerParams(
            collective_id=kernel_id, has_side_effects=True, vmem_limit_bytes=56 * 1024 * 1024
        ),
    )(block)


def swap_kernel(src_ref, out_ref, landed, sems):
    other = 1 - lax.axis_index("req")
    barrier = pltpu.get_barrier_semaphore()
    pl.semaphore_signal(barrier, inc=1, device_id=peer_on("req", other), device_id_type=MESH_IDS)
    pl.semaphore_wait(barrier, 1)
    copy = pltpu.make_async_remote_copy(
        src_ref=src_ref,
        dst_ref=landed,
        send_sem=sems.at[0],
        recv_sem=sems.at[1],
        device_id=peer_on("req", other),
        device_id_type=MESH_IDS,
    )
    copy.start()
    copy.wait_send()
    copy.wait_recv()
    out_ref[...] = landed[...]


def partner_swap(value, kernel_id):
    return pl.pallas_call(
        swap_kernel,
        out_shape=jax.ShapeDtypeStruct(value.shape, value.dtype),
        in_specs=[pl.BlockSpec(memory_space=pltpu.VMEM)],
        out_specs=pl.BlockSpec(memory_space=pltpu.VMEM),
        scratch_shapes=[pltpu.VMEM(value.shape, value.dtype), pltpu.SemaphoreType.DMA((2,))],
        compiler_params=pltpu.CompilerParams(collective_id=kernel_id, has_side_effects=True),
    )(value)


def halo_kernel(tile_ref, out_ref, slots, send_sems, recv_sems):
    req = lax.axis_index("req")
    row = lax.axis_index("row")
    col = lax.axis_index("col")
    rows = lax.axis_size("row")
    cols = lax.axis_size("col")
    offsets = [(a, b) for a in (-1, 0, 1) for b in (-1, 0, 1) if (a, b) != (0, 0)]

    def present(a, b):
        return (row + a >= 0) & (row + a < rows) & (col + b >= 0) & (col + b < cols)

    def link(a, b):
        return pltpu.make_async_remote_copy(
            src_ref=tile_ref,
            dst_ref=slots.at[1 - a, 1 - b],
            send_sem=send_sems.at[1 + a, 1 + b],
            recv_sem=recv_sems.at[1 - a, 1 - b],
            device_id=(req, row + a, col + b),
            device_id_type=MESH_IDS,
        )

    barrier = pltpu.get_barrier_semaphore()
    for a, b in offsets:
        @pl.when(present(a, b))
        def _():
            pl.semaphore_signal(barrier, inc=1, device_id=(req, row + a, col + b), device_id_type=MESH_IDS)
    up = (row + rows - 1) // rows
    down = (2 * rows - 2 - row) // rows
    left = (col + cols - 1) // cols
    right = (2 * cols - 2 - col) // cols
    pl.semaphore_wait(barrier, (1 + up + down) * (1 + left + right) - 1)
    for a, b in offsets:
        @pl.when(present(a, b))
        def _():
            link(a, b).start()
    for a, b in offsets:
        @pl.when(present(a, b))
        def _():
            copy = link(a, b)
            copy.wait_send()
            pltpu.make_async_remote_copy(
                src_ref=tile_ref,
                dst_ref=slots.at[1 + a, 1 + b],
                send_sem=send_sems.at[1 + a, 1 + b],
                recv_sem=recv_sems.at[1 + a, 1 + b],
                device_id=(req, row + a, col + b),
                device_id_type=MESH_IDS,
            ).wait_recv()
            out_ref[1 + a, 1 + b] = slots[1 + a, 1 + b]

        @pl.when(jnp.logical_not(present(a, b)))
        def _():
            out_ref[1 + a, 1 + b] = jnp.zeros(out_ref.shape[2:], out_ref.dtype)
    out_ref[1, 1] = tile_ref[...]


def halo_extend(tile):
    gathered = pl.pallas_call(
        halo_kernel,
        out_shape=jax.ShapeDtypeStruct((3, 3) + tile.shape, tile.dtype),
        in_specs=[pl.BlockSpec(memory_space=pltpu.VMEM)],
        out_specs=pl.BlockSpec(memory_space=pltpu.VMEM),
        scratch_shapes=[
            pltpu.VMEM((3, 3) + tile.shape, tile.dtype),
            pltpu.SemaphoreType.DMA((3, 3)),
            pltpu.SemaphoreType.DMA((3, 3)),
        ],
        compiler_params=pltpu.CompilerParams(collective_id=6, has_side_effects=True),
    )(tile)
    bands = []
    for a, pick_rows in ((0, slice(-1, None)), (1, slice(None)), (2, slice(0, 1))):
        pieces = [
            gathered[a, 0][:, pick_rows, -1:],
            gathered[a, 1][:, pick_rows, :],
            gathered[a, 2][:, pick_rows, :1],
        ]
        bands.append(jnp.concatenate(pieces, axis=2))
    return jnp.concatenate(bands, axis=1)


def prep_kernel(eps, raw_ref, q_gain_ref, k_gain_ref, q_ref, kv_ref):
    span = raw_ref.shape[1]
    lane = lax.broadcasted_iota(jnp.int32, (1, 128), 1)
    first = lane < 64
    kv_ref[...] = jnp.zeros(kv_ref.shape, kv_ref.dtype)
    for pair in range(raw_ref.shape[2] // 128):
        cols = slice(pair * 128, (pair + 1) * 128)
        for which, gain_ref in ((0, q_gain_ref), (1, k_gain_ref)):
            piece = raw_ref[which, :, cols]
            low = jnp.sum(jnp.where(first, piece, 0.0), axis=1, keepdims=True)
            high = jnp.sum(jnp.where(first, 0.0, piece), axis=1, keepdims=True)
            centered = piece - jnp.where(first, low, high) / 64.0
            squared = centered * centered
            low = jnp.sum(jnp.where(first, squared, 0.0), axis=1, keepdims=True)
            high = jnp.sum(jnp.where(first, 0.0, squared), axis=1, keepdims=True)
            spread = jnp.where(first, low, high) / 64.0
            normed = (centered * lax.rsqrt(spread + eps) * gain_ref[:, cols]).astype(jnp.bfloat16)
            if which == 0:
                q_ref[:, cols] = normed
            else:
                kv_ref[0, :span, cols] = normed
        kv_ref[1, :span, cols] = raw_ref[2, :, cols].astype(jnp.bfloat16)


def prep_heads(raw, q_gain, k_gain, padded_span):
    width = raw.shape[2]
    tiles = width // q_gain.shape[0]
    return pl.pallas_call(
        functools.partial(prep_kernel, 1e-06),
        out_shape=(
            jax.ShapeDtypeStruct((raw.shape[1], width), jnp.bfloat16),
            jax.ShapeDtypeStruct((2, padded_span, width), jnp.bfloat16),
        ),
        in_specs=[pl.BlockSpec(memory_space=pltpu.VMEM)] * 3,
        out_specs=(pl.BlockSpec(memory_space=pltpu.VMEM), pl.BlockSpec(memory_space=pltpu.VMEM)),
    )(raw, jnp.tile(q_gain, tiles)[None], jnp.tile(k_gain, tiles)[None])


def layer_norm(tensor, epsilon):
    average = jnp.mean(tensor, axis=-1, keepdims=True)
    centered = tensor - average
    spread = jnp.mean(centered * centered, axis=-1, keepdims=True)
    return centered * lax.rsqrt(spread + epsilon)


def modulate(tensor, offset, factor):
    return (layer_norm(tensor, 1e-05) * (1.0 + factor) + offset).astype(jnp.bfloat16)


def head_norm(tensor, scaling):
    return (layer_norm(tensor, 1e-06) * scaling).astype(jnp.bfloat16)


def pick_entry(entries, position):
    slot_ids = jnp.arange(entries.shape[0], dtype=jnp.int32)
    return jnp.sum(jnp.where(slot_ids == position, entries, jnp.zeros_like(entries)))


def solver_weights(step_index):
    plan = jnp.linspace(0.00085**0.5, 0.012**0.5, TRAIN_STEPS, dtype=jnp.float32) ** 2
    cumulative = jnp.cumprod(1.0 - plan)
    alpha_now = pick_entry(cumulative, step_index)
    alpha_prev = pick_entry(cumulative, step_index - STRIDE)
    root_now = jnp.sqrt(alpha_now)
    rest_now = jnp.sqrt(1.0 - alpha_now)
    root_prev = jnp.sqrt(alpha_prev)
    rest_prev = jnp.sqrt(1.0 - alpha_prev)
    return (
        root_prev * root_now + rest_prev * rest_now,
        rest_prev * root_now - root_prev * rest_now,
    )


def key_mask(count, owners, grid, text_len, span, block_tokens, tile, text_rows):
    positions = jnp.arange(count, dtype=jnp.int32)
    owner_row = positions // span
    within = positions % span
    is_video = within < block_tokens
    owner_col = within // tile
    local_ids = within % tile
    token_row = owner_row * TR + local_ids // TC % TR
    token_col = owner_col * TC + local_ids % TC
    text_index = owner_row * text_rows + within - block_tokens
    matches = jnp.arange(grid.shape[0], dtype=jnp.int32)[None, :] == owners[:, None]
    rows_live = jnp.sum(jnp.where(matches, grid[None, :, 0], 0), axis=1)
    cols_live = jnp.sum(jnp.where(matches, grid[None, :, 1], 0), axis=1)
    text_lens = jnp.sum(jnp.where(matches, text_len[None, :], 0), axis=1)
    video_live = (token_row[None, :] < rows_live[:, None]) & (
        token_col[None, :] < cols_live[:, None]
    )
    text_live = (text_index[None, :] < text_lens[:, None]) & (within < block_tokens + text_rows)[None, :]
    return jnp.where(is_video[None, :], video_live, text_live).astype(jnp.float32)


def projector(stacked, piece):
    return jnp.einsum("gld,cde->cgle", stacked, piece, preferred_element_type=jnp.float32)


def attention_step(queries, owners, grid, text_len, span, block_tokens, tile, text_rows):
    score_scale = queries.shape[3] ** (-0.5)

    def attend(carry, pieces, start):
        key_piece, value_piece = pieces
        live_keys = key_mask(
            key_piece.shape[1], owners, grid, text_len, span, block_tokens, tile, text_rows
        )
        scores = (
            jnp.einsum("gqhd,gkhd->gqhk", queries, key_piece, preferred_element_type=jnp.float32)
            * score_scale
        )
        raw_weights = jnp.exp(scores) * live_keys[:, None, None, :]
        weighted = jnp.einsum(
            "gqhk,gkhd->gqhd",
            raw_weights.astype(jnp.bfloat16),
            value_piece,
            preferred_element_type=jnp.float32,
        )
        return (weighted, jnp.sum(raw_weights, axis=3))

    return attend


def shards(
    hidden,
    text_hidden,
    text_len,
    grid,
    timestep,
    modulation,
    q_gain,
    k_gain,
    w_qkv,
    w_out,
    w_up,
    w_down,
    w_proj,
    latent,
    conv_w,
):
    col_count = lax.axis_size("col")
    request_id = lax.axis_index("req")
    row_id = lax.axis_index("row")
    col_id = lax.axis_index("col")
    block_tokens = hidden.shape[1]
    tile = block_tokens // col_count
    text_rows = text_hidden.shape[1]
    head_dim = q_gain.shape[0]
    adaptive = modulation[0]
    source = hidden[0].astype(jnp.float32)
    joined = jnp.concatenate(
        [
            modulate(source, adaptive[0], adaptive[1]),
            modulate(text_hidden[0].astype(jnp.float32), adaptive[0], adaptive[1]),
        ],
        axis=0,
    )
    span = joined.shape[0]
    stacked = joined[None]
    owners = jnp.reshape(request_id, (1,))
    half_cols = w_qkv.shape[2] // 2
    own_half = lax.dynamic_slice_in_dim(w_qkv, request_id * half_cols, half_cols, 2)
    gathered_half = lax.all_gather(own_half, "row", axis=1, tiled=True)
    half_heads = half_cols // head_dim

    both_rows = jnp.concatenate([joined, partner_swap(joined, 4)], axis=0)
    projected_rows = jnp.einsum("ld,cde->cle", both_rows, gathered_half, preferred_element_type=jnp.float32)
    own_raw = projected_rows[:, :span]
    received_raw = partner_swap(projected_rows[:, span:], 5)
    raw = jnp.concatenate(
        [jnp.where(request_id == 0, own_raw, received_raw), jnp.where(request_id == 0, received_raw, own_raw)], axis=2
    )
    heads_here = raw.shape[2] // head_dim
    padded_span = 16 * pl.cdiv(span, 16)
    all_queries, both = prep_heads(raw, q_gain, k_gain, padded_span)
    gathered = lax.all_gather(both[None], "row", axis=0, tiled=True)
    live = key_mask(
        gathered.shape[0] * padded_span, owners, grid, text_len, padded_span, block_tokens, tile, text_rows
    )
    attended = attention(all_queries[:block_tokens], gathered, live, head_dim ** (-0.5))
    partial_out = jnp.dot(attended, w_out, preferred_element_type=jnp.float32)
    projected = scatter_sum(partial_out.astype(jnp.bfloat16), "col", 1)
    own_rows = lax.dynamic_slice_in_dim(source, col_id * tile, tile, 0)
    mixed = lax.optimization_barrier(
        (own_rows + adaptive[2] * projected).astype(jnp.bfloat16)
    ).astype(jnp.float32)
    second_norm = modulate(mixed, adaptive[3], adaptive[4])
    hidden_units = jax.nn.gelu(
        jnp.dot(
            ring_gather(second_norm, 4, 8, 2).reshape(-1, second_norm.shape[1]),
            w_up,
            preferred_element_type=jnp.float32,
        ),
        approximate=True,
    ).astype(jnp.bfloat16)
    feed_terms = jnp.dot(hidden_units, w_down, preferred_element_type=jnp.float32)
    feed_out = ring_scatter_sum(feed_terms.astype(jnp.bfloat16), 4, 8, 0)
    out_hidden = (mixed + adaptive[5] * feed_out).astype(jnp.bfloat16)
    final_norm = modulate(out_hidden.astype(jnp.float32), adaptive[6], adaptive[7])
    velocity = jnp.dot(final_norm, w_proj, preferred_element_type=jnp.float32)
    local_ids = jnp.arange(tile, dtype=jnp.int32)
    token_row = row_id * TR + local_ids // TC % TR
    token_col = col_id * TC + local_ids % TC
    rows_live = pick_entry(grid[:, 0], request_id)
    cols_live = pick_entry(grid[:, 1], request_id)
    live_tokens = ((token_row < rows_live) & (token_col < cols_live)).astype(jnp.float32)
    keep_part, velocity_part = solver_weights(pick_entry(timestep, request_id))
    updated = (keep_part * latent[0] + velocity_part * velocity) * live_tokens[:, None]
    pixels = (
        updated.reshape(FR, TR, TC, CH, 2, 2)
        .transpose(0, 1, 4, 2, 5, 3)
        .reshape(FR, 2 * TR, 2 * TC, CH)
    )
    scaled = (pixels / latent_scale).astype(jnp.bfloat16)
    padded = halo_extend(scaled)
    running = jnp.zeros((FR, 2 * TR, 2 * TC, conv_w.shape[3]), jnp.float32)
    for row_tap in range(3):
        for col_tap in range(3):
            window = padded[:, row_tap : row_tap + 2 * TR, col_tap : col_tap + 2 * TC, :]
            running = running + jnp.einsum(
                "fyxc,cd->fyxd",
                window,
                conv_w[row_tap, col_tap],
                preferred_element_type=jnp.float32,
            )
    return (out_hidden[None], updated[None], running.astype(jnp.bfloat16)[None])


def solution(mesh):
    placed = (
        P("req", "row", None),
        P("req", "row", None),
        P(),
        P(),
        P(),
        P("req", None, None),
        P(),
        P(),
        P(None, "row", "col"),
        P("col", None),
        P(None, "row"),
        P("row", None),
        P(),
        P("req", ("row", "col"), None),
        P(),
    )
    return jax.shard_map(
        shards,
        mesh=mesh,
        in_specs=placed,
        out_specs=(
            P("req", ("row", "col"), None),
            P("req", ("row", "col"), None),
            P("req", None, "row", "col", None),
        ),
        check_vma=False,
    )
```
